32 devices in a mesh: dp: 8 (over z, core), mp: 4 (over y, x).
Axes of the slice: x: 2, y: 2, z: 4, core: 2. Of those that a mesh axis runs over, the one named last changes fastest.
Arguments:
- layer_in: bfloat16 [2, 8192, 2048], P(None, ('dp', 'mp')), may hold values from -6 to 6
- norm1_gain: bfloat16 [2048], replicated, may hold values from 0.5 to 1.5
- w_query: bfloat16 [2048, 2048], P(None, 'mp'), may hold values from -0.125 to 0.125
- w_key: bfloat16 [2048, 2048], P(None, 'mp'), may hold values from -0.125 to 0.125
- w_value: bfloat16 [2048, 4096], P(None, 'mp'), may hold values from -0.125 to 0.125
- w_gate: bfloat16 [2048, 4096], P(None, 'mp'), may hold values from -0.125 to 0.125
- w_out: bfloat16 [4096, 2048], P('mp'), may hold values from -0.09375 to 0.09375
- norm2_gain: bfloat16 [2048], replicated, may hold values from 0.5 to 1.5
- w_up: bfloat16 [2048, 4096], P(None, 'mp'), may hold values from -0.125 to 0.125
- w_down: bfloat16 [4096, 2048], P('mp'), may hold values from -0.09375 to 0.09375
- decay_rates: float32 [8], P('mp'), may hold values from 0.0005 to 0.03
- seq_counts: int32 [8, 2, 3], P('dp'), may hold values from 0 to 4, as said below
- out_grad: bfloat16 [2, 8192, 2048], P(None, ('dp', 'mp')), may hold values from -6 to 6
Outputs:
- layer_out: bfloat16 [2, 8192, 2048], P(None, ('dp', 'mp'))
- grad_input: float32 [2, 8192, 2048], P(None, ('dp', 'mp'))
- grad_norm1_gain: float32 [2048], P('dp')
- grad_w_query: float32 [2048, 2048], P('dp', 'mp')
- grad_w_key: float32 [2048, 2048], P('dp', 'mp')
- grad_w_value: float32 [2048, 4096], P('dp', 'mp')
- grad_w_gate: float32 [2048, 4096], P('dp', 'mp')
- grad_w_out: float32 [4096, 2048], P('mp', 'dp')
- grad_norm2_gain: float32 [2048], P('dp')
- grad_w_up: float32 [2048, 4096], P('dp', 'mp')
- grad_w_down: float32 [4096, 2048], P('mp', 'dp')
The draws below stay inside these ranges and needn't reach their ends.
Inputs may be any that keep to these rules, and one draw needn't show every extreme that they name: `seq_counts`: for each index of dp and micro-batch the last dimension counts sequences of 256, 512 and 1024 tokens, in this order; their tokens come to exactly 1024; in some micro-batch of some index of dp four sequences of 256 tokens fill it.
All inputs are finite; a program needn't handle non-finite values.
Results may differ from the reference program's by a relative error of at most 0.02.
Values may be sent and summed in bfloat16 or wider, within the bound.
A program may use at most 384 MiB of HBM per device.

```python
import math
import jax
import jax.numpy as jnp
from jax import lax

D = 2048
HEADS = 8
KEY_DIM = 256
VALUE_W = 4096
FF = 4096
LONGEST = 1024
BLOCK = 512
MICRO = 2
KEY_W = 2048
GROUP_TOK = 8192
N_DP = 8


def draw_seq_counts(key, part):
    options = jnp.array([[4, 0, 0], [0, 0, 1], [0, 2, 0], [2, 1, 0]], jnp.int32)
    picked = jax.random.randint(jax.random.fold_in(key, 11), (N_DP, MICRO), 0, 4)
    target_dp = jax.random.randint(jax.random.fold_in(key, 12), (), 0, N_DP)
    target_micro = jax.random.randint(jax.random.fold_in(key, 13), (), 0, MICRO)
    forced = (jnp.arange(N_DP)[:, None] == target_dp) & (jnp.arange(MICRO)[None, :] == target_micro)
    picked = jnp.where(forced, 0, picked)
    return options[picked]


def spiked(drawn, key, source, target, shards_of, factor):
    owner, partner = [(jnp.arange(drawn.shape[dim]) // (drawn.shape[dim] // shards_of)).reshape([-1 if axis == dim else 1 for axis in range(drawn.ndim)]) for dim in (source, target)]
    chosen = jax.random.permutation(key, shards_of)[partner]
    strong = (owner == chosen) | (owner == (partner + shards_of // 2) % shards_of)
    return jnp.where(strong, factor * drawn, drawn)


def block_scale(stream_key, extent, shards, least, top_value):
    loudness, own = 1.0, jax.random.fold_in(stream_key, 6)
    for dim, shards_of in shards:
        draws = jnp.exp(jax.random.uniform(jax.random.fold_in(own, dim), (shards_of,), jnp.float32, least / len(shards), top_value / len(shards)))
        loudness = loudness * jnp.repeat(draws, extent[dim] // shards_of).reshape([-1 if axis == dim else 1 for axis in range(len(extent))])
    return loudness


def scatter_about(stream_key, extent, deviation, bound, cuts=(), kind=jnp.bfloat16):
    values = jax.random.normal(stream_key, extent, jnp.float32) * deviation
    if len(cuts) > 0:
        values = block_scale(stream_key, extent, cuts, -0.22, 0.18) * values
    return jnp.clip(values, min=-bound, max=bound).astype(kind)


def bell_draw_with(own_key, shape, width, bound, split, heavy, held_as=jnp.bfloat16):
    drawn = width * jax.random.normal(own_key, shape, jnp.float32)
    if split:
        drawn = drawn * block_scale(own_key, shape, split, -0.22, 0.18)
    return jnp.clip(spiked(drawn, jax.random.fold_in(own_key, 3), *heavy), -bound, bound).astype(held_as)


def setup_inputs(seed: int = 0) -> dict:
    seeds = jax.random.split(jax.random.key(seed), 14)
    layer_in = scatter_about(seeds[0], (MICRO, GROUP_TOK, D), 1.0, 6.0, ((1, 32),))
    norm1_gain = jnp.clip(1.0 + 0.1 * jax.random.normal(seeds[1], (D,), jnp.float32), 0.5, 1.5).astype(jnp.bfloat16)
    w_query = scatter_about(seeds[2], (D, KEY_W), D ** -0.5, 0.125, ((1, 4),))
    w_key = scatter_about(seeds[3], (D, KEY_W), D ** -0.5, 0.125, ((1, 4),))
    w_value = scatter_about(seeds[4], (D, VALUE_W), D ** -0.5, 0.125, ((1, 4),))
    w_gate = scatter_about(seeds[5], (D, VALUE_W), D ** -0.5, 0.125, ((1, 4),))
    w_out = scatter_about(seeds[6], (VALUE_W, D), VALUE_W ** -0.5, 0.09375, ((0, 4),))
    norm2_gain = jnp.clip(1.0 + 0.1 * jax.random.normal(seeds[7], (D,), jnp.float32), 0.5, 1.5).astype(jnp.bfloat16)
    w_up = scatter_about(seeds[8], (D, FF), D ** -0.5, 0.125, ((1, 4),))
    w_down = scatter_about(seeds[9], (FF, D), FF ** -0.5, 0.09375, ((0, 4),))
    decay_rates = jnp.clip(jnp.exp(math.log(0.03) - 4.0943445 * jax.random.uniform(seeds[10], (HEADS,), jnp.float32) ** block_scale(seeds[10], (HEADS,), ((0, 4),), -0.2, 0.2)), 0.0005, 0.03)
    seq_counts = draw_seq_counts(jax.random.fold_in(seeds[13], 71), 0)
    out_grad = bell_draw_with(seeds[12], (MICRO, GROUP_TOK, D), 1.0, 6.0, ((1, 32),), (1, 2, 32, 2.75))
    return {"layer_in": layer_in, "norm1_gain": norm1_gain, "w_query": w_query, "w_key": w_key, "w_value": w_value, "w_gate": w_gate, "w_out": w_out, "norm2_gain": norm2_gain, "w_up": w_up, "w_down": w_down, "decay_rates": decay_rates, "seq_counts": seq_counts, "out_grad": out_grad}


@jax.custom_vjp
def low(v):
    return lax.optimization_barrier(v.astype(jnp.bfloat16)).astype(jnp.float32)

@jax.custom_vjp
def low_back(v):
    return v

def low_keep(v):
    return (low(v), None)

def low_pass(kept, grad):
    return (grad,)

def back_keep(v):
    return (v, None)

def back_low(kept, grad):
    return (low(grad),)
low.defvjp(low_keep, low_pass)
low_back.defvjp(back_keep, back_low)
NORM_EPS = 1e-05
GROUP_FLOOR = 1.0
HIGH = lax.Precision.HIGHEST

def matmul(left, right):
    return jnp.dot(left, right, preferred_element_type=jnp.float32, precision=HIGH)

def layer_norm(rows, gain):
    center = rows - lax.optimization_barrier(jnp.mean(rows, axis=-1, keepdims=True))
    variance = lax.optimization_barrier(jnp.mean(center * center, axis=-1, keepdims=True))
    return center * lax.rsqrt(variance + NORM_EPS) * gain

def group_norm(values, heads):
    shaped = values.reshape(values.shape[0], heads, -1)
    center = shaped - lax.optimization_barrier(jnp.mean(shaped, axis=-1, keepdims=True))
    variance = lax.optimization_barrier(jnp.mean(center * center, axis=-1, keepdims=True))
    return (center * lax.rsqrt(jnp.maximum(variance, GROUP_FLOOR))).reshape(values.shape)

def document_ids(counts, length):
    position = jnp.arange(length, dtype=jnp.int32)
    half_len = length // 2
    quarter_len = length // 4
    long_end = counts[2] * length
    half_end = long_end + counts[1] * half_len
    quarter_end = half_end + counts[0] * quarter_len
    long_ids = position // length
    half_ids = counts[2] + (position - long_end) // half_len
    quarter_ids = counts[2] + counts[1] + (position - half_end) // quarter_len
    inner = jnp.where(position < quarter_end, quarter_ids, -1)
    inner = jnp.where(position < half_end, half_ids, inner)
    return jnp.where(position < long_end, long_ids, inner).astype(jnp.int32)

def decay_mask(row_ids, col_ids, row_pos, col_pos, log_gamma, scale):
    before = col_pos[None, :] <= row_pos[:, None]
    valid = (row_ids[:, None] == col_ids[None, :]) & (row_ids[:, None] >= 0) & before
    distance = jnp.where(before, row_pos[:, None] - col_pos[None, :], 0).astype(jnp.float32)
    return jnp.where(valid[None], jnp.exp(distance[None] * log_gamma[:, None, None]) * scale, jnp.float32(0.0))

def retention(queries, keys_all, values_all, seq_ids, log_gamma):
    length = queries.shape[0]
    query_heads = queries.reshape(length, HEADS, -1)
    key_heads = keys_all.reshape(length, HEADS, -1)
    value_heads = values_all.reshape(length, HEADS, -1)
    position = jnp.arange(length, dtype=jnp.int32)
    scale = KEY_DIM ** (-0.5)

    def one_block(index):
        start = (index * BLOCK).astype(jnp.int32)
        query_block = lax.dynamic_slice_in_dim(query_heads, start, BLOCK, 0)
        seq_block = lax.dynamic_slice_in_dim(seq_ids, start, BLOCK, 0)
        place_block = start + jnp.arange(BLOCK, dtype=jnp.int32)
        raw = jnp.einsum('rhd,chd->hrc', query_block, key_heads, precision=HIGH)
        mask = decay_mask(seq_block, seq_ids, place_block, position, log_gamma, scale)
        scores = low(low_back(raw) * mask)
        return jnp.einsum('hrc,che->rhe', scores, value_heads, precision=HIGH)
    blocks = lax.map(jax.checkpoint(one_block), jnp.arange(length // BLOCK, dtype=jnp.int32))
    return blocks.reshape(length, -1)

def group_forward(rows, seq_ids, params, log_gamma):
    gain_one, w_query, w_key, w_value, w_gate, w_out, gain_two, w_up, w_down = params
    normed = low(layer_norm(rows, gain_one))
    queries = low(low_back(matmul(normed, w_query)))
    keys_all = low(low_back(matmul(normed, w_key)))
    values_all = low(low_back(matmul(normed, w_value)))
    gate = low_back(matmul(normed, w_gate))
    retained = low_back(retention(queries, keys_all, values_all, seq_ids, log_gamma))
    mixed = low(jax.nn.silu(gate) * group_norm(retained, HEADS))
    hidden = rows + low_back(matmul(mixed, w_out))
    normed_two = low(layer_norm(hidden, gain_two))
    upper = low_back(matmul(normed_two, w_up))
    active = low(jax.nn.gelu(upper, approximate=True))
    return hidden + low_back(matmul(active, w_down))

def reference(layer_in, norm1_gain, w_query, w_key, w_value, w_gate, w_out, norm2_gain, w_up, w_down, decay_rates, seq_counts, out_grad):
    groups = MICRO * N_DP
    rows_all = layer_in.astype(jnp.float32).reshape(groups, LONGEST, D)
    counts = jnp.transpose(seq_counts, (1, 0, 2)).reshape(groups, 3)
    seq_ids_all = jax.vmap(lambda single: document_ids(single, LONGEST))(counts)
    log_gamma = jnp.log1p(-decay_rates.astype(jnp.float32))
    params = tuple((weight.astype(jnp.float32) for weight in (norm1_gain, w_query, w_key, w_value, w_gate, w_out, norm2_gain, w_up, w_down)))

    def forward(rows_in, weights):

        def scan_step(carry, inputs):
            rows_group, seq_group = inputs
            return (carry, jax.checkpoint(group_forward)(rows_group, seq_group, weights, log_gamma))
        _, result = lax.scan(scan_step, jnp.zeros((), jnp.float32), (rows_in, seq_ids_all))
        return result
    result, pullback = jax.vjp(forward, rows_all, params)
    grad_rows, grad_params = pullback(out_grad.astype(jnp.float32).reshape(groups, LONGEST, D))
    full_shape = (MICRO, N_DP * LONGEST, D)
    return (result.reshape(full_shape).astype(jnp.bfloat16), grad_rows.reshape(full_shape), grad_params[0], grad_params[1], grad_params[2], grad_params[3], grad_params[4], grad_params[5], grad_params[6], grad_params[7], grad_params[8])
```

```python
import functools

import jax
import jax.numpy as jnp
from jax import lax
from jax.experimental import pallas as pl
from jax.experimental.pallas import tpu as pltpu
from jax.sharding import PartitionSpec as P

NORM_EPS = 1e-05
GROUP_FLOOR = 1.0
BF16 = jnp.bfloat16
F32 = jnp.float32


def layer_norm(rows, gain):
    center = rows - jnp.mean(rows, axis=-1, keepdims=True)
    variance = jnp.mean(center * center, axis=-1, keepdims=True)
    return center * lax.rsqrt(variance + NORM_EPS) * gain


def gelu_tanh(values):
    return jax.nn.gelu(values, approximate=True)


def document_ids(counts, position, length):
    half_len = length // 2
    quarter_len = length // 4
    long_end = counts[2] * length
    half_end = long_end + counts[1] * half_len
    quarter_end = half_end + counts[0] * quarter_len
    long_ids = position // length
    half_ids = counts[2] + (position - long_end) // half_len
    quarter_ids = counts[2] + counts[1] + (position - half_end) // quarter_len
    inner = jnp.where(position < quarter_end, quarter_ids, -1)
    inner = jnp.where(position < half_end, half_ids, inner)
    return jnp.where(position < long_end, long_ids, inner)


def dot_nt(left, right):
    return lax.dot_general(left, right, (((1,), (1,)), ((), ())), preferred_element_type=F32)


def dot_tn(left, right):
    return lax.dot_general(left, right, (((0,), (0,)), ((), ())), preferred_element_type=F32)


def dot_nn(left, right):
    return jnp.dot(left, right, preferred_element_type=F32)


def move(value, axis, step):
    size = lax.axis_size(axis)
    return lax.ppermute(value, axis, [(i, i ^ step) for i in range(size)])


def gather(rows):
    size = lax.axis_size("mp")
    if size != 4:
        return jnp.concatenate([rows] + [move(rows, "mp", k) for k in range(1, size)], 0)
    half = rows.shape[0] // 2
    first = move(rows, "mp", 1)
    second = move(rows, "mp", 2)
    upper = move(first[:half], "mp", 2)
    lower = move(second[half:], "mp", 1)
    return jnp.concatenate([rows, first, second, upper, lower], 0)


def scatter_sum(partial):
    size = lax.axis_size("mp")
    rows = partial.shape[0] // size
    parts = [partial[k * rows : (k + 1) * rows] for k in range(size)]
    if size != 4:
        total = parts[0].astype(F32)
        for k in range(1, size):
            total = total + move(parts[k], "mp", k).astype(F32)
        return total
    half = rows // 2
    upper = move(parts[3][:half], "mp", 1)
    lower = move(parts[3][half:], "mp", 2)
    first_up = move(parts[1][:half], "mp", 1)
    second_low = move(parts[2][half:], "mp", 2)
    second_up = move(parts[2][:half] + upper, "mp", 2)
    first_low = move(parts[1][half:] + lower, "mp", 1)
    top = first_up.astype(F32) + second_up.astype(F32)
    bottom = first_low.astype(F32) + second_low.astype(F32)
    return parts[0].astype(F32) + jnp.concatenate([top, bottom], 0)


def small_sum(value):
    step = lax.axis_size("mp") // 2
    while step:
        value = value + move(value, "mp", step)
        step //= 2
    step = lax.axis_size("dp") // 2
    place = lax.axis_index("dp")
    while step:
        half = value.shape[1] // 2
        low, high = value[:, :half], value[:, half:]
        upper = (place // step) % 2 == 1
        value = jnp.where(upper, high, low) + move(jnp.where(upper, low, high), "dp", step)
        step //= 2
    return value


def decay_table(log_gamma, size, scale):
    row = lax.broadcasted_iota(jnp.int32, (size, size), 0)
    col = lax.broadcasted_iota(jnp.int32, (size, size), 1)
    table = jnp.exp((row - col).astype(F32) * log_gamma) * scale
    return table, jnp.where(row >= col, table, 0.0)


def pair_scale(docs, i, j, log_gamma, size):
    same = jnp.logical_and(docs[i] == docs[j], docs[i] >= 0)
    far = jnp.exp(jnp.full((1, 1), (i - j) * size, F32) * log_gamma)
    return jnp.where(same, far, 0.0)


def retention_forward_kernel(
    blocks, kd, me_ref, docs_ref, rates_ref, qkv_ref, gate_ref, mixed_ref, full_ref, diag_ref
):
    head = pl.program_id(0)
    size = qkv_ref.shape[0] // blocks
    log_gamma = rates_ref[head]
    full_ref[...], diag_ref[...] = decay_table(log_gamma, size, kd**-0.5)
    me = me_ref[0]
    docs = [docs_ref[i] for i in range(blocks)]
    slots = [pl.ds(pl.multiple_of((i ^ me) * size, size), size) for i in range(blocks)]
    for i in range(blocks):
        query = qkv_ref[slots[i], :kd]
        total = None
        for j in range(i + 1):
            table = diag_ref if j == i else full_ref
            raw = dot_nt(query, qkv_ref[slots[j], kd : 2 * kd])
            scores = (raw * (table[...] * pair_scale(docs, i, j, log_gamma, size))).astype(BF16)
            term = dot_nn(scores, qkv_ref[slots[j], 2 * kd :])
            total = term if total is None else total + term
        center = total - jnp.mean(total, axis=-1, keepdims=True)
        variance = jnp.mean(center * center, axis=-1, keepdims=True)
        normal = center * lax.rsqrt(jnp.maximum(variance, GROUP_FLOOR))
        gate = gate_ref[slots[i], :].astype(F32)
        mixed_ref[slots[i], :] = (gate * jax.nn.sigmoid(gate) * normal).astype(BF16)


def retention_backward_kernel(
    blocks,
    kd,
    me_ref,
    docs_ref,
    rates_ref,
    qkv_ref,
    gate_ref,
    grad_ref,
    gqkv_ref,
    ggate_ref,
    full_ref,
    diag_ref,
    gkey_ref,
    gvalue_ref,
):
    head = pl.program_id(0)
    size = qkv_ref.shape[0] // blocks
    log_gamma = rates_ref[head]
    full_ref[...], diag_ref[...] = decay_table(log_gamma, size, kd**-0.5)
    me = me_ref[0]
    docs = [docs_ref[i] for i in range(blocks)]
    slots = [pl.ds(pl.multiple_of((i ^ me) * size, size), size) for i in range(blocks)]
    for i in range(blocks):
        query = qkv_ref[slots[i], :kd]
        total = None
        masks = []
        kept = []
        for j in range(i + 1):
            table = diag_ref if j == i else full_ref
            mask = table[...] * pair_scale(docs, i, j, log_gamma, size)
            raw = dot_nt(query, qkv_ref[slots[j], kd : 2 * kd])
            scores = (raw * mask).astype(BF16)
            term = dot_nn(scores, qkv_ref[slots[j], 2 * kd :])
            total = term if total is None else total + term
            kept.append(scores)
            masks.append(mask)
        center = total - jnp.mean(total, axis=-1, keepdims=True)
        variance = jnp.mean(center * center, axis=-1, keepdims=True)
        inverse = lax.rsqrt(jnp.maximum(variance, GROUP_FLOOR))
        normal = center * inverse
        gate = gate_ref[slots[i], :].astype(F32)
        grad = grad_ref[slots[i], :].astype(F32)
        sig = jax.nn.sigmoid(gate)
        ggate = grad * normal * (sig * (1.0 + gate * (1.0 - sig)))
        ggate_ref[slots[i], :] = ggate.astype(BF16)
        gnormal = grad * gate * sig
        along = jnp.mean(gnormal * normal, axis=-1, keepdims=True)
        along = jnp.where(variance > GROUP_FLOOR, along, 0.0)
        gcenter = inverse * (gnormal - normal * along)
        gret = (gcenter - jnp.mean(gcenter, axis=-1, keepdims=True)).astype(BF16)
        gquery = None
        for j in range(i + 1):
            graw = dot_nt(gret, qkv_ref[slots[j], 2 * kd :])
            graw = (graw * masks[j]).astype(BF16)
            term = dot_nn(graw, qkv_ref[slots[j], kd : 2 * kd])
            gquery = term if gquery is None else gquery + term
            place = pl.ds(j * size, size)
            gkey = dot_tn(graw, query)
            gvalue = dot_tn(kept[j], gret)
            if j == i:
                gkey_ref[place, :] = gkey
                gvalue_ref[place, :] = gvalue
            else:
                gkey_ref[place, :] += gkey
                gvalue_ref[place, :] += gvalue
        gqkv_ref[slots[i], :kd] = gquery.astype(BF16)
    for i in range(blocks):
        place = pl.ds(i * size, size)
        gqkv_ref[slots[i], kd : 2 * kd] = gkey_ref[place, :].astype(BF16)
        gqkv_ref[slots[i], 2 * kd :] = gvalue_ref[place, :].astype(BF16)


def smem():
    return pl.BlockSpec(memory_space=pltpu.SMEM)


def retention_forward(blocks, heads, kd, vd, me, docs, rates, qkv, gate):
    length = qkv.shape[0]
    size = length // blocks
    return pl.pallas_call(
        functools.partial(retention_forward_kernel, blocks, kd),
        grid=(heads,),
        out_shape=jax.ShapeDtypeStruct((length, heads * vd), BF16),
        in_specs=[
            smem(),
            smem(),
            smem(),
            pl.BlockSpec((length, 2 * kd + vd), lambda h: (0, h)),
            pl.BlockSpec((length, vd), lambda h: (0, h)),
        ],
        out_specs=pl.BlockSpec((length, vd), lambda h: (0, h)),
        scratch_shapes=[pltpu.VMEM((size, size), F32), pltpu.VMEM((size, size), F32)],
        compiler_params=pltpu.CompilerParams(vmem_limit_bytes=28 << 20),
        cost_estimate=pl.CostEstimate(
            flops=heads * length * length * (kd + vd) * 5 // 4,
            bytes_accessed=2 * length * heads * (2 * kd + 3 * vd),
            transcendentals=length * heads * vd,
        ),
    )(me, docs, rates, qkv, gate)


def retention_backward(blocks, heads, kd, vd, me, docs, rates, qkv, gate, grad):
    length = qkv.shape[0]
    size = length // blocks
    return pl.pallas_call(
        functools.partial(retention_backward_kernel, blocks, kd),
        grid=(heads,),
        out_shape=(
            jax.ShapeDtypeStruct((length, heads * (2 * kd + vd)), BF16),
            jax.ShapeDtypeStruct((length, heads * vd), BF16),
        ),
        in_specs=[
            smem(),
            smem(),
            smem(),
            pl.BlockSpec((length, 2 * kd + vd), lambda h: (0, h)),
            pl.BlockSpec((length, vd), lambda h: (0, h)),
            pl.BlockSpec((length, vd), lambda h: (0, h)),
        ],
        out_specs=(
            pl.BlockSpec((length, 2 * kd + vd), lambda h: (0, h)),
            pl.BlockSpec((length, vd), lambda h: (0, h)),
        ),
        scratch_shapes=[
            pltpu.VMEM((size, size), F32),
            pltpu.VMEM((size, size), F32),
            pltpu.VMEM((length, kd), F32),
            pltpu.VMEM((length, vd), F32),
        ],
        compiler_params=pltpu.CompilerParams(vmem_limit_bytes=36 << 20),
        cost_estimate=pl.CostEstimate(
            flops=heads * length * length * (3 * kd + 3 * vd) * 5 // 4,
            bytes_accessed=2 * length * heads * (4 * kd + 5 * vd),
            transcendentals=length * heads * vd,
        ),
    )(me, docs, rates, qkv, gate, grad)


def body(
    layer_in,
    norm1_gain,
    w_query,
    w_key,
    w_value,
    w_gate,
    w_out,
    norm2_gain,
    w_up,
    w_down,
    decay_rates,
    seq_counts,
    out_grad,
):
    heads = decay_rates.shape[0]
    kd = w_query.shape[1] // heads
    vd = w_value.shape[1] // heads
    micros, rows_dev, width = layer_in.shape
    blocks = lax.axis_size("mp")
    length = rows_dev * blocks
    head_width = 2 * kd + vd
    pieces = []
    for h in range(heads):
        pieces += [
            w_query[:, h * kd : (h + 1) * kd],
            w_key[:, h * kd : (h + 1) * kd],
            w_value[:, h * vd : (h + 1) * vd],
        ]
    w_qkv = jnp.concatenate(pieces, 1)
    gain_one = norm1_gain.astype(F32)
    gain_two = norm2_gain.astype(F32)
    rates = jnp.log1p(-decay_rates)
    me = lax.axis_index("mp").reshape(1).astype(jnp.int32)
    starts = jnp.arange(blocks, dtype=jnp.int32) * rows_dev
    both = range(micros)

    docs = [document_ids(seq_counts[0, m], starts, length) for m in both]
    rows = [layer_in[m].astype(F32) for m in both]
    pulls_one = []
    gathered = []
    for m in both:
        normed, pull = jax.vjp(layer_norm, rows[m], gain_one)
        pulls_one.append(pull)
        gathered.append(gather(normed.astype(BF16)))
    cotangent = [gather(out_grad[m]) for m in both]

    qkv, gate, mixed, hidden = [], [], [], []
    for m in both:
        qkv.append(dot_nn(gathered[m], w_qkv).astype(BF16))
        gate.append(dot_nn(gathered[m], w_gate).astype(BF16))
        mixed.append(
            retention_forward(blocks, heads, kd, vd, me, docs[m], rates, qkv[m], gate[m])
        )
        hidden.append(rows[m] + scatter_sum(dot_nn(mixed[m], w_out).astype(BF16)))

    gathered_two, pulls_two = [], []
    for m in both:
        normed, pull = jax.vjp(layer_norm, hidden[m], gain_two)
        pulls_two.append(pull)
        gathered_two.append(gather(normed.astype(BF16)))

    layer_out, active, grad_upper, grad_hidden, grad_branch, gains_two = [], [], [], [], [], []
    for m in both:
        upper = dot_nn(gathered_two[m], w_up)
        active_full, pull_gelu = jax.vjp(gelu_tanh, upper)
        active.append(active_full.astype(BF16))
        grad_upper.append(pull_gelu(dot_nt(cotangent[m], w_down))[0].astype(BF16))
        grad_normed_two = scatter_sum(dot_nt(grad_upper[m], w_up).astype(BF16))
        part, gain_part = pulls_two[m](grad_normed_two)
        gains_two.append(gain_part)
        grad_hidden.append(out_grad[m].astype(F32) + part)
        grad_branch.append(gather(grad_hidden[m].astype(BF16)))
        layer_out.append(
            (hidden[m] + scatter_sum(dot_nn(active[m], w_down).astype(BF16))).astype(BF16)
        )

    def weight_sum(lefts, rights, dim):
        total = sum(dot_tn(left, right) for left, right in zip(lefts, rights))
        return lax.psum_scatter(
            total.astype(BF16), "dp", scatter_dimension=dim, tiled=True
        ).astype(F32)

    grad_w_down = weight_sum(active, cotangent, 1)
    grad_w_up = weight_sum(gathered_two, grad_upper, 0)
    grad_w_out = weight_sum(mixed, grad_branch, 1)

    grad_input, gains_one, gqkv, ggate = [], [], [], []
    for m in both:
        grad_mixed = dot_nt(grad_branch[m], w_out).astype(BF16)
        head_grads, gate_grads = retention_backward(
            blocks, heads, kd, vd, me, docs[m], rates, qkv[m], gate[m], grad_mixed
        )
        gqkv.append(head_grads)
        ggate.append(gate_grads)
        grad_normed = scatter_sum(
            (dot_nt(gqkv[m], w_qkv) + dot_nt(ggate[m], w_gate)).astype(BF16)
        )
        part, gain_part = pulls_one[m](grad_normed)
        gains_one.append(gain_part)
        grad_input.append(grad_hidden[m] + part)
    grad_w_gate = weight_sum(gathered, ggate, 0)
    grad_w_qkv = weight_sum(gathered, gqkv, 0)
    split = grad_w_qkv.reshape(-1, heads, head_width)
    grad_w_query = split[:, :, :kd].reshape(-1, heads * kd)
    grad_w_key = split[:, :, kd : 2 * kd].reshape(-1, heads * kd)
    grad_w_value = split[:, :, 2 * kd :].reshape(-1, heads * vd)
    gains = small_sum(jnp.stack([sum(gains_one), sum(gains_two)]))
    return (
        jnp.stack(layer_out),
        jnp.stack(grad_input),
        gains[0],
        grad_w_query,
        grad_w_key,
        grad_w_value,
        grad_w_gate,
        grad_w_out,
        gains[1],
        grad_w_up,
        grad_w_down,
    )


def solution(mesh):
    in_specs = (
        P(None, ("dp", "mp"), None),
        P(),
        P(None, "mp"),
        P(None, "mp"),
        P(None, "mp"),
        P(None, "mp"),
        P("mp", None),
        P(),
        P(None, "mp"),
        P("mp", None),
        P("mp"),
        P("dp", None, None),
        P(None, ("dp", "mp"), None),
    )
    out_specs = (
        P(None, ("dp", "mp"), None),
        P(None, ("dp", "mp"), None),
        P("dp"),
        P("dp", "mp"),
        P("dp", "mp"),
        P("dp", "mp"),
        P("dp", "mp"),
        P("mp", "dp"),
        P("dp"),
        P("dp", "mp"),
        P("mp", "dp"),
    )
    return jax.shard_map(body, mesh=mesh, in_specs=in_specs, out_specs=out_specs, check_vma=False)
```

```python
import functools

import jax
import jax.numpy as jnp
from jax import lax
from jax.experimental import pallas as pl
from jax.experimental.pallas import tpu as pltpu
from jax.sharding import PartitionSpec as P

NORM_EPS = 1e-05
GROUP_FLOOR = 1.0
BF16 = jnp.bfloat16
F32 = jnp.float32
TINY = pl.CostEstimate(flops=1, bytes_accessed=1, transcendentals=0)


def document_ids(counts, position, length):
    half_len = length // 2
    quarter_len = length // 4
    long_end = counts[2] * length
    half_end = long_end + counts[1] * half_len
    quarter_end = half_end + counts[0] * quarter_len
    long_ids = position // length
    half_ids = counts[2] + (position - long_end) // half_len
    quarter_ids = counts[2] + counts[1] + (position - half_end) // quarter_len
    inner = jnp.where(position < quarter_end, quarter_ids, -1)
    inner = jnp.where(position < half_end, half_ids, inner)
    return jnp.where(position < long_end, long_ids, inner)


def dot_nt(left, right):
    return lax.dot_general(left, right, (((1,), (1,)), ((), ())), preferred_element_type=F32)


def dot_tn(left, right):
    return lax.dot_general(left, right, (((0,), (0,)), ((), ())), preferred_element_type=F32)


def dot_nn(left, right):
    return jnp.dot(left, right, preferred_element_type=F32)


def move(value, axis, step):
    size = lax.axis_size(axis)
    return lax.ppermute(value, axis, [(i, i ^ step) for i in range(size)])


def after(value, *earlier):
    return lax.optimization_barrier((value, earlier))[0]


def segment_rows(rows_dev):
    size = lax.axis_size("mp")
    if size == 4:
        return [rows_dev] * 3 + [rows_dev // 2] * 2
    return [rows_dev] * size


class Gather:
    def __init__(self, rows):
        self.size = lax.axis_size("mp")
        self.rows = rows
        if self.size != 4:
            self.pieces = [move(rows, "mp", k) for k in range(1, self.size)]
            self.early = self.pieces[:1]
            return
        self.early = self.pieces = [move(rows, "mp", 1), move(rows, "mp", 2)]

    def middle(self, *earlier):
        if self.size == 4:
            first, second = after(self.early, earlier)
            half = first.shape[0] // 2
            self.pieces = [
                *self.early,
                move(first[:half], "mp", 2),
                move(second[half:], "mp", 1),
            ]

    def result(self, *earlier):
        return after([self.rows, *self.pieces], earlier)


class ScatterSum:
    def __init__(self, segments):
        self.size = lax.axis_size("mp")
        self.own = segments[0]
        self.rest = segments[1:]
        if self.size != 4:
            self.pieces = [move(part, "mp", k + 1) for k, part in enumerate(self.rest)]
            self.early = self.pieces[:1]
            return
        upper, lower = self.rest[2:]
        self.early = (move(upper, "mp", 1), move(lower, "mp", 2))

    def middle(self, *earlier):
        if self.size == 4:
            upper, lower = after(self.early, earlier)
            half = upper.shape[0]
            first, second = self.rest[:2]
            first = jnp.concatenate([first[:half], first[half:] + lower], 0)
            second = jnp.concatenate([second[:half] + upper, second[half:]], 0)
            self.pieces = [move(first, "mp", 1), move(second, "mp", 2)]

    def result(self, *earlier):
        return after([self.own, *self.pieces], earlier)


class PairGather:
    def __init__(self, rows):
        if lax.axis_size("mp") != 4:
            self.pieces = Gather(rows).pieces
        else:
            self.pieces = [move(rows, "mp", 1)]
        self.rows = rows

    def result(self, *earlier):
        return after([self.rows, *self.pieces], earlier)


class PairScatter:
    def __init__(self, segments):
        self.own, *rest = segments
        self.pieces = [move(part, "mp", k + 1) for k, part in enumerate(rest)]

    def result(self, *earlier):
        return after([self.own, *self.pieces], earlier)


def small_sum(value):
    step = lax.axis_size("mp") // 2
    while step:
        value = value + move(value, "mp", step)
        step //= 2
    step = lax.axis_size("dp") // 2
    place = lax.axis_index("dp")
    while step:
        half = value.shape[1] // 2
        low, high = value[:, :half], value[:, half:]
        upper = (place // step) % 2 == 1
        value = jnp.where(upper, high, low) + move(jnp.where(upper, low, high), "dp", step)
        step //= 2
    return value


def resident(shape):
    zeros = (0,) * len(shape)
    return pl.BlockSpec(tuple(shape), lambda i: zeros, pipeline_mode=pl.Buffered(1))


def smem():
    return pl.BlockSpec(memory_space=pltpu.SMEM)


def call(kernel, steps, in_specs, out_specs, out_shape, scratch=(), limit=32, aliases=None):
    name = getattr(kernel, "func", kernel).__name__.removesuffix("_kernel")
    return pl.pallas_call(
        kernel,
        name=name,
        grid=(steps,),
        in_specs=in_specs,
        out_specs=out_specs,
        out_shape=out_shape,
        scratch_shapes=list(scratch),
        input_output_aliases=aliases or {},
        compiler_params=pltpu.CompilerParams(vmem_limit_bytes=limit << 20),
        cost_estimate=TINY,
    )


def assemble(out_ref, refs):
    offset = 0
    for ref in refs:
        rows = ref.shape[0]
        out_ref[offset : offset + rows, :] = ref[...]
        offset += rows


def dissolve(refs, value):
    offset = 0
    for ref in refs:
        rows = ref.shape[0]
        ref[...] = value[offset : offset + rows].astype(ref.dtype)
        offset += rows


def add_up(refs):
    total = refs[0][...].astype(F32)
    for ref in refs[1:]:
        total = total + ref[...].astype(F32)
    return total


def normalize(rows):
    center = rows - jnp.mean(rows, axis=-1, keepdims=True)
    variance = jnp.mean(center * center, axis=-1, keepdims=True)
    inverse = lax.rsqrt(variance + NORM_EPS)
    return center * inverse, inverse


def first_norm_kernel(rows_ref, gain_ref, out_ref):
    normal, _ = normalize(rows_ref[0].astype(F32))
    out_ref[...] = (normal * gain_ref[...].astype(F32)).astype(BF16)


def first_norm(m, rows, gain):
    _, count, width = rows.shape
    narrow = jax.ShapeDtypeStruct((count, width), BF16)
    return call(
        first_norm_kernel,
        1,
        [pl.BlockSpec((1, count, width), lambda i: (m, 0, 0)), resident((1, width))],
        resident((count, width)),
        narrow,
    )(rows, gain)


def second_norm_kernel(rows_ref, gain_ref, *refs):
    hidden_ref, out_ref = refs[-2:]
    hidden = rows_ref[0].astype(F32) + add_up(refs[:-2])
    hidden_ref[...] = hidden
    normal, _ = normalize(hidden)
    out_ref[...] = (normal * gain_ref[...].astype(F32)).astype(BF16)


def second_norm(m, rows, gain, terms):
    _, count, width = rows.shape
    narrow = jax.ShapeDtypeStruct((count, width), BF16)
    return call(
        second_norm_kernel,
        1,
        [pl.BlockSpec((1, count, width), lambda i: (m, 0, 0)), resident((1, width))]
        + [resident(piece.shape) for piece in terms],
        (resident((count, width)),) * 2,
        (jax.ShapeDtypeStruct((count, width), F32), narrow),
    )(rows, gain, *terms)


def norm_back(rows, gain, grad):
    normal, inverse = normalize(rows)
    scaled = grad * gain
    along = jnp.mean(scaled * normal, axis=-1, keepdims=True)
    inner = scaled - jnp.mean(scaled, axis=-1, keepdims=True) - normal * along
    return inverse * inner, jnp.sum(grad * normal, axis=0, keepdims=True)


def second_back_kernel(cot_ref, hidden_ref, gain_ref, *refs):
    total_ref, out_ref, ggain_ref = refs[-3:]
    grad = add_up(refs[:-3])
    part, ggain_ref[...] = norm_back(hidden_ref[...], gain_ref[...].astype(F32), grad)
    total = cot_ref[0].astype(F32) + part
    total_ref[...] = total
    out_ref[...] = total.astype(BF16)


def second_back(m, cotangent, hidden, gain, terms):
    count, width = hidden.shape
    narrow = jax.ShapeDtypeStruct((count, width), BF16)
    return call(
        second_back_kernel,
        1,
        [
            pl.BlockSpec((1, count, width), lambda i: (m, 0, 0)),
            resident((count, width)),
            resident((1, width)),
        ]
        + [resident(piece.shape) for piece in terms],
        (resident((count, width)), resident((count, width)), resident((1, width))),
        (
            jax.ShapeDtypeStruct((count, width), F32),
            narrow,
            jax.ShapeDtypeStruct((1, width), F32),
        ),
    )(cotangent, hidden, gain, *terms)


def first_back_kernel(terms, rows_ref, ghidden_ref, gain_ref, *refs):
    out_ref, ggain_ref = refs[-2:]
    grad = add_up(refs[:terms])
    part, ggain_ref[...] = norm_back(
        rows_ref[0].astype(F32), gain_ref[...].astype(F32), grad
    )
    out_ref[0] = ghidden_ref[...] + part


def first_back(m, rows, ghidden, gain, terms, before):
    micros, count, width = rows.shape
    block = pl.BlockSpec((1, count, width), lambda i: (m, 0, 0))
    specs = [block, resident((count, width)), resident((1, width))]
    specs += [resident(piece.shape) for piece in terms]
    operands = [rows, ghidden, gain, *terms]
    aliases = {}
    if before is not None:
        aliases = {len(operands): 0}
        operands.append(before)
        specs.append(pl.BlockSpec(memory_space=pl.ANY))
    return call(
        functools.partial(first_back_kernel, len(terms)),
        1,
        specs,
        (block, resident((1, width))),
        (
            jax.ShapeDtypeStruct((micros, count, width), F32),
            jax.ShapeDtypeStruct((1, width), F32),
        ),
        aliases=aliases,
    )(*operands)


def layer_end_kernel(terms, hidden_ref, *refs):
    out_ref = refs[-1]
    total = add_up(refs[:terms])
    out_ref[0] = (hidden_ref[...] + total).astype(BF16)


def layer_end(m, micros, hidden, terms, before):
    count, width = hidden.shape
    specs = [resident((count, width))] + [resident(piece.shape) for piece in terms]
    operands = [hidden, *terms]
    aliases = {}
    if before is not None:
        aliases = {len(operands): 0}
        operands.append(before)
        specs.append(pl.BlockSpec(memory_space=pl.ANY))
    return call(
        functools.partial(layer_end_kernel, len(terms)),
        1,
        specs,
        pl.BlockSpec((1, count, width), lambda i: (m, 0, 0)),
        jax.ShapeDtypeStruct((micros, count, width), BF16),
        aliases=aliases,
    )(*operands)


def gather_product_kernel(dot, pieces, *refs):
    right_ref, all_ref, out_ref = refs[pieces:]

    @pl.when(pl.program_id(0) == 0)
    def _():
        assemble(all_ref, refs[:pieces])

    out_ref[...] = dot(all_ref[...], right_ref[...]).astype(out_ref.dtype)


def gather_product(segments, right, transposed, tile=512):
    rows = sum(segment.shape[0] for segment in segments)
    width = segments[0].shape[1]
    cols = right.shape[0] if transposed else right.shape[1]
    tile = min(tile, cols)
    if transposed:
        spec = pl.BlockSpec((tile, width), lambda i: (i, 0))
    else:
        spec = pl.BlockSpec((width, tile), lambda i: (0, i))
    return call(
        functools.partial(
            gather_product_kernel, dot_nt if transposed else dot_nn, len(segments)
        ),
        cols // tile,
        [resident(segment.shape) for segment in segments] + [spec],
        (resident((rows, width)), pl.BlockSpec((rows, tile), lambda i: (0, i))),
        (jax.ShapeDtypeStruct((rows, width), BF16), jax.ShapeDtypeStruct((rows, cols), BF16)),
    )(*segments, right)


def product_scatter_kernel(transposed, lefts, rights, *refs):
    left_refs = refs[:lefts]
    right_refs = refs[lefts : lefts + rights]
    axis = 1 if transposed else 0
    width = min(
        [ref.shape[1] for ref in left_refs] + [ref.shape[axis] for ref in right_refs]
    )
    depth = sum(ref.shape[1] for ref in left_refs)
    total = None
    for start in range(0, depth, width):
        place, offset = divmod(start, left_refs[0].shape[1])
        left = left_refs[place][:, offset : offset + width]
        place, offset = divmod(start, right_refs[0].shape[axis])
        if transposed:
            term = dot_nt(left, right_refs[place][:, offset : offset + width])
        else:
            term = dot_nn(left, right_refs[place][offset : offset + width, :])
        total = term if total is None else total + term
    dissolve(refs[lefts + rights :], total)


def product_scatter(lefts, rights, transposed, counts, tile=512):
    cols = rights[0].shape[0] if transposed else rights[0].shape[1]
    tile = min(tile, cols)
    if transposed:
        specs = [pl.BlockSpec((tile, right.shape[1]), lambda i: (i, 0)) for right in rights]
    else:
        specs = [pl.BlockSpec((right.shape[0], tile), lambda i: (0, i)) for right in rights]
    return call(
        functools.partial(product_scatter_kernel, transposed, len(lefts), len(rights)),
        cols // tile,
        [resident(left.shape) for left in lefts] + specs,
        tuple(pl.BlockSpec((count, tile), lambda i: (0, i)) for count in counts),
        tuple(jax.ShapeDtypeStruct((count, cols), BF16) for count in counts),
    )(*lefts, *rights)


def weight_kernel(micros, *refs):
    out_ref = refs[-1]
    total = dot_tn(refs[0][...], refs[micros][...])
    for m in range(1, micros):
        total = total + dot_tn(refs[m][...], refs[micros + m][...])
    out_ref[...] = total.astype(out_ref.dtype)


def weight_product(lefts, rights, tile=256):
    tokens, rows = lefts[0].shape
    cols = rights[0].shape[1]
    tile = min(tile, rows)
    micros = len(lefts)
    return call(
        functools.partial(weight_kernel, micros),
        rows // tile,
        [pl.BlockSpec((tokens, tile), lambda i: (0, i))] * micros
        + [resident((tokens, cols))] * micros,
        pl.BlockSpec((tile, cols), lambda i: (i, 0)),
        jax.ShapeDtypeStruct((rows, cols), BF16),
    )(*lefts, *rights)


def feed_kernel(pieces, parts, steps, *refs):
    weights = refs[2 * pieces : 2 * (pieces + parts)]
    rows_ref, grad_ref, active_ref, gupper_ref = refs[2 * (pieces + parts) :]
    step = pl.program_id(0)

    @pl.when(step == 0)
    def _():
        assemble(rows_ref, refs[:pieces])
        assemble(grad_ref, refs[pieces : 2 * pieces])

    for part in range(parts):

        @pl.when(step // steps == part)
        def _(up_ref=weights[part], down_ref=weights[parts + part]):
            upper = dot_nn(rows_ref[...], up_ref[...])
            square = upper * upper
            slope = 0.7978845608028654
            bent = jnp.tanh(slope * upper * (1.0 + 0.044715 * square))
            half = 0.5 * (1.0 + bent)
            active_ref[...] = (upper * half).astype(BF16)
            inner = slope * (1.0 + 0.134145 * square)
            turn = half + 0.5 * upper * (1.0 - bent * bent) * inner
            gactive = dot_nt(grad_ref[...], down_ref[...])
            gupper_ref[...] = (gactive * turn).astype(BF16)


def feed_forward(segments, cotangents, ups, downs, tile=512):
    rows = sum(segment.shape[0] for segment in segments)
    width = segments[0].shape[1]
    units = ups[0].shape[1]
    tile = min(tile, units)
    steps = units // tile
    parts = len(ups)

    def column(part):
        return lambda i: (0, jnp.clip(i - part * steps, 0, steps - 1))

    def row(part):
        return lambda i: (jnp.clip(i - part * steps, 0, steps - 1), 0)

    narrow = jax.ShapeDtypeStruct((rows, parts * units), BF16)
    wide = jax.ShapeDtypeStruct((rows, width), BF16)
    return call(
        functools.partial(feed_kernel, len(segments), parts, steps),
        parts * steps,
        [resident(segment.shape) for segment in (*segments, *cotangents)]
        + [pl.BlockSpec((width, tile), column(part)) for part in range(parts)]
        + [pl.BlockSpec((tile, width), row(part)) for part in range(parts)],
        (resident((rows, width)),) * 2 + (pl.BlockSpec((rows, tile), lambda i: (0, i)),) * 2,
        (wide, wide, narrow, narrow),
        limit=44,
    )(*segments, *cotangents, *ups, *downs)


def decay_table(log_gamma, size, scale):
    row = lax.broadcasted_iota(jnp.int32, (size, size), 0)
    col = lax.broadcasted_iota(jnp.int32, (size, size), 1)
    table = jnp.exp((row - col).astype(F32) * log_gamma) * scale
    return table, jnp.where(row >= col, table, 0.0)


def pair_scale(docs, i, j, log_gamma, size):
    same = jnp.logical_and(docs[i] == docs[j], docs[i] >= 0)
    far = jnp.exp(jnp.full((1, 1), (i - j) * size, F32) * log_gamma)
    return jnp.where(same, far, 0.0)


def retention_forward_kernel(
    blocks, kd, vd, me_ref, docs_ref, rates_ref, proj_ref, mixed_ref, full_ref, diag_ref
):
    head = pl.program_id(0)
    size = proj_ref.shape[0] // blocks
    log_gamma = rates_ref[head]
    full_ref[...], diag_ref[...] = decay_table(log_gamma, size, kd**-0.5)
    me = me_ref[0]
    docs = [docs_ref[i] for i in range(blocks)]
    slots = [pl.ds(pl.multiple_of((i ^ me) * size, size), size) for i in range(blocks)]
    keys = slice(kd, 2 * kd)
    values = slice(2 * kd, 2 * kd + vd)
    for i in range(blocks):
        query = proj_ref[slots[i], :kd]
        total = None
        for j in range(i + 1):
            table = diag_ref if j == i else full_ref
            raw = dot_nt(query, proj_ref[slots[j], keys])
            scores = (raw * (table[...] * pair_scale(docs, i, j, log_gamma, size))).astype(BF16)
            term = dot_nn(scores, proj_ref[slots[j], values])
            total = term if total is None else total + term
        center = total - jnp.mean(total, axis=-1, keepdims=True)
        variance = jnp.mean(center * center, axis=-1, keepdims=True)
        normal = center * lax.rsqrt(jnp.maximum(variance, GROUP_FLOOR))
        gate = proj_ref[slots[i], 2 * kd + vd :].astype(F32)
        mixed_ref[slots[i], :] = (gate * jax.nn.sigmoid(gate) * normal).astype(BF16)


def retention_backward_kernel(
    head,
    blocks,
    kd,
    vd,
    me_ref,
    docs_ref,
    rates_ref,
    proj_ref,
    grad_ref,
    gproj_ref,
    full_ref,
    diag_ref,
    gkey_ref,
    gvalue_ref,
):
    size = proj_ref.shape[0] // blocks
    log_gamma = rates_ref[head]
    full_ref[...], diag_ref[...] = decay_table(log_gamma, size, kd**-0.5)
    me = me_ref[0]
    docs = [docs_ref[i] for i in range(blocks)]
    slots = [pl.ds(pl.multiple_of((i ^ me) * size, size), size) for i in range(blocks)]
    keys = slice(kd, 2 * kd)
    values = slice(2 * kd, 2 * kd + vd)
    gates = slice(2 * kd + vd, 2 * kd + 2 * vd)
    for i in range(blocks):
        query = proj_ref[slots[i], :kd]
        total = None
        masks = []
        kept = []
        for j in range(i + 1):
            table = diag_ref if j == i else full_ref
            mask = table[...] * pair_scale(docs, i, j, log_gamma, size)
            raw = dot_nt(query, proj_ref[slots[j], keys])
            scores = (raw * mask).astype(BF16)
            term = dot_nn(scores, proj_ref[slots[j], values])
            total = term if total is None else total + term
            kept.append(scores)
            masks.append(mask)
        center = total - jnp.mean(total, axis=-1, keepdims=True)
        variance = jnp.mean(center * center, axis=-1, keepdims=True)
        inverse = lax.rsqrt(jnp.maximum(variance, GROUP_FLOOR))
        normal = center * inverse
        gate = proj_ref[slots[i], gates].astype(F32)
        grad = grad_ref[slots[i], :].astype(F32)
        sig = jax.nn.sigmoid(gate)
        ggate = grad * normal * (sig * (1.0 + gate * (1.0 - sig)))
        gproj_ref[slots[i], gates] = ggate.astype(BF16)
        gnormal = grad * gate * sig
        along = jnp.mean(gnormal * normal, axis=-1, keepdims=True)
        along = jnp.where(variance > GROUP_FLOOR, along, 0.0)
        gcenter = inverse * (gnormal - normal * along)
        gret = (gcenter - jnp.mean(gcenter, axis=-1, keepdims=True)).astype(BF16)
        gquery = None
        for j in range(i + 1):
            graw = dot_nt(gret, proj_ref[slots[j], values])
            graw = (graw * masks[j]).astype(BF16)
            term = dot_nn(graw, proj_ref[slots[j], keys])
            gquery = term if gquery is None else gquery + term
            place = pl.ds(j * size, size)
            gkey = dot_tn(graw, query)
            gvalue = dot_tn(kept[j], gret)
            if j == i:
                gkey_ref[place, :] = gkey
                gvalue_ref[place, :] = gvalue
            else:
                gkey_ref[place, :] += gkey
                gvalue_ref[place, :] += gvalue
        gproj_ref[slots[i], :kd] = gquery.astype(BF16)
    for i in range(blocks):
        place = pl.ds(i * size, size)
        gproj_ref[slots[i], keys] = gkey_ref[place, :].astype(BF16)
        gproj_ref[slots[i], values] = gvalue_ref[place, :].astype(BF16)


def retention_forward(blocks, heads, kd, vd, me, docs, rates, proj):
    length = proj.shape[0]
    size = length // blocks
    return call(
        functools.partial(retention_forward_kernel, blocks, kd, vd),
        heads,
        [smem(), smem(), smem(), pl.BlockSpec((length, 2 * (kd + vd)), lambda h: (0, h))],
        pl.BlockSpec((length, vd), lambda h: (0, h)),
        jax.ShapeDtypeStruct((length, heads * vd), BF16),
        [pltpu.VMEM((size, size), F32)] * 2,
    )(me, docs, rates, proj)


def retention_backward(head, blocks, kd, vd, me, docs, rates, proj, grad):
    length = proj.shape[0]
    size = length // blocks
    width = 2 * (kd + vd)
    one = pl.Buffered(1)
    return call(
        functools.partial(retention_backward_kernel, head, blocks, kd, vd),
        1,
        [
            smem(),
            smem(),
            smem(),
            pl.BlockSpec((length, width), lambda i: (0, head), pipeline_mode=one),
            pl.BlockSpec((length, vd), lambda i: (0, head), pipeline_mode=one),
        ],
        resident((length, width)),
        jax.ShapeDtypeStruct((length, width), BF16),
        [pltpu.VMEM((size, size), F32)] * 2
        + [pltpu.VMEM((length, kd), F32), pltpu.VMEM((length, vd), F32)],
    )(me, docs, rates, proj, grad)


def body(
    layer_in,
    norm1_gain,
    w_query,
    w_key,
    w_value,
    w_gate,
    w_out,
    norm2_gain,
    w_up,
    w_down,
    decay_rates,
    seq_counts,
    out_grad,
):
    heads = decay_rates.shape[0]
    kd = w_query.shape[1] // heads
    vd = w_value.shape[1] // heads
    micros, rows_dev, width = layer_in.shape
    blocks = lax.axis_size("mp")
    length = rows_dev * blocks
    counts = segment_rows(rows_dev)
    pieces = []
    for h in range(heads):
        pieces += [
            w_query[:, h * kd : (h + 1) * kd],
            w_key[:, h * kd : (h + 1) * kd],
            w_value[:, h * vd : (h + 1) * vd],
            w_gate[:, h * vd : (h + 1) * vd],
        ]
    w_in = jnp.concatenate(pieces, 1)
    gain_one = norm1_gain.reshape(1, -1)
    gain_two = norm2_gain.reshape(1, -1)
    rates = jnp.log1p(-decay_rates)
    me = lax.axis_index("mp").reshape(1).astype(jnp.int32)
    starts = jnp.arange(blocks, dtype=jnp.int32) * rows_dev
    a, b = range(micros)
    docs = [document_ids(seq_counts[0, m], starts, length) for m in (a, b)]
    forward = (blocks, heads, kd, vd, me)

    def backward(h, m, proj, grad):
        return retention_backward(h, blocks, kd, vd, me, docs[m], rates, proj, grad)

    def neighbour_eighths(*earlier):
        if blocks != 4:
            return []
        place = lax.axis_index("dp")
        parts = []
        for weight in (w_up, w_down):
            count = weight.shape[0] // lax.axis_size("dp")
            parts.append(lax.dynamic_slice_in_dim(weight, place * count, count, 0))
        return [move(part, "mp", 2) for part in after(parts, earlier)]

    def neighbour_weights(parts, *earlier):
        return [
            lax.all_gather(part, "dp", axis=0, tiled=True) for part in after(parts, earlier)
        ]

    def pair_sum(total, dim):
        if blocks != 4:
            return total
        half = total.shape[1 - dim] // 2
        own = lax.slice_in_dim(total, 0, half, axis=1 - dim)
        other = lax.slice_in_dim(total, half, 2 * half, axis=1 - dim)
        return own.astype(F32) + move(other, "mp", 2).astype(F32)

    def weight_sum(total, dim):
        return lax.psum_scatter(total, "dp", scatter_dimension=dim, tiled=True)

    go_one_a = Gather(first_norm(a, layer_in, gain_one))
    normed_b = first_norm(b, after(layer_in, go_one_a.rows, w_in), gain_one)
    go_one_a.middle(normed_b)
    go_one_b = Gather(after(normed_b, go_one_a.early))
    eighths = neighbour_eighths(normed_b, go_one_a.early)
    gathered_a, proj_a = gather_product(go_one_a.result(), w_in, False)
    more = neighbour_weights(eighths, proj_a)
    cot_a = PairGather(after(out_grad[a], proj_a))
    mixed_a = retention_forward(*forward, docs[a], rates, proj_a)
    go_one_b.middle(mixed_a)
    sum_one_a = ScatterSum(
        product_scatter([after(mixed_a, go_one_b.early)], [w_out], False, counts)
    )
    gathered_b, proj_b = gather_product(go_one_b.result(sum_one_a.own), w_in, False)
    sum_one_a.middle(proj_b)
    mixed_b = retention_forward(*forward, docs[b], rates, after(proj_b, sum_one_a.early))
    sum_one_b = ScatterSum(product_scatter([mixed_b], [w_out], False, counts))

    ups, downs = [w_up, *more[:1]], [w_down, *more[1:]]
    pair = counts if blocks != 4 else [rows_dev] * 2
    hidden_a, normed = second_norm(a, layer_in, gain_two, sum_one_a.result(sum_one_b.own))
    go_two_a = PairGather(normed)
    sum_one_b.middle(hidden_a)
    cot_b = PairGather(after(out_grad[b], hidden_a, sum_one_b.early))
    rows_two_a, cotangent_a, active_a, gupper_a = feed_forward(
        go_two_a.result(sum_one_b.early), cot_a.result(), ups, downs
    )
    hidden_b, normed = second_norm(b, layer_in, gain_two, sum_one_b.result(active_a))
    go_two_b = PairGather(normed)
    sum_three_a = PairScatter(
        product_scatter([after(gupper_a, hidden_b)], ups, True, pair)
    )
    rows_two_b, cotangent_b, active_b, gupper_b = feed_forward(
        go_two_b.result(sum_three_a.own), cot_b.result(), ups, downs
    )
    dw_down = weight_product((active_a, active_b), (cotangent_a, cotangent_b))
    down_total = weight_sum(dw_down, 1)
    sum_three_b = PairScatter(
        product_scatter([after(gupper_b, dw_down)], ups, True, pair)
    )
    ghidden_a, normed, gain_two_a = second_back(
        a, out_grad, hidden_a, gain_two, sum_three_a.result(sum_three_b.own)
    )
    go_three_a = Gather(normed)
    dw_up = weight_product(
        after((rows_two_a, rows_two_b), ghidden_a), (gupper_a, gupper_b)
    )
    up_total = weight_sum(dw_up, 0)
    go_three_a.middle(dw_up)
    ghidden_b, normed, gain_two_b = second_back(
        b, out_grad, hidden_b, gain_two, sum_three_b.result(dw_up, go_three_a.early)
    )
    go_three_b = Gather(normed)

    branch_a, gmixed_a = gather_product(go_three_a.result(ghidden_b), w_out, True)
    gproj_a = []
    last = gmixed_a
    for h in range(heads):
        gproj_a.append(backward(h, a, proj_a, after(gmixed_a, last)))
        if h == 0:
            go_three_b.middle(gproj_a[0])
        last = (gproj_a[h], go_three_b.early)
    gnormed_a = product_scatter(after(gproj_a, last), [w_in], True, counts)
    branch_b, gmixed_b = gather_product(go_three_b.result(gnormed_a), w_out, True)
    dw_out = weight_product(
        after((mixed_a, mixed_b), down_total), (branch_a, after(branch_b, gmixed_b))
    )
    grad_w_out = weight_sum(dw_out, 1)
    sum_four_a = ScatterSum(after(gnormed_a, dw_out))
    gproj_b = []
    grad_w_in = []
    last = dw_out
    for h in range(heads):
        gproj_b.append(backward(h, b, proj_b, after(gmixed_b, last)))
        last = weight_product((gathered_a, gathered_b), (gproj_a[h], gproj_b[h]))
        grad_w_in.append(weight_sum(last, 0))
        if h == 0:
            sum_four_a.middle(last)
            last = (last, sum_four_a.early)
    gnormed_b = product_scatter(after(gproj_b, last, up_total), [w_in], True, counts)
    sum_four_b = ScatterSum(gnormed_b)
    feed_a = product_scatter([after(active_a, gnormed_b)], downs, False, pair)
    sum_two_a = PairScatter(feed_a)
    feed_b = product_scatter([after(active_b, feed_a)], downs, False, pair)
    sum_two_b = PairScatter(feed_b)
    sum_four_b.middle(feed_b)
    grad_input, gain_one_a = first_back(
        a, layer_in, ghidden_a, gain_one, sum_four_a.result(feed_b, sum_four_b.early), None
    )
    layer_out = layer_end(a, micros, hidden_a, sum_two_a.result(grad_input), None)
    layer_out = layer_end(b, micros, hidden_b, sum_two_b.result(), layer_out)
    grad_input, gain_one_b = first_back(
        b, layer_in, ghidden_b, gain_one, sum_four_b.result(layer_out), grad_input
    )
    grad_w_down = pair_sum(down_total, 1)
    grad_w_up = pair_sum(up_total, 0)

    def columns(start, stop):
        return jnp.concatenate([grad[:, start:stop] for grad in grad_w_in], 1).astype(F32)

    gains = small_sum(
        jnp.concatenate([gain_one_a + gain_one_b, gain_two_a + gain_two_b], 0)
    )
    return (
        layer_out,
        grad_input,
        gains[0],
        columns(0, kd),
        columns(kd, 2 * kd),
        columns(2 * kd, 2 * kd + vd),
        columns(2 * kd + vd, 2 * (kd + vd)),
        grad_w_out.astype(F32),
        gains[1],
        grad_w_up.astype(F32),
        grad_w_down.astype(F32),
    )


def solution(mesh):
    in_specs = (
        P(None, ("dp", "mp"), None),
        P(),
        P(None, "mp"),
        P(None, "mp"),
        P(None, "mp"),
        P(None, "mp"),
        P("mp", None),
        P(),
        P(None, "mp"),
        P("mp", None),
        P("mp"),
        P("dp", None, None),
        P(None, ("dp", "mp"), None),
    )
    out_specs = (
        P(None, ("dp", "mp"), None),
        P(None, ("dp", "mp"), None),
        P("dp"),
        P("dp", "mp"),
        P("dp", "mp"),
        P("dp", "mp"),
        P("dp", "mp"),
        P("mp", "dp"),
        P("dp"),
        P("dp", "mp"),
        P("mp", "dp"),
    )
    return jax.shard_map(body, mesh=mesh, in_specs=in_specs, out_specs=out_specs, check_vma=False)
```

```python
import functools

import jax
import jax.numpy as jnp
from jax import lax
from jax.experimental import pallas as pl
from jax.experimental.pallas import tpu as pltpu
from jax.sharding import PartitionSpec as P

NORM_EPS = 1e-05
GROUP_FLOOR = 1.0
BF16 = jnp.bfloat16
F32 = jnp.float32
TINY = pl.CostEstimate(flops=1, bytes_accessed=1, transcendentals=0)


def document_ids(counts, position, length):
    half_len = length // 2
    quarter_len = length // 4
    long_end = counts[2] * length
    half_end = long_end + counts[1] * half_len
    quarter_end = half_end + counts[0] * quarter_len
    long_ids = position // length
    half_ids = counts[2] + (position - long_end) // half_len
    quarter_ids = counts[2] + counts[1] + (position - half_end) // quarter_len
    inner = jnp.where(position < quarter_end, quarter_ids, -1)
    inner = jnp.where(position < half_end, half_ids, inner)
    return jnp.where(position < long_end, long_ids, inner)


def dot_nt(left, right):
    return lax.dot_general(left, right, (((1,), (1,)), ((), ())), preferred_element_type=F32)


def dot_tn(left, right):
    return lax.dot_general(left, right, (((0,), (0,)), ((), ())), preferred_element_type=F32)


def dot_nn(left, right):
    return jnp.dot(left, right, preferred_element_type=F32)


def move(value, axis, step):
    size = lax.axis_size(axis)
    return lax.ppermute(value, axis, [(i, i ^ step) for i in range(size)])


def after(value, *earlier):
    return lax.optimization_barrier((value, earlier))[0]


def fence(*values):
    return lax.optimization_barrier(values)


class Transfer:
    def __init_subclass__(cls):
        jax.tree_util.register_pytree_node(
            cls, lambda self: (self.parts(), None), lambda _, parts: cls.rebuild(parts)
        )

    def parts(self):
        return (self.kept, self.pieces)

    @classmethod
    def rebuild(cls, parts):
        self = object.__new__(cls)
        self.kept, self.pieces = parts
        return self

    def result(self, *earlier):
        return after([*self.kept, *self.pieces], earlier)


class Gather(Transfer):
    def __init__(self, rows):
        steps = (1, 2) if lax.axis_size("mp") == 4 else range(1, lax.axis_size("mp"))
        self.kept = [rows]
        self.pieces = [move(rows, "mp", k) for k in steps]

    def middle(self):
        if lax.axis_size("mp") == 4:
            first, second = self.pieces
            half = first.shape[0] // 2
            self.kept = [*self.kept, first, second]
            self.pieces = [move(first[:half], "mp", 2), move(second[half:], "mp", 1)]


class ScatterSum(Transfer):
    def __init__(self, segments):
        if lax.axis_size("mp") == 4:
            self.kept = [*segments[:3]]
            self.pieces = [move(segments[3], "mp", 2)]
        else:
            self.kept = [segments[0]]
            self.pieces = [move(part, "mp", k + 1) for k, part in enumerate(segments[1:])]

    def middle(self):
        if lax.axis_size("mp") == 4:
            own, first, second = self.kept
            self.kept = [own]
            self.pieces = [move(first + self.pieces[0], "mp", 1), move(second, "mp", 2)]


class PairGather(Transfer):
    def __init__(self, rows):
        steps = (1,) if lax.axis_size("mp") == 4 else range(1, lax.axis_size("mp"))
        self.kept = [rows]
        self.pieces = [move(rows, "mp", k) for k in steps]


class PairScatter(Transfer):
    def __init__(self, segments):
        self.kept = [segments[0]]
        self.pieces = [move(part, "mp", k + 1) for k, part in enumerate(segments[1:])]


def small_sum(value):
    step = lax.axis_size("mp") // 2
    while step:
        value = value + move(value, "mp", step)
        step //= 2
    step = lax.axis_size("dp") // 2
    place = lax.axis_index("dp")
    while step:
        half = value.shape[1] // 2
        low, high = value[:, :half], value[:, half:]
        upper = (place // step) % 2 == 1
        value = jnp.where(upper, high, low) + move(jnp.where(upper, low, high), "dp", step)
        step //= 2
    return value


LARGE = 5 << 19


def nbytes(array):
    return array.size * array.dtype.itemsize


def resident(shape):
    zeros = (0,) * len(shape)
    return pl.BlockSpec(tuple(shape), lambda i: zeros, pipeline_mode=pl.Buffered(1))


def smem():
    return pl.BlockSpec(memory_space=pltpu.SMEM)


def call(kernel, steps, in_specs, out_specs, out_shape, scratch=(), limit=32, aliases=None):
    name = getattr(kernel, "func", kernel).__name__.removesuffix("_kernel")
    several = isinstance(out_shape, tuple)
    outs = [
        pltpu.HBM(out.shape, out.dtype) if nbytes(out) > LARGE else out
        for out in (out_shape if several else (out_shape,))
    ]
    run = pl.pallas_call(
        kernel,
        name=name,
        grid=(steps,),
        in_specs=in_specs,
        out_specs=out_specs,
        out_shape=tuple(outs) if several else outs[0],
        scratch_shapes=list(scratch),
        input_output_aliases=aliases or {},
        compiler_params=pltpu.CompilerParams(vmem_limit_bytes=limit << 20),
        cost_estimate=TINY,
    )

    def placed(*operands):
        return run(
            *[
                pltpu.with_memory_space_constraint(operand, pltpu.HBM)
                if nbytes(operand) > LARGE
                else operand
                for operand in operands
            ]
        )

    return placed


def assemble(out_ref, refs):
    offset = 0
    for ref in refs:
        rows = ref.shape[0]
        out_ref[offset : offset + rows, :] = ref[...]
        offset += rows


def dissolve(refs, value):
    offset = 0
    for ref in refs:
        rows = ref.shape[0]
        ref[...] = value[offset : offset + rows].astype(ref.dtype)
        offset += rows


def add_up(refs):
    total = refs[0][...].astype(F32)
    for ref in refs[1:]:
        total = total + ref[...].astype(F32)
    return total


def normalize(rows):
    center = rows - jnp.mean(rows, axis=-1, keepdims=True)
    variance = jnp.mean(center * center, axis=-1, keepdims=True)
    inverse = lax.rsqrt(variance + NORM_EPS)
    return center * inverse, inverse


def first_norm_kernel(rows_ref, gain_ref, out_ref):
    normal, _ = normalize(rows_ref[0].astype(F32))
    out_ref[...] = (normal * gain_ref[...].astype(F32)).astype(BF16)


def first_norm(m, rows, gain):
    _, count, width = rows.shape
    narrow = jax.ShapeDtypeStruct((count, width), BF16)
    return call(
        first_norm_kernel,
        1,
        [pl.BlockSpec((1, count, width), lambda i: (m, 0, 0)), resident((1, width))],
        resident((count, width)),
        narrow,
    )(rows, gain)


def second_norm_kernel(rows_ref, gain_ref, *refs):
    hidden_ref, out_ref = refs[-2:]
    hidden = rows_ref[0].astype(F32) + add_up(refs[:-2])
    hidden_ref[...] = hidden
    normal, _ = normalize(hidden)
    out_ref[...] = (normal * gain_ref[...].astype(F32)).astype(BF16)


def second_norm(m, rows, gain, terms):
    _, count, width = rows.shape
    narrow = jax.ShapeDtypeStruct((count, width), BF16)
    return call(
        second_norm_kernel,
        1,
        [pl.BlockSpec((1, count, width), lambda i: (m, 0, 0)), resident((1, width))]
        + [resident(piece.shape) for piece in terms],
        (resident((count, width)),) * 2,
        (jax.ShapeDtypeStruct((count, width), F32), narrow),
    )(rows, gain, *terms)


def norm_back(rows, gain, grad):
    normal, inverse = normalize(rows)
    scaled = grad * gain
    along = jnp.mean(scaled * normal, axis=-1, keepdims=True)
    inner = scaled - jnp.mean(scaled, axis=-1, keepdims=True) - normal * along
    return inverse * inner, jnp.sum(grad * normal, axis=0, keepdims=True)


def second_back_kernel(cot_ref, hidden_ref, gain_ref, *refs):
    total_ref, out_ref, ggain_ref = refs[-3:]
    grad = add_up(refs[:-3])
    part, ggain_ref[...] = norm_back(hidden_ref[...], gain_ref[...].astype(F32), grad)
    total = cot_ref[0].astype(F32) + part
    total_ref[...] = total
    out_ref[...] = total.astype(BF16)


def second_back(m, cotangent, hidden, gain, terms):
    count, width = hidden.shape
    narrow = jax.ShapeDtypeStruct((count, width), BF16)
    return call(
        second_back_kernel,
        1,
        [
            pl.BlockSpec((1, count, width), lambda i: (m, 0, 0)),
            resident((count, width)),
            resident((1, width)),
        ]
        + [resident(piece.shape) for piece in terms],
        (resident((count, width)), resident((count, width)), resident((1, width))),
        (
            jax.ShapeDtypeStruct((count, width), F32),
            narrow,
            jax.ShapeDtypeStruct((1, width), F32),
        ),
    )(cotangent, hidden, gain, *terms)


def first_back_kernel(terms, rows_ref, ghidden_ref, gain_ref, *refs):
    out_ref, ggain_ref = refs[-2:]
    grad = add_up(refs[:terms])
    part, ggain_ref[...] = norm_back(
        rows_ref[0].astype(F32), gain_ref[...].astype(F32), grad
    )
    out_ref[0] = ghidden_ref[...] + part


def first_back(m, rows, ghidden, gain, terms, before):
    micros, count, width = rows.shape
    block = pl.BlockSpec((1, count, width), lambda i: (m, 0, 0))
    specs = [block, resident((count, width)), resident((1, width))]
    specs += [resident(piece.shape) for piece in terms]
    operands = [rows, ghidden, gain, *terms]
    aliases = {}
    if before is not None:
        aliases = {len(operands): 0}
        operands.append(before)
        specs.append(pl.BlockSpec(memory_space=pl.ANY))
    return call(
        functools.partial(first_back_kernel, len(terms)),
        1,
        specs,
        (block, resident((1, width))),
        (
            jax.ShapeDtypeStruct((micros, count, width), F32),
            jax.ShapeDtypeStruct((1, width), F32),
        ),
        aliases=aliases,
    )(*operands)


def layer_end_kernel(terms, hidden_ref, *refs):
    out_ref = refs[-1]
    total = add_up(refs[:terms])
    out_ref[0] = (hidden_ref[...] + total).astype(BF16)


def layer_end(m, micros, hidden, terms, before):
    count, width = hidden.shape
    specs = [resident((count, width))] + [resident(piece.shape) for piece in terms]
    operands = [hidden, *terms]
    aliases = {}
    if before is not None:
        aliases = {len(operands): 0}
        operands.append(before)
        specs.append(pl.BlockSpec(memory_space=pl.ANY))
    return call(
        functools.partial(layer_end_kernel, len(terms)),
        1,
        specs,
        pl.BlockSpec((1, count, width), lambda i: (m, 0, 0)),
        jax.ShapeDtypeStruct((micros, count, width), BF16),
        aliases=aliases,
    )(*operands)


def gather_product_kernel(dot, pieces, *refs):
    right_ref, all_ref, out_ref = refs[pieces:]

    @pl.when(pl.program_id(0) == 0)
    def _():
        assemble(all_ref, refs[:pieces])

    out_ref[...] = dot(all_ref[...], right_ref[...]).astype(out_ref.dtype)


def gather_product(segments, right, transposed, tile=512):
    rows = sum(segment.shape[0] for segment in segments)
    width = segments[0].shape[1]
    cols = right.shape[0] if transposed else right.shape[1]
    tile = min(tile, cols)
    if transposed:
        spec = pl.BlockSpec((tile, width), lambda i: (i, 0))
    else:
        spec = pl.BlockSpec((width, tile), lambda i: (0, i))
    return call(
        functools.partial(
            gather_product_kernel, dot_nt if transposed else dot_nn, len(segments)
        ),
        cols // tile,
        [resident(segment.shape) for segment in segments] + [spec],
        (resident((rows, width)), pl.BlockSpec((rows, tile), lambda i: (0, i))),
        (jax.ShapeDtypeStruct((rows, width), BF16), jax.ShapeDtypeStruct((rows, cols), BF16)),
    )(*segments, right)


def product_scatter_kernel(transposed, lefts, rights, *refs):
    left_refs = refs[:lefts]
    right_refs = refs[lefts : lefts + rights]
    axis = 1 if transposed else 0
    width = min(
        [ref.shape[1] for ref in left_refs] + [ref.shape[axis] for ref in right_refs]
    )
    depth = sum(ref.shape[1] for ref in left_refs)
    total = None
    for start in range(0, depth, width):
        place, offset = divmod(start, left_refs[0].shape[1])
        left = left_refs[place][:, offset : offset + width]
        place, offset = divmod(start, right_refs[0].shape[axis])
        if transposed:
            term = dot_nt(left, right_refs[place][:, offset : offset + width])
        else:
            term = dot_nn(left, right_refs[place][offset : offset + width, :])
        total = term if total is None else total + term
    dissolve(refs[lefts + rights :], total)


def product_scatter(lefts, rights, transposed, counts, tile=512):
    cols = rights[0].shape[0] if transposed else rights[0].shape[1]
    tile = min(tile, cols)
    if transposed:
        specs = [pl.BlockSpec((tile, right.shape[1]), lambda i: (i, 0)) for right in rights]
    else:
        specs = [pl.BlockSpec((right.shape[0], tile), lambda i: (0, i)) for right in rights]
    return call(
        functools.partial(product_scatter_kernel, transposed, len(lefts), len(rights)),
        cols // tile,
        [resident(left.shape) for left in lefts] + specs,
        tuple(pl.BlockSpec((count, tile), lambda i: (0, i)) for count in counts),
        tuple(jax.ShapeDtypeStruct((count, cols), BF16) for count in counts),
    )(*lefts, *rights)


def weight_kernel(micros, *refs):
    out_ref = refs[-1]
    total = dot_tn(refs[0][...], refs[micros][...])
    for m in range(1, micros):
        total = total + dot_tn(refs[m][...], refs[micros + m][...])
    out_ref[...] = total.astype(out_ref.dtype)


def weight_product(lefts, rights, tile=256):
    tokens, rows = lefts[0].shape
    cols = rights[0].shape[1]
    tile = min(tile, rows)
    micros = len(lefts)
    return call(
        functools.partial(weight_kernel, micros),
        rows // tile,
        [pl.BlockSpec((tokens, tile), lambda i: (0, i))] * micros
        + [resident((tokens, cols))] * micros,
        pl.BlockSpec((tile, cols), lambda i: (i, 0)),
        jax.ShapeDtypeStruct((rows, cols), BF16),
    )(*lefts, *rights)


def weight_halves_kernel(micros, *refs):
    outs = refs[2 * micros :]
    cut = outs[0].shape[1]
    for n, out_ref in enumerate(outs):
        cols = slice(n * cut, (n + 1) * cut)
        total = dot_tn(refs[0][...], refs[micros][:, cols])
        for m in range(1, micros):
            total = total + dot_tn(refs[m][...], refs[micros + m][:, cols])
        out_ref[...] = total.astype(out_ref.dtype)


def weight_halves(lefts, rights, tile=256):
    tokens, rows = lefts[0].shape
    cols = rights[0].shape[1] // 2
    tile = min(tile, rows)
    micros = len(lefts)
    return call(
        functools.partial(weight_halves_kernel, micros),
        rows // tile,
        [pl.BlockSpec((tokens, tile), lambda i: (0, i))] * micros
        + [resident((tokens, 2 * cols))] * micros,
        (pl.BlockSpec((tile, cols), lambda i: (i, 0)),) * 2,
        (jax.ShapeDtypeStruct((rows, cols), BF16),) * 2,
    )(*lefts, *rights)


def feed_kernel(pieces, parts, steps, *refs):
    weights = refs[2 * pieces : 2 * (pieces + parts)]
    rows_ref, grad_ref, active_ref, gupper_ref = refs[2 * (pieces + parts) :]
    step = pl.program_id(0)

    @pl.when(step == 0)
    def _():
        assemble(rows_ref, refs[:pieces])
        assemble(grad_ref, refs[pieces : 2 * pieces])

    for part in range(parts):

        @pl.when(step // steps == part)
        def _(up_ref=weights[part], down_ref=weights[parts + part]):
            upper = dot_nn(rows_ref[...], up_ref[...])
            square = upper * upper
            slope = 0.7978845608028654
            bent = jnp.tanh(slope * upper * (1.0 + 0.044715 * square))
            half = 0.5 * (1.0 + bent)
            active_ref[...] = (upper * half).astype(BF16)
            inner = slope * (1.0 + 0.134145 * square)
            turn = half + 0.5 * upper * (1.0 - bent * bent) * inner
            gactive = dot_nt(grad_ref[...], down_ref[...])
            gupper_ref[...] = (gactive * turn).astype(BF16)


def feed_forward(segments, cotangents, ups, downs, tile=512):
    rows = sum(segment.shape[0] for segment in segments)
    width = segments[0].shape[1]
    units = ups[0].shape[1]
    tile = min(tile, units)
    steps = units // tile
    parts = len(ups)

    def column(part):
        return lambda i: (0, jnp.clip(i - part * steps, 0, steps - 1))

    def row(part):
        return lambda i: (jnp.clip(i - part * steps, 0, steps - 1), 0)

    narrow = jax.ShapeDtypeStruct((rows, parts * units), BF16)
    wide = jax.ShapeDtypeStruct((rows, width), BF16)
    return call(
        functools.partial(feed_kernel, len(segments), parts, steps),
        parts * steps,
        [resident(segment.shape) for segment in (*segments, *cotangents)]
        + [pl.BlockSpec((width, tile), column(part)) for part in range(parts)]
        + [pl.BlockSpec((tile, width), row(part)) for part in range(parts)],
        (resident((rows, width)),) * 2 + (pl.BlockSpec((rows, tile), lambda i: (0, i)),) * 2,
        (wide, wide, narrow, narrow),
        limit=44,
    )(*segments, *cotangents, *ups, *downs)


def decay_table(log_gamma, size, scale):
    row = lax.broadcasted_iota(jnp.int32, (size, size), 0)
    col = lax.broadcasted_iota(jnp.int32, (size, size), 1)
    table = jnp.exp((row - col).astype(F32) * log_gamma) * scale
    return table, jnp.where(row >= col, table, 0.0)


def pair_scale(docs, i, j, log_gamma, size):
    same = jnp.logical_and(docs[i] == docs[j], docs[i] >= 0)
    far = jnp.exp(jnp.full((1, 1), (i - j) * size, F32) * log_gamma)
    return jnp.where(same, far, 0.0)


def retention_forward_kernel(
    blocks, kd, vd, me_ref, docs_ref, rates_ref, proj_ref, mixed_ref, full_ref, diag_ref
):
    head = pl.program_id(0)
    size = proj_ref.shape[0] // blocks
    log_gamma = rates_ref[head]
    full_ref[...], diag_ref[...] = decay_table(log_gamma, size, kd**-0.5)
    me = me_ref[0]
    docs = [docs_ref[i] for i in range(blocks)]
    slots = [pl.ds(pl.multiple_of((i ^ me) * size, size), size) for i in range(blocks)]
    keys = slice(kd, 2 * kd)
    values = slice(2 * kd, 2 * kd + vd)
    for i in range(blocks):
        query = proj_ref[slots[i], :kd]
        total = None
        for j in range(i + 1):
            table = diag_ref if j == i else full_ref
            raw = dot_nt(query, proj_ref[slots[j], keys])
            scores = (raw * (table[...] * pair_scale(docs, i, j, log_gamma, size))).astype(BF16)
            term = dot_nn(scores, proj_ref[slots[j], values])
            total = term if total is None else total + term
        center = total - jnp.mean(total, axis=-1, keepdims=True)
        variance = jnp.mean(center * center, axis=-1, keepdims=True)
        normal = center * lax.rsqrt(jnp.maximum(variance, GROUP_FLOOR))
        gate = proj_ref[slots[i], 2 * kd + vd :].astype(F32)
        mixed_ref[slots[i], :] = (gate * jax.nn.sigmoid(gate) * normal).astype(BF16)


def retention_backward_kernel(
    head,
    blocks,
    kd,
    vd,
    me_ref,
    docs_ref,
    rates_ref,
    proj_ref,
    grad_ref,
    gproj_ref,
    full_ref,
    diag_ref,
    gkey_ref,
    gvalue_ref,
):
    size = proj_ref.shape[0] // blocks
    log_gamma = rates_ref[head]
    full_ref[...], diag_ref[...] = decay_table(log_gamma, size, kd**-0.5)
    me = me_ref[0]
    docs = [docs_ref[i] for i in range(blocks)]
    slots = [pl.ds(pl.multiple_of((i ^ me) * size, size), size) for i in range(blocks)]
    keys = slice(kd, 2 * kd)
    values = slice(2 * kd, 2 * kd + vd)
    gates = slice(2 * kd + vd, 2 * kd + 2 * vd)
    for i in range(blocks):
        query = proj_ref[slots[i], :kd]
        total = None
        masks = []
        kept = []
        for j in range(i + 1):
            table = diag_ref if j == i else full_ref
            mask = table[...] * pair_scale(docs, i, j, log_gamma, size)
            raw = dot_nt(query, proj_ref[slots[j], keys])
            scores = (raw * mask).astype(BF16)
            term = dot_nn(scores, proj_ref[slots[j], values])
            total = term if total is None else total + term
            kept.append(scores)
            masks.append(mask)
        center = total - jnp.mean(total, axis=-1, keepdims=True)
        variance = jnp.mean(center * center, axis=-1, keepdims=True)
        inverse = lax.rsqrt(jnp.maximum(variance, GROUP_FLOOR))
        normal = center * inverse
        gate = proj_ref[slots[i], gates].astype(F32)
        grad = grad_ref[slots[i], :].astype(F32)
        sig = jax.nn.sigmoid(gate)
        ggate = grad * normal * (sig * (1.0 + gate * (1.0 - sig)))
        gproj_ref[slots[i], gates] = ggate.astype(BF16)
        gnormal = grad * gate * sig
        along = jnp.mean(gnormal * normal, axis=-1, keepdims=True)
        along = jnp.where(variance > GROUP_FLOOR, along, 0.0)
        gcenter = inverse * (gnormal - normal * along)
        gret = (gcenter - jnp.mean(gcenter, axis=-1, keepdims=True)).astype(BF16)
        gquery = None
        for j in range(i + 1):
            graw = dot_nt(gret, proj_ref[slots[j], values])
            graw = (graw * masks[j]).astype(BF16)
            term = dot_nn(graw, proj_ref[slots[j], keys])
            gquery = term if gquery is None else gquery + term
            place = pl.ds(j * size, size)
            gkey = dot_tn(graw, query)
            gvalue = dot_tn(kept[j], gret)
            if j == i:
                gkey_ref[place, :] = gkey
                gvalue_ref[place, :] = gvalue
            else:
                gkey_ref[place, :] += gkey
                gvalue_ref[place, :] += gvalue
        gproj_ref[slots[i], :kd] = gquery.astype(BF16)
    for i in range(blocks):
        place = pl.ds(i * size, size)
        gproj_ref[slots[i], keys] = gkey_ref[place, :].astype(BF16)
        gproj_ref[slots[i], values] = gvalue_ref[place, :].astype(BF16)


def retention_forward(blocks, heads, kd, vd, me, docs, rates, proj):
    length = proj.shape[0]
    size = length // blocks
    return call(
        functools.partial(retention_forward_kernel, blocks, kd, vd),
        heads,
        [smem(), smem(), smem(), pl.BlockSpec((length, 2 * (kd + vd)), lambda h: (0, h))],
        pl.BlockSpec((length, vd), lambda h: (0, h)),
        jax.ShapeDtypeStruct((length, heads * vd), BF16),
        [pltpu.VMEM((size, size), F32)] * 2,
    )(me, docs, rates, proj)


def retention_backward(head, blocks, kd, vd, me, docs, rates, proj, grad):
    length = proj.shape[0]
    size = length // blocks
    width = 2 * (kd + vd)
    one = pl.Buffered(1)
    return call(
        functools.partial(retention_backward_kernel, head, blocks, kd, vd),
        1,
        [
            smem(),
            smem(),
            smem(),
            pl.BlockSpec((length, width), lambda i: (0, head), pipeline_mode=one),
            pl.BlockSpec((length, vd), lambda i: (0, head), pipeline_mode=one),
        ],
        resident((length, width)),
        jax.ShapeDtypeStruct((length, width), BF16),
        [pltpu.VMEM((size, size), F32)] * 2
        + [pltpu.VMEM((length, kd), F32), pltpu.VMEM((length, vd), F32)],
    )(me, docs, rates, proj, grad)


def body(
    layer_in,
    norm1_gain,
    w_query,
    w_key,
    w_value,
    w_gate,
    w_out,
    norm2_gain,
    w_up,
    w_down,
    decay_rates,
    seq_counts,
    out_grad,
):
    heads = decay_rates.shape[0]
    kd = w_query.shape[1] // heads
    vd = w_value.shape[1] // heads
    micros, rows_dev, width = layer_in.shape
    blocks = lax.axis_size("mp")
    length = rows_dev * blocks
    tall = [rows_dev] * blocks
    pieces = []
    for h in range(heads):
        pieces += [
            w_query[:, h * kd : (h + 1) * kd],
            w_key[:, h * kd : (h + 1) * kd],
            w_value[:, h * vd : (h + 1) * vd],
            w_gate[:, h * vd : (h + 1) * vd],
        ]
    w_in = jnp.concatenate(pieces, 1)
    gain_one = norm1_gain.reshape(1, -1)
    gain_two = norm2_gain.reshape(1, -1)
    rates = jnp.log1p(-decay_rates)
    me = lax.axis_index("mp").reshape(1).astype(jnp.int32)
    starts = jnp.arange(blocks, dtype=jnp.int32) * rows_dev
    a, b = range(micros)
    docs = [document_ids(seq_counts[0, m], starts, length) for m in (a, b)]
    def backward(h, m, proj, grad):
        return retention_backward(h, blocks, kd, vd, me, docs[m], rates, proj, grad)

    up_rows, down_rows = (
        weight.shape[0] // lax.axis_size("dp") for weight in (w_up, w_down)
    )

    def eighth_rows():
        place = lax.axis_index("dp")
        up = lax.dynamic_slice_in_dim(w_up, place * up_rows, up_rows, 0)
        down = lax.dynamic_slice_in_dim(w_down, place * down_rows, down_rows, 0)
        cut = w_up.shape[1]
        return jnp.concatenate(
            [up] + [down[:, k : k + cut] for k in range(0, width, cut)], 0
        )

    def exchange(rows):
        return move(rows, "mp", 2) if blocks == 4 else rows

    def neighbour_weights(rows):
        if blocks != 4:
            return []
        down = [
            rows[k : k + down_rows] for k in range(up_rows, rows.shape[0], down_rows)
        ]
        return [
            lax.all_gather(part, "dp", axis=0, tiled=True)
            for part in (rows[:up_rows], jnp.concatenate(down, 1))
        ]

    def pair_sum(total, dim):
        if blocks != 4:
            return total
        half = total.shape[1 - dim] // 2
        own = lax.slice_in_dim(total, 0, half, axis=1 - dim)
        other = lax.slice_in_dim(total, half, 2 * half, axis=1 - dim)
        return own.astype(F32) + move(other, "mp", 2).astype(F32)

    def weight_sum(total, dim):
        return lax.psum_scatter(total, "dp", scatter_dimension=dim, tiled=True)

    normed_a = first_norm(a, layer_in, gain_one)
    normed_b = first_norm(b, after(layer_in, normed_a, w_in), gain_one)
    go_one_a = Gather(normed_a)
    eighths = eighth_rows()
    fenced = fence(go_one_a, normed_b, eighths, docs, rates, me)
    go_one_a, normed_b, eighths, docs, rates, me = fenced
    forward = (blocks, heads, kd, vd, me)
    go_one_a.middle()
    go_one_a, normed_b = fence(go_one_a, normed_b)

    go_one_b = Gather(normed_b)
    eighths = exchange(after(eighths, normed_b))
    cot_a = PairGather(after(out_grad[a], normed_b))
    gathered_a, proj_a = gather_product(go_one_a.result(), w_in, False)
    mixed_a = retention_forward(*forward, docs[a], rates, proj_a)
    go_one_b, eighths, cot_a, mixed_a = fence(go_one_b, eighths, cot_a, mixed_a)
    go_one_b.middle()
    more = neighbour_weights(eighths)
    parts = product_scatter([mixed_a], [w_out], False, tall)
    go_one_b, parts = fence(go_one_b, parts)

    sum_one_a = ScatterSum(parts)
    cot_b = PairGather(after(out_grad[b], parts))
    gathered_b, proj_b = gather_product(go_one_b.result(), w_in, False)
    sum_one_a, cot_b, proj_b = fence(sum_one_a, cot_b, proj_b)
    sum_one_a.middle()
    mixed_b = retention_forward(*forward, docs[b], rates, proj_b)
    parts = product_scatter([mixed_b], [w_out], False, tall)
    sum_one_a, parts = fence(sum_one_a, parts)

    pair = [rows_dev] * 2 if blocks == 4 else tall
    hidden_a, normed = second_norm(a, layer_in, gain_two, sum_one_a.result())
    go_two_a = PairGather(normed)
    sum_one_b = ScatterSum(parts)
    go_two_a, sum_one_b, hidden_a = fence(go_two_a, sum_one_b, hidden_a)
    sum_one_b.middle()
    sum_one_b, more = fence(sum_one_b, more)

    ups, downs = [w_up, *more[:1]], [w_down, *more[1:]]
    hidden_b, normed = second_norm(b, layer_in, gain_two, sum_one_b.result())
    go_two_b = PairGather(normed)
    rows_two_a, cotangent_a, active_a, gupper_a = feed_forward(
        go_two_a.result(hidden_b), cot_a.result(), ups, downs
    )
    parts = product_scatter([gupper_a], ups, True, pair)
    go_two_b, parts = fence(go_two_b, parts)

    sum_three_a = PairScatter(parts)
    rows_two_b, cotangent_b, active_b, gupper_b = feed_forward(
        go_two_b.result(), cot_b.result(), ups, downs
    )
    parts = product_scatter([gupper_b], ups, True, pair)
    sum_three_a, parts, actives = fence(sum_three_a, parts, (active_a, active_b))

    ghidden_a, normed, gain_two_a = second_back(
        a, out_grad, hidden_a, gain_two, sum_three_a.result()
    )
    go_three_a = Gather(normed)
    sum_three_b = PairScatter(parts)
    dw_down = weight_product(after(actives, ghidden_a), (cotangent_a, cotangent_b))
    down_total = weight_sum(dw_down, 1)
    ups_left = after((rows_two_a, rows_two_b), dw_down)
    if blocks == 4:
        dw_up, dw_up_other = weight_halves(ups_left, (gupper_a, gupper_b))
    else:
        dw_up = dw_up_other = weight_product(ups_left, (gupper_a, gupper_b))
    fenced = fence(go_three_a, sum_three_b, dw_up, dw_up_other, actives)
    go_three_a, sum_three_b, dw_up, dw_up_other, actives = fenced
    go_three_a.middle()
    feeds = [product_scatter([active], downs, False, pair) for active in actives]
    go_three_a, sum_three_b, feeds = fence(go_three_a, sum_three_b, feeds)

    ghidden_b, normed, gain_two_b = second_back(
        b, out_grad, hidden_b, gain_two, sum_three_b.result()
    )
    go_three_b = Gather(normed)
    branch_a, gmixed_a = gather_product(go_three_a.result(ghidden_b), w_out, True)
    gproj_a = [backward(0, a, proj_a, gmixed_a)]
    go_three_b, gproj_a, gmixed_a = fence(go_three_b, gproj_a, gmixed_a)
    go_three_b.middle()
    for h in range(1, heads):
        gproj_a.append(backward(h, a, proj_a, gmixed_a))
    fenced = fence(go_three_b, gproj_a, feeds, dw_up_other, down_total)
    go_three_b, gproj_a, feeds, dw_up_other, down_total = fenced

    count = 2 + heads
    cut = width // count
    others = [dw_up_other[k : k + cut] for k in range(0, width, cut)]
    sums_two = [PairScatter(feeds[0])]
    others[0] = exchange(others[0])
    branch_b, gmixed_b = gather_product(go_three_b.result(), w_out, True)
    dw_out = weight_product((mixed_a, mixed_b), (branch_a, after(branch_b, gmixed_b)))
    sums_two[0], others, dw_out, gmixed_b, feeds = fence(
        sums_two[0], others, dw_out, gmixed_b, feeds
    )
    grad_w_out = weight_sum(dw_out, 1)
    sums_two.append(PairScatter(feeds[1]))
    gproj_b = []
    grad_w_in = []
    for h in range(heads):
        others[1 + h] = exchange(others[1 + h])
        gproj_b.append(backward(h, b, proj_b, gmixed_b))
        dw_in = weight_product((gathered_a, gathered_b), (gproj_a[h], gproj_b[h]))
        sums_two, others, dw_in, gproj_b, gproj_a, gmixed_b = fence(
            sums_two, others, dw_in, gproj_b, gproj_a, gmixed_b
        )
        grad_w_in.append(weight_sum(dw_in, 0))
    others[-1] = exchange(others[-1])
    layer_out = layer_end(a, micros, hidden_a, sums_two[0].result(), None)
    layer_out = layer_end(b, micros, hidden_b, sums_two[1].result(), layer_out)
    parts = product_scatter(after(gproj_a, layer_out), [w_in], True, tall)
    others, parts, grad_w_out, layer_out = fence(others, parts, grad_w_out, layer_out)

    sum_four_a = ScatterSum(parts)
    if blocks == 4:
        other = jnp.concatenate(others, 0)
        dw_up = (dw_up.astype(F32) + after(other, parts).astype(F32)).astype(BF16)
    parts = product_scatter(after(gproj_b, dw_up), [w_in], True, tall)
    sum_four_a, parts, dw_up, grad_w_in[0] = fence(sum_four_a, parts, dw_up, grad_w_in[0])
    grad_w_up = weight_sum(dw_up, 0)
    sum_four_a.middle()
    sum_four_b = ScatterSum(parts)
    sum_four_a, sum_four_b, down_total = fence(sum_four_a, sum_four_b, down_total)
    sum_four_b.middle()
    grad_w_down = pair_sum(down_total, 1)
    grad_input, gain_one_a = first_back(
        a, layer_in, ghidden_a, gain_one, sum_four_a.result(), None
    )
    sum_four_b, grad_input, grad_w_down, grad_w_in[-1] = fence(
        sum_four_b, grad_input, grad_w_down, grad_w_in[-1]
    )
    grad_input, gain_one_b = first_back(
        b, layer_in, ghidden_b, gain_one, sum_four_b.result(), grad_input
    )

    def columns(start, stop):
        return jnp.concatenate([grad[:, start:stop] for grad in grad_w_in], 1).astype(F32)

    gains = small_sum(
        jnp.concatenate([gain_one_a + gain_one_b, gain_two_a + gain_two_b], 0)
    )
    return (
        layer_out,
        grad_input,
        gains[0],
        columns(0, kd),
        columns(kd, 2 * kd),
        columns(2 * kd, 2 * kd + vd),
        columns(2 * kd + vd, 2 * (kd + vd)),
        grad_w_out.astype(F32),
        gains[1],
        grad_w_up.astype(F32),
        grad_w_down.astype(F32),
    )


def solution(mesh):
    in_specs = (
        P(None, ("dp", "mp"), None),
        P(),
        P(None, "mp"),
        P(None, "mp"),
        P(None, "mp"),
        P(None, "mp"),
        P("mp", None),
        P(),
        P(None, "mp"),
        P("mp", None),
        P("mp"),
        P("dp", None, None),
        P(None, ("dp", "mp"), None),
    )
    out_specs = (
        P(None, ("dp", "mp"), None),
        P(None, ("dp", "mp"), None),
        P("dp"),
        P("dp", "mp"),
        P("dp", "mp"),
        P("dp", "mp"),
        P("dp", "mp"),
        P("mp", "dp"),
        P("dp"),
        P("dp", "mp"),
        P("mp", "dp"),
    )
    return jax.shard_map(body, mesh=mesh, in_specs=in_specs, out_specs=out_specs, check_vma=False)
```

```python
import functools

import jax
import jax.numpy as jnp
from jax import lax
from jax.experimental import pallas as pl
from jax.experimental.pallas import tpu as pltpu
from jax.sharding import PartitionSpec as P

NORM_EPS = 1e-05
GROUP_FLOOR = 1.0
BF16 = jnp.bfloat16
F32 = jnp.float32
TINY = pl.CostEstimate(flops=1, bytes_accessed=1, transcendentals=0)


def document_ids(counts, position, length):
    half_len = length // 2
    quarter_len = length // 4
    long_end = counts[2] * length
    half_end = long_end + counts[1] * half_len
    quarter_end = half_end + counts[0] * quarter_len
    long_ids = position // length
    half_ids = counts[2] + (position - long_end) // half_len
    quarter_ids = counts[2] + counts[1] + (position - half_end) // quarter_len
    inner = jnp.where(position < quarter_end, quarter_ids, -1)
    inner = jnp.where(position < half_end, half_ids, inner)
    return jnp.where(position < long_end, long_ids, inner)


def dot_nt(left, right):
    return lax.dot_general(left, right, (((1,), (1,)), ((), ())), preferred_element_type=F32)


def dot_tn(left, right):
    return lax.dot_general(left, right, (((0,), (0,)), ((), ())), preferred_element_type=F32)


def dot_nn(left, right):
    return jnp.dot(left, right, preferred_element_type=F32)


def move(value, axis, step):
    size = lax.axis_size(axis)
    return lax.ppermute(value, axis, [(i, i ^ step) for i in range(size)])


def after(value, *earlier):
    return lax.optimization_barrier((value, earlier))[0]


def fence(*values):
    return lax.optimization_barrier(values)


class Transfer:
    def __init_subclass__(cls):
        jax.tree_util.register_pytree_node(
            cls, lambda self: (self.parts(), None), lambda _, parts: cls.rebuild(parts)
        )

    def parts(self):
        return (self.kept, self.pieces)

    @classmethod
    def rebuild(cls, parts):
        self = object.__new__(cls)
        self.kept, self.pieces = parts
        return self

    def result(self, *earlier):
        return after([*self.kept, *self.pieces], earlier)


class Gather(Transfer):
    def __init__(self, rows):
        steps = (1, 2) if lax.axis_size("mp") == 4 else range(1, lax.axis_size("mp"))
        self.kept = [rows]
        self.pieces = [move(rows, "mp", k) for k in steps]

    def middle(self):
        if lax.axis_size("mp") == 4:
            first, second = self.pieces
            half = first.shape[0] // 2
            self.kept = [*self.kept, first, second]
            self.pieces = [move(first[:half], "mp", 2), move(second[half:], "mp", 1)]


class ScatterSum(Transfer):
    def __init__(self, segments):
        if lax.axis_size("mp") == 4:
            self.kept = [*segments[:3]]
            upper, lower = segments[3:]
            self.pieces = [move(upper, "mp", 1), move(lower, "mp", 2)]
        else:
            self.kept = [segments[0]]
            self.pieces = [move(part, "mp", k + 1) for k, part in enumerate(segments[1:])]

    def middle(self):
        if lax.axis_size("mp") == 4:
            own, first, second = self.kept
            upper, lower = self.pieces
            half = upper.shape[0]
            first = jnp.concatenate([first[:half], first[half:] + lower], 0)
            second = jnp.concatenate([second[:half] + upper, second[half:]], 0)
            self.kept = [own]
            self.pieces = [move(first, "mp", 1), move(second, "mp", 2)]


class TallScatterSum(ScatterSum):
    def __init__(self, segments):
        if lax.axis_size("mp") == 4:
            self.kept = [*segments[:3]]
            self.pieces = [move(segments[3], "mp", 2)]
        else:
            super().__init__(segments)

    def middle(self):
        if lax.axis_size("mp") == 4:
            own, first, second = self.kept
            self.kept = [own]
            self.pieces = [move(first + self.pieces[0], "mp", 1), move(second, "mp", 2)]


class PairGather(Transfer):
    def __init__(self, rows):
        steps = (1,) if lax.axis_size("mp") == 4 else range(1, lax.axis_size("mp"))
        self.kept = [rows]
        self.pieces = [move(rows, "mp", k) for k in steps]


class PairScatter(Transfer):
    def __init__(self, segments):
        self.kept = [segments[0]]
        self.pieces = [move(part, "mp", k + 1) for k, part in enumerate(segments[1:])]


def small_sum(value):
    value = value + sum(move(value, "mp", k) for k in range(1, lax.axis_size("mp")))
    half = lax.axis_size("dp") // 2
    place = lax.axis_index("dp")
    split = value.reshape(value.shape[0], half, 2, -1)
    even = place % 2 == 0
    kept = jnp.where(even, split[:, :, 0], split[:, :, 1])
    sent = jnp.where(even, split[:, :, 1], split[:, :, 0])
    kept = kept + move(sent, "dp", 1)
    pick = lambda chip: lax.dynamic_index_in_dim(kept, chip, 1, False)
    chip = place // 2
    return pick(chip) + sum(move(pick(chip ^ k), "dp", 2 * k) for k in range(1, half))


LARGE, SMALL = 5 << 19, 1 << 18


def nbytes(array):
    return array.size * array.dtype.itemsize


def resident(shape):
    zeros = (0,) * len(shape)
    return pl.BlockSpec(tuple(shape), lambda i: zeros, pipeline_mode=pl.Buffered(1))


def smem():
    return pl.BlockSpec(memory_space=pltpu.SMEM)


def call(kernel, steps, in_specs, out_specs, out_shape, scratch=(), limit=32, aliases=None, far=LARGE):
    name = getattr(kernel, "func", kernel).__name__.removesuffix("_kernel")
    several = isinstance(out_shape, tuple)
    outs = [
        pltpu.HBM(out.shape, out.dtype) if nbytes(out) > far else out
        for out in (out_shape if several else (out_shape,))
    ]
    run = pl.pallas_call(
        kernel,
        name=name,
        grid=(steps,),
        in_specs=in_specs,
        out_specs=out_specs,
        out_shape=tuple(outs) if several else outs[0],
        scratch_shapes=list(scratch),
        input_output_aliases=aliases or {},
        compiler_params=pltpu.CompilerParams(vmem_limit_bytes=limit << 20),
        cost_estimate=TINY,
    )

    def placed(*operands):
        return run(
            *[
                pltpu.with_memory_space_constraint(operand, pltpu.HBM)
                if nbytes(operand) > far
                else operand
                for operand in operands
            ]
        )

    return placed


def assemble(out_ref, refs):
    offset = 0
    for ref in refs:
        rows = ref.shape[0]
        out_ref[offset : offset + rows, :] = ref[...]
        offset += rows


def dissolve(refs, value):
    offset = 0
    for ref in refs:
        rows = ref.shape[0]
        ref[...] = value[offset : offset + rows].astype(ref.dtype)
        offset += rows


def add_up(refs):
    total = refs[0][...].astype(F32)
    for ref in refs[1:]:
        total = total + ref[...].astype(F32)
    return total


def normalize(rows):
    center = rows - jnp.mean(rows, axis=-1, keepdims=True)
    variance = jnp.mean(center * center, axis=-1, keepdims=True)
    inverse = lax.rsqrt(variance + NORM_EPS)
    return center * inverse, inverse


def first_norm_kernel(rows_ref, gain_ref, out_ref):
    normal, _ = normalize(rows_ref[0].astype(F32))
    out_ref[...] = (normal * gain_ref[...].astype(F32)).astype(BF16)


def first_norm(m, rows, gain):
    _, count, width = rows.shape
    narrow = jax.ShapeDtypeStruct((count, width), BF16)
    return call(
        first_norm_kernel,
        1,
        [pl.BlockSpec((1, count, width), lambda i: (m, 0, 0)), resident((1, width))],
        resident((count, width)),
        narrow,
    )(rows, gain)


def second_norm_kernel(rows_ref, gain_ref, *refs):
    hidden_ref, out_ref = refs[-2:]
    hidden = rows_ref[0].astype(F32) + add_up(refs[:-2])
    hidden_ref[...] = hidden
    normal, _ = normalize(hidden)
    out_ref[...] = (normal * gain_ref[...].astype(F32)).astype(BF16)


def second_norm(m, rows, gain, terms):
    _, count, width = rows.shape
    narrow = jax.ShapeDtypeStruct((count, width), BF16)
    return call(
        second_norm_kernel,
        1,
        [pl.BlockSpec((1, count, width), lambda i: (m, 0, 0)), resident((1, width))]
        + [resident(piece.shape) for piece in terms],
        (resident((count, width)),) * 2,
        (jax.ShapeDtypeStruct((count, width), F32), narrow),
    )(rows, gain, *terms)


def norm_back(rows, gain, grad):
    normal, inverse = normalize(rows)
    scaled = grad * gain
    along = jnp.mean(scaled * normal, axis=-1, keepdims=True)
    inner = scaled - jnp.mean(scaled, axis=-1, keepdims=True) - normal * along
    return inverse * inner, jnp.sum(grad * normal, axis=0, keepdims=True)


def second_back_kernel(cot_ref, hidden_ref, gain_ref, *refs):
    total_ref, out_ref, ggain_ref = refs[-3:]
    grad = add_up(refs[:-3])
    part, ggain_ref[...] = norm_back(hidden_ref[...], gain_ref[...].astype(F32), grad)
    total = cot_ref[0].astype(F32) + part
    total_ref[...] = total
    out_ref[...] = total.astype(BF16)


def second_back(m, cotangent, hidden, gain, terms):
    count, width = hidden.shape
    narrow = jax.ShapeDtypeStruct((count, width), BF16)
    return call(
        second_back_kernel,
        1,
        [
            pl.BlockSpec((1, count, width), lambda i: (m, 0, 0)),
            resident((count, width)),
            resident((1, width)),
        ]
        + [resident(piece.shape) for piece in terms],
        (resident((count, width)), resident((count, width)), resident((1, width))),
        (
            jax.ShapeDtypeStruct((count, width), F32),
            narrow,
            jax.ShapeDtypeStruct((1, width), F32),
        ),
    )(cotangent, hidden, gain, *terms)


def first_back_kernel(terms, rows_ref, ghidden_ref, gain_ref, *refs):
    out_ref, ggain_ref = refs[-2:]
    grad = add_up(refs[:terms])
    part, ggain_ref[...] = norm_back(
        rows_ref[0].astype(F32), gain_ref[...].astype(F32), grad
    )
    out_ref[0] = ghidden_ref[...] + part


def first_back(m, rows, ghidden, gain, terms, before):
    micros, count, width = rows.shape
    block = pl.BlockSpec((1, count, width), lambda i: (m, 0, 0))
    specs = [block, resident((count, width)), resident((1, width))]
    specs += [resident(piece.shape) for piece in terms]
    operands = [rows, ghidden, gain, *terms]
    aliases = {}
    if before is not None:
        aliases = {len(operands): 0}
        operands.append(before)
        specs.append(pl.BlockSpec(memory_space=pl.ANY))
    return call(
        functools.partial(first_back_kernel, len(terms)),
        1,
        specs,
        (block, resident((1, width))),
        (
            jax.ShapeDtypeStruct((micros, count, width), F32),
            jax.ShapeDtypeStruct((1, width), F32),
        ),
        aliases=aliases,
    )(*operands)


def layer_end_kernel(terms, hidden_ref, *refs):
    out_ref = refs[-1]
    total = add_up(refs[:terms])
    out_ref[0] = (hidden_ref[...] + total).astype(BF16)


def layer_end(m, micros, hidden, terms, before):
    count, width = hidden.shape
    specs = [resident((count, width))] + [resident(piece.shape) for piece in terms]
    operands = [hidden, *terms]
    aliases = {}
    if before is not None:
        aliases = {len(operands): 0}
        operands.append(before)
        specs.append(pl.BlockSpec(memory_space=pl.ANY))
    return call(
        functools.partial(layer_end_kernel, len(terms)),
        1,
        specs,
        pl.BlockSpec((1, count, width), lambda i: (m, 0, 0)),
        jax.ShapeDtypeStruct((micros, count, width), BF16),
        aliases=aliases,
    )(*operands)


def gather_product_kernel(dot, pieces, *refs):
    right_ref, all_ref, out_ref = refs[pieces:]

    @pl.when(pl.program_id(0) == 0)
    def _():
        assemble(all_ref, refs[:pieces])

    out_ref[...] = dot(all_ref[...], right_ref[...]).astype(out_ref.dtype)


def gather_product(segments, right, transposed, tile=512):
    rows = sum(segment.shape[0] for segment in segments)
    width = segments[0].shape[1]
    cols = right.shape[0] if transposed else right.shape[1]
    tile = min(tile, cols)
    if transposed:
        spec = pl.BlockSpec((tile, width), lambda i: (i, 0))
    else:
        spec = pl.BlockSpec((width, tile), lambda i: (0, i))
    return call(
        functools.partial(
            gather_product_kernel, dot_nt if transposed else dot_nn, len(segments)
        ),
        cols // tile,
        [resident(segment.shape) for segment in segments] + [spec],
        (resident((rows, width)), pl.BlockSpec((rows, tile), lambda i: (0, i))),
        (jax.ShapeDtypeStruct((rows, width), BF16), jax.ShapeDtypeStruct((rows, cols), BF16)),
    )(*segments, right)


def product_scatter_kernel(transposed, lefts, rights, *refs):
    left_refs = refs[:lefts]
    right_refs = refs[lefts : lefts + rights]
    axis = 1 if transposed else 0
    width = min(
        [ref.shape[1] for ref in left_refs] + [ref.shape[axis] for ref in right_refs]
    )
    depth = sum(ref.shape[1] for ref in left_refs)
    total = None
    for start in range(0, depth, width):
        place, offset = divmod(start, left_refs[0].shape[1])
        left = left_refs[place][:, offset : offset + width]
        place, offset = divmod(start, right_refs[0].shape[axis])
        if transposed:
            term = dot_nt(left, right_refs[place][:, offset : offset + width])
        else:
            term = dot_nn(left, right_refs[place][offset : offset + width, :])
        total = term if total is None else total + term
    dissolve(refs[lefts + rights :], total)


def product_scatter(lefts, rights, transposed, counts, tile=512, far=LARGE):
    cols = rights[0].shape[0] if transposed else rights[0].shape[1]
    tile = min(tile, cols)
    if transposed:
        specs = [pl.BlockSpec((tile, right.shape[1]), lambda i: (i, 0)) for right in rights]
    else:
        specs = [pl.BlockSpec((right.shape[0], tile), lambda i: (0, i)) for right in rights]
    return call(
        functools.partial(product_scatter_kernel, transposed, len(lefts), len(rights)),
        cols // tile,
        [resident(left.shape) for left in lefts] + specs,
        tuple(pl.BlockSpec((count, tile), lambda i: (0, i)) for count in counts),
        tuple(jax.ShapeDtypeStruct((count, cols), BF16) for count in counts),
        far=far,
    )(*lefts, *rights)


def weight_total(micros, refs):
    total = dot_tn(refs[0][...], refs[micros][...])
    for m in range(1, micros):
        total = total + dot_tn(refs[m][...], refs[micros + m][...])
    return total


def weight_rows_kernel(micros, core_ref, *refs):
    keep_ref, send_ref = refs[-2:]
    total = weight_total(micros, refs)
    kept = pl.program_id(0) % 2 == core_ref[0]

    @pl.when(kept)
    def _():
        keep_ref[...] = total.astype(BF16)

    @pl.when(jnp.logical_not(kept))
    def _():
        send_ref[...] = total.astype(BF16)


def weight_rows(ranks, core, lefts, rights):
    tokens, rows = lefts[0].shape
    cols = rights[0].shape[1]
    tile = rows // ranks
    micros = len(lefts)
    return call(
        functools.partial(weight_rows_kernel, micros),
        ranks,
        [smem()]
        + [pl.BlockSpec((tokens, tile), lambda i: (0, i))] * micros
        + [resident((tokens, cols))] * micros,
        (pl.BlockSpec((tile, cols), lambda i: (i // 2, 0)),) * 2,
        (jax.ShapeDtypeStruct((rows // 2, cols), BF16),) * 2,
    far=SMALL,
    )(core, *lefts, *rights)


def weight_cols_kernel(micros, ranks, pieces, core_ref, *refs):
    keep_ref, send_ref = refs[2 * micros + pieces - 1 : 2 * micros + pieces + 1]
    sides = list(refs[: 2 * micros - 1])
    if pieces == 1:
        sides.append(refs[2 * micros - 1])
    else:
        last_ref = refs[-1]
        sides.append(last_ref)

        @pl.when(pl.program_id(0) == 0)
        def _():
            assemble(last_ref, refs[2 * micros - 1 : 2 * micros - 1 + pieces])

    total = weight_total(micros, sides).astype(BF16)
    width = total.shape[1] // ranks
    even = core_ref[0] == 0
    for k in range(ranks // 2):
        first = total[:, 2 * k * width : (2 * k + 1) * width]
        second = total[:, (2 * k + 1) * width : (2 * k + 2) * width]
        place = slice(k * width, (k + 1) * width)
        keep_ref[:, place] = jnp.where(even, first, second)
        send_ref[:, place] = jnp.where(even, second, first)


def weight_cols(ranks, core, lefts, rights, tile=256):
    tokens, rows = lefts[0].shape
    *whole, last = rights
    pieces = last if isinstance(last, (list, tuple)) else [last]
    cols = pieces[0].shape[1]
    tile = min(tile, rows)
    micros = len(lefts)
    scratch = [] if len(pieces) == 1 else [pltpu.VMEM((tokens, cols), BF16)]
    return call(
        functools.partial(weight_cols_kernel, micros, ranks, len(pieces)),
        rows // tile,
        [smem()]
        + [pl.BlockSpec((tokens, tile), lambda i: (0, i))] * micros
        + [resident(side.shape) for side in (*whole, *pieces)],
        (pl.BlockSpec((tile, cols // 2), lambda i: (i, 0)),) * 2,
        (jax.ShapeDtypeStruct((rows, cols // 2), BF16),) * 2,
        scratch,
        far=SMALL,
    )(core, *lefts, *whole, *pieces)


def weight_kernel(micros, *refs):
    refs[-1][...] = weight_total(micros, refs).astype(BF16)


def weight_product(lefts, rights, tile=256):
    tokens, rows = lefts[0].shape
    cols = rights[0].shape[1]
    tile = min(tile, rows)
    micros = len(lefts)
    return call(
        functools.partial(weight_kernel, micros),
        rows // tile,
        [pl.BlockSpec((tokens, tile), lambda i: (0, i))] * micros
        + [resident((tokens, cols))] * micros,
        pl.BlockSpec((tile, cols), lambda i: (i, 0)),
        jax.ShapeDtypeStruct((rows, cols), BF16),
        far=SMALL,
    )(*lefts, *rights)


def add_kernel(left_ref, right_ref, out_ref):
    out_ref[...] = (left_ref[...].astype(F32) + right_ref[...].astype(F32)).astype(BF16)


def add_pair(left, right, tile=256):
    rows, cols = left.shape
    tile = min(tile, rows)
    spec = pl.BlockSpec((tile, cols), lambda i: (i, 0))
    return call(
        add_kernel,
        rows // tile,
        [spec, spec],
        spec,
        jax.ShapeDtypeStruct((rows, cols), BF16),
        far=SMALL,
    )(left, right)


def feed_kernel(pieces, parts, steps, *refs):
    weights = refs[2 * pieces : 2 * (pieces + parts)]
    rows_ref, grad_ref, active_ref, gupper_ref = refs[2 * (pieces + parts) :]
    step = pl.program_id(0)

    @pl.when(step == 0)
    def _():
        assemble(rows_ref, refs[:pieces])
        assemble(grad_ref, refs[pieces : 2 * pieces])

    for part in range(parts):

        @pl.when(step // steps == part)
        def _(up_ref=weights[part], down_ref=weights[parts + part]):
            upper = dot_nn(rows_ref[...], up_ref[...])
            square = upper * upper
            slope = 0.7978845608028654
            bent = jnp.tanh(slope * upper * (1.0 + 0.044715 * square))
            half = 0.5 * (1.0 + bent)
            active_ref[...] = (upper * half).astype(BF16)
            inner = slope * (1.0 + 0.134145 * square)
            turn = half + 0.5 * upper * (1.0 - bent * bent) * inner
            gactive = dot_nt(grad_ref[...], down_ref[...])
            gupper_ref[...] = (gactive * turn).astype(BF16)


def feed_forward(segments, cotangents, ups, downs, tile=512):
    rows = sum(segment.shape[0] for segment in segments)
    width = segments[0].shape[1]
    units = ups[0].shape[1]
    tile = min(tile, units)
    steps = units // tile
    parts = len(ups)

    def column(part):
        return lambda i: (0, jnp.clip(i - part * steps, 0, steps - 1))

    def row(part):
        return lambda i: (jnp.clip(i - part * steps, 0, steps - 1), 0)

    narrow = jax.ShapeDtypeStruct((rows, parts * units), BF16)
    wide = jax.ShapeDtypeStruct((rows, width), BF16)
    return call(
        functools.partial(feed_kernel, len(segments), parts, steps),
        parts * steps,
        [resident(segment.shape) for segment in (*segments, *cotangents)]
        + [pl.BlockSpec((width, tile), column(part)) for part in range(parts)]
        + [pl.BlockSpec((tile, width), row(part)) for part in range(parts)],
        (resident((rows, width)),) * 2 + (pl.BlockSpec((rows, tile), lambda i: (0, i)),) * 2,
        (wide, wide, narrow, narrow),
        limit=44,
    )(*segments, *cotangents, *ups, *downs)


def unpack_kernel(kd, vd, grad_ref, *refs):
    start = 0
    for out_ref, width in zip(refs[-4:], (kd, kd, vd, vd)):
        out_ref[...] = grad_ref[:, start : start + width].astype(F32)
        start += width


def unpack(head, heads, kd, vd, grad, before):
    rows = grad.shape[0]
    widths = (kd, kd, vd, vd)
    operands = [grad]
    specs = [resident(grad.shape)]
    aliases = {}
    if before is not None:
        operands += before
        specs += [pl.BlockSpec(memory_space=pl.ANY)] * 4
        aliases = {1 + n: n for n in range(4)}
    return call(
        functools.partial(unpack_kernel, kd, vd),
        1,
        specs,
        tuple(pl.BlockSpec((rows, width), lambda i: (0, head)) for width in widths),
        tuple(jax.ShapeDtypeStruct((rows, heads * width), F32) for width in widths),
        aliases=aliases,
    )(*operands)


def decay_table(log_gamma, size, scale):
    row = lax.broadcasted_iota(jnp.int32, (size, size), 0)
    col = lax.broadcasted_iota(jnp.int32, (size, size), 1)
    table = jnp.exp((row - col).astype(F32) * log_gamma) * scale
    return table, jnp.where(row >= col, table, 0.0)


def pair_scale(docs, i, j, log_gamma, size):
    same = jnp.logical_and(docs[i] == docs[j], docs[i] >= 0)
    far = jnp.exp(jnp.full((1, 1), (i - j) * size, F32) * log_gamma)
    return jnp.where(same, far, 0.0)


def retention_forward_kernel(
    blocks, kd, vd, me_ref, docs_ref, rates_ref, proj_ref, mixed_ref, full_ref, diag_ref
):
    head = pl.program_id(0)
    size = proj_ref.shape[0] // blocks
    log_gamma = rates_ref[head]
    full_ref[...], diag_ref[...] = decay_table(log_gamma, size, kd**-0.5)
    me = me_ref[0]
    docs = [docs_ref[i] for i in range(blocks)]
    slots = [pl.ds(pl.multiple_of((i ^ me) * size, size), size) for i in range(blocks)]
    keys = slice(kd, 2 * kd)
    values = slice(2 * kd, 2 * kd + vd)
    for i in range(blocks):
        query = proj_ref[slots[i], :kd]
        total = None
        for j in range(i + 1):
            table = diag_ref if j == i else full_ref
            raw = dot_nt(query, proj_ref[slots[j], keys])
            scores = (raw * (table[...] * pair_scale(docs, i, j, log_gamma, size))).astype(BF16)
            term = dot_nn(scores, proj_ref[slots[j], values])
            total = term if total is None else total + term
        center = total - jnp.mean(total, axis=-1, keepdims=True)
        variance = jnp.mean(center * center, axis=-1, keepdims=True)
        normal = center * lax.rsqrt(jnp.maximum(variance, GROUP_FLOOR))
        gate = proj_ref[slots[i], 2 * kd + vd :].astype(F32)
        mixed_ref[slots[i], :] = (gate * jax.nn.sigmoid(gate) * normal).astype(BF16)


def retention_backward_kernel(
    head,
    blocks,
    kd,
    vd,
    me_ref,
    docs_ref,
    rates_ref,
    proj_ref,
    grad_ref,
    gproj_ref,
    full_ref,
    diag_ref,
    gkey_ref,
    gvalue_ref,
):
    size = proj_ref.shape[0] // blocks
    log_gamma = rates_ref[head]
    full_ref[...], diag_ref[...] = decay_table(log_gamma, size, kd**-0.5)
    me = me_ref[0]
    docs = [docs_ref[i] for i in range(blocks)]
    slots = [pl.ds(pl.multiple_of((i ^ me) * size, size), size) for i in range(blocks)]
    keys = slice(kd, 2 * kd)
    values = slice(2 * kd, 2 * kd + vd)
    gates = slice(2 * kd + vd, 2 * kd + 2 * vd)
    for i in range(blocks):
        query = proj_ref[slots[i], :kd]
        total = None
        masks = []
        kept = []
        for j in range(i + 1):
            table = diag_ref if j == i else full_ref
            mask = table[...] * pair_scale(docs, i, j, log_gamma, size)
            raw = dot_nt(query, proj_ref[slots[j], keys])
            scores = (raw * mask).astype(BF16)
            term = dot_nn(scores, proj_ref[slots[j], values])
            total = term if total is None else total + term
            kept.append(scores)
            masks.append(mask)
        center = total - jnp.mean(total, axis=-1, keepdims=True)
        variance = jnp.mean(center * center, axis=-1, keepdims=True)
        inverse = lax.rsqrt(jnp.maximum(variance, GROUP_FLOOR))
        normal = center * inverse
        gate = proj_ref[slots[i], gates].astype(F32)
        grad = grad_ref[slots[i], :].astype(F32)
        sig = jax.nn.sigmoid(gate)
        ggate = grad * normal * (sig * (1.0 + gate * (1.0 - sig)))
        gproj_ref[slots[i], gates] = ggate.astype(BF16)
        gnormal = grad * gate * sig
        along = jnp.mean(gnormal * normal, axis=-1, keepdims=True)
        along = jnp.where(variance > GROUP_FLOOR, along, 0.0)
        gcenter = inverse * (gnormal - normal * along)
        gret = (gcenter - jnp.mean(gcenter, axis=-1, keepdims=True)).astype(BF16)
        gquery = None
        for j in range(i + 1):
            graw = dot_nt(gret, proj_ref[slots[j], values])
            graw = (graw * masks[j]).astype(BF16)
            term = dot_nn(graw, proj_ref[slots[j], keys])
            gquery = term if gquery is None else gquery + term
            place = pl.ds(j * size, size)
            gkey = dot_tn(graw, query)
            gvalue = dot_tn(kept[j], gret)
            if j == i:
                gkey_ref[place, :] = gkey
                gvalue_ref[place, :] = gvalue
            else:
                gkey_ref[place, :] += gkey
                gvalue_ref[place, :] += gvalue
        gproj_ref[slots[i], :kd] = gquery.astype(BF16)
    for i in range(blocks):
        place = pl.ds(i * size, size)
        gproj_ref[slots[i], keys] = gkey_ref[place, :].astype(BF16)
        gproj_ref[slots[i], values] = gvalue_ref[place, :].astype(BF16)


def retention_forward(blocks, heads, kd, vd, me, docs, rates, proj):
    length = proj.shape[0]
    size = length // blocks
    return call(
        functools.partial(retention_forward_kernel, blocks, kd, vd),
        heads,
        [smem(), smem(), smem(), pl.BlockSpec((length, 2 * (kd + vd)), lambda h: (0, h))],
        pl.BlockSpec((length, vd), lambda h: (0, h)),
        jax.ShapeDtypeStruct((length, heads * vd), BF16),
        [pltpu.VMEM((size, size), F32)] * 2,
    )(me, docs, rates, proj)


def retention_backward(head, blocks, kd, vd, me, docs, rates, proj, grad):
    length = proj.shape[0]
    size = length // blocks
    width = 2 * (kd + vd)
    one = pl.Buffered(1)
    return call(
        functools.partial(retention_backward_kernel, head, blocks, kd, vd),
        1,
        [
            smem(),
            smem(),
            smem(),
            pl.BlockSpec((length, width), lambda i: (0, head), pipeline_mode=one),
            pl.BlockSpec((length, vd), lambda i: (0, head), pipeline_mode=one),
        ],
        resident((length, width)),
        jax.ShapeDtypeStruct((length, width), BF16),
        [pltpu.VMEM((size, size), F32)] * 2
        + [pltpu.VMEM((length, kd), F32), pltpu.VMEM((length, vd), F32)],
    )(me, docs, rates, proj, grad)


def body(
    layer_in,
    norm1_gain,
    w_query,
    w_key,
    w_value,
    w_gate,
    w_out,
    norm2_gain,
    w_up,
    w_down,
    decay_rates,
    seq_counts,
    out_grad,
):
    heads = decay_rates.shape[0]
    kd = w_query.shape[1] // heads
    vd = w_value.shape[1] // heads
    micros, rows_dev, width = layer_in.shape
    blocks = lax.axis_size("mp")
    length = rows_dev * blocks
    tall = [rows_dev] * blocks
    wide = [rows_dev] * 3 + [rows_dev // 2] * 2 if blocks == 4 else tall
    pieces = []
    for h in range(heads):
        pieces += [
            w_query[:, h * kd : (h + 1) * kd],
            w_key[:, h * kd : (h + 1) * kd],
            w_value[:, h * vd : (h + 1) * vd],
            w_gate[:, h * vd : (h + 1) * vd],
        ]
    w_in = jnp.concatenate(pieces, 1)
    gain_one = norm1_gain.reshape(1, -1)
    gain_two = norm2_gain.reshape(1, -1)
    rates = jnp.log1p(-decay_rates)
    me = lax.axis_index("mp").reshape(1).astype(jnp.int32)
    starts = jnp.arange(blocks, dtype=jnp.int32) * rows_dev
    a, b = range(micros)
    docs = [document_ids(seq_counts[0, m], starts, length) for m in (a, b)]
    def backward(h, m, proj, grad):
        return retention_backward(h, blocks, kd, vd, me, docs[m], rates, proj, grad)

    up_rows, down_rows = (
        weight.shape[0] // lax.axis_size("dp") for weight in (w_up, w_down)
    )

    def eighth_rows():
        place = lax.axis_index("dp")
        up = lax.dynamic_slice_in_dim(w_up, place * up_rows, up_rows, 0)
        down = lax.dynamic_slice_in_dim(w_down, place * down_rows, down_rows, 0)
        cut = w_up.shape[1]
        return jnp.concatenate(
            [up] + [down[:, k : k + cut] for k in range(0, width, cut)], 0
        )

    def exchange(rows):
        return move(rows, "mp", 2) if blocks == 4 else rows

    def neighbour_weights(rows):
        if blocks != 4:
            return []
        down = [
            rows[k : k + down_rows] for k in range(up_rows, rows.shape[0], down_rows)
        ]
        return [
            lax.all_gather(part, "dp", axis=0, tiled=True)
            for part in (rows[:up_rows], jnp.concatenate(down, 1))
        ]

    def pair_send(total, dim):
        if blocks != 4:
            return [total]
        half = total.shape[1 - dim] // 2
        own = lax.slice_in_dim(total, 0, half, axis=1 - dim)
        other = lax.slice_in_dim(total, half, 2 * half, axis=1 - dim)
        return [own, move(other, "mp", 2)]

    def pair_sum(halves):
        return sum(half.astype(F32) for half in halves)

    ranks = lax.axis_size("dp")
    core = (lax.axis_index("dp") % 2).reshape(1).astype(jnp.int32)

    def cores(kept_sent):
        kept, sent = kept_sent
        return kept, move(sent, "dp", 1)

    def weight_sum(total, dim, whole=False):
        groups = [list(range(parity, ranks, 2)) for parity in (0, 1)]
        return lax.psum_scatter(
            total,
            "dp",
            scatter_dimension=dim,
            tiled=True,
            axis_index_groups=None if whole else groups,
        )

    normed_a = first_norm(a, layer_in, gain_one)
    normed_b = first_norm(b, after(layer_in, normed_a, w_in), gain_one)
    go_one_a = Gather(normed_a)
    eighths = eighth_rows()
    fenced = fence(go_one_a, normed_b, eighths, docs, rates, me)
    go_one_a, normed_b, eighths, docs, rates, me = fenced
    forward = (blocks, heads, kd, vd, me)
    go_one_a.middle()
    go_one_a, normed_b = fence(go_one_a, normed_b)

    go_one_b = Gather(normed_b)
    eighths = exchange(after(eighths, normed_b))
    cot_a = PairGather(after(out_grad[a], normed_b))
    gathered_a, proj_a = gather_product(go_one_a.result(), w_in, False)
    mixed_a = retention_forward(*forward, docs[a], rates, proj_a)
    go_one_b, eighths, cot_a, mixed_a = fence(go_one_b, eighths, cot_a, mixed_a)
    go_one_b.middle()
    more = neighbour_weights(eighths)
    parts = product_scatter([mixed_a], [w_out], False, tall)
    go_one_b, parts = fence(go_one_b, parts)

    sum_one_a = TallScatterSum(parts)
    cot_b = PairGather(after(out_grad[b], parts))
    gathered_b, proj_b = gather_product(go_one_b.result(), w_in, False)
    sum_one_a, cot_b, proj_b = fence(sum_one_a, cot_b, proj_b)
    sum_one_a.middle()
    mixed_b = retention_forward(*forward, docs[b], rates, proj_b)
    parts = product_scatter([mixed_b], [w_out], False, tall)
    sum_one_a, parts = fence(sum_one_a, parts)

    pair = [rows_dev] * 2 if blocks == 4 else tall
    hidden_a, normed = second_norm(a, layer_in, gain_two, sum_one_a.result())
    go_two_a = PairGather(normed)
    sum_one_b = TallScatterSum(parts)
    go_two_a, sum_one_b, hidden_a = fence(go_two_a, sum_one_b, hidden_a)
    sum_one_b.middle()
    sum_one_b, more = fence(sum_one_b, more)

    ups, downs = [w_up, *more[:1]], [w_down, *more[1:]]
    hidden_b, normed = second_norm(b, layer_in, gain_two, sum_one_b.result())
    go_two_b = PairGather(normed)
    rows_two_a, cotangent_a, active_a, gupper_a = feed_forward(
        go_two_a.result(hidden_b), cot_a.result(), ups, downs
    )
    parts = product_scatter([gupper_a], ups, True, pair)
    go_two_b, parts = fence(go_two_b, parts)

    sum_three_a = PairScatter(parts)
    rows_two_b, cotangent_b, active_b, gupper_b = feed_forward(
        go_two_b.result(), cot_b.result(), ups, downs
    )
    dw_down = weight_product((active_a, active_b), (cotangent_a, cotangent_b))
    fenced = fence(sum_three_a, dw_down, gupper_b, (active_a, active_b))
    sum_three_a, dw_down, gupper_b, actives = fenced

    down_total = weight_sum(dw_down, 1, True)
    parts = product_scatter([gupper_b], ups, True, pair)
    ghidden_a, normed_a, gain_two_a = second_back(
        a, out_grad, hidden_a, gain_two, sum_three_a.result(parts)
    )
    parts, normed_a = fence(parts, normed_a)
    sum_three_b = PairScatter(parts)
    dw_up = weight_rows(
        ranks, core, after((rows_two_a, rows_two_b), normed_a), (gupper_a, gupper_b)
    )
    feeds = [product_scatter([after(actives[0], dw_up)], downs, False, pair, far=SMALL)]
    sum_three_b, normed_a, dw_up, feeds = fence(sum_three_b, normed_a, dw_up, feeds)
    go_three_a = Gather(normed_a)
    dw_up = cores(dw_up)
    ghidden_b, normed_b, gain_two_b = second_back(
        b, out_grad, hidden_b, gain_two, sum_three_b.result()
    )
    feeds.append(
        product_scatter([after(actives[1], normed_b)], downs, False, pair, far=SMALL)
    )
    go_three_a, normed_b, dw_up, feeds = fence(go_three_a, normed_b, dw_up, feeds)
    go_three_a.middle()
    dw_up = add_pair(*dw_up)
    go_three_a, normed_b, dw_up, feeds = fence(go_three_a, normed_b, dw_up, feeds)

    up_total = weight_sum(dw_up, 0)
    go_three_b = Gather(normed_b)
    branch_a, gmixed_a = gather_product(go_three_a.result(), w_out, True)
    gproj_a = [backward(0, a, proj_a, gmixed_a)]
    go_three_b, gproj_a, gmixed_a = fence(go_three_b, gproj_a, gmixed_a)
    go_three_b.middle()
    for h in range(1, heads):
        gproj_a.append(backward(h, a, proj_a, gmixed_a))
    go_three_b, gproj_a, down_total = fence(go_three_b, gproj_a, down_total)

    dw_out = weight_cols(ranks, core, (mixed_a, mixed_b), (branch_a, go_three_b.result()))
    dw_out, go_three_b = fence(dw_out, go_three_b)
    dw_out = cores(dw_out)
    branch_b, gmixed_b = gather_product(go_three_b.result(), w_out, True)
    dw_out, gmixed_b = fence(dw_out, gmixed_b)
    dw_out = add_pair(*dw_out)
    dw_out, gmixed_b, feeds, up_total = fence(dw_out, gmixed_b, feeds, up_total)
    grad_w_out = weight_sum(dw_out, 1)
    sum_two_a = PairScatter(feeds[0])
    gproj_b = [backward(0, b, proj_b, gmixed_b)]
    dw_in = weight_product((gathered_a, gathered_b), (gproj_a[0], gproj_b[0]))
    fenced = fence(sum_two_a, dw_in, gproj_b, gproj_a, gmixed_b, feeds)
    sum_two_a, dw_in, gproj_b, gproj_a, gmixed_b, feeds = fenced
    grad_w_in = [weight_sum(dw_in, 0, True)]
    grad_w_down = pair_send(down_total, 1)
    sum_two_b = PairScatter(feeds[1])
    parts = product_scatter(gproj_a, [w_in], True, wide, far=SMALL)
    fenced = fence(sum_two_b, parts, gproj_b, grad_w_out, grad_w_down, up_total)
    sum_two_b, parts, gproj_b, grad_w_out, grad_w_down, up_total = fenced
    grad_w_up = pair_send(up_total, 0)
    sum_four_a = ScatterSum(parts)
    for h in range(1, heads):
        gproj_b.append(backward(h, b, proj_b, after(gmixed_b, gproj_b)))
        dw_in = weight_product((gathered_a, gathered_b), (gproj_a[h], gproj_b[h]))
    sum_four_a, dw_in, gproj_b, grad_w_up = fence(sum_four_a, dw_in, gproj_b, grad_w_up)
    sum_four_a.middle()
    parts = product_scatter(gproj_b, [w_in], True, wide)
    fenced = fence(sum_four_a, dw_in, parts, grad_w_in)
    sum_four_a, dw_in, parts, grad_w_in = fenced
    in_grads = unpack(0, heads, kd, vd, grad_w_in[0], None)

    if heads > 1:
        grad_w_in.append(weight_sum(dw_in, 0, True))
    sum_four_b = ScatterSum(parts)
    grad_input, gain_one_a = first_back(
        a, layer_in, ghidden_a, gain_one, sum_four_a.result(), None
    )
    layer_out = layer_end(a, micros, hidden_a, sum_two_a.result(grad_input), None)
    layer_out = layer_end(b, micros, hidden_b, sum_two_b.result(), layer_out)
    fenced = fence(sum_four_b, layer_out, grad_input, in_grads)
    sum_four_b, layer_out, grad_input, in_grads = fenced
    sum_four_b.middle()
    fenced = fence(
        sum_four_b, grad_w_out.astype(F32), pair_sum(grad_w_down), pair_sum(grad_w_up)
    )
    sum_four_b, grad_w_out, grad_w_down, grad_w_up = fenced
    grad_input, gain_one_b = first_back(
        b, layer_in, ghidden_b, gain_one, sum_four_b.result(), grad_input
    )

    for h in range(1, heads):
        in_grads = unpack(h, heads, kd, vd, grad_w_in[h], in_grads)
    gains = small_sum(
        jnp.concatenate([gain_one_a + gain_one_b, gain_two_a + gain_two_b], 0)
    )
    return (
        layer_out,
        grad_input,
        gains[0],
        *in_grads,
        grad_w_out,
        gains[1],
        grad_w_up,
        grad_w_down,
    )


def solution(mesh):
    in_specs = (
        P(None, ("dp", "mp"), None),
        P(),
        P(None, "mp"),
        P(None, "mp"),
        P(None, "mp"),
        P(None, "mp"),
        P("mp", None),
        P(),
        P(None, "mp"),
        P("mp", None),
        P("mp"),
        P("dp", None, None),
        P(None, ("dp", "mp"), None),
    )
    out_specs = (
        P(None, ("dp", "mp"), None),
        P(None, ("dp", "mp"), None),
        P("dp"),
        P("dp", "mp"),
        P("dp", "mp"),
        P("dp", "mp"),
        P("dp", "mp"),
        P("mp", "dp"),
        P("dp"),
        P("dp", "mp"),
        P("mp", "dp"),
    )
    return jax.shard_map(body, mesh=mesh, in_specs=in_specs, out_specs=out_specs, check_vma=False)
```

```python
import functools

import jax
import jax.numpy as jnp
from jax import lax
from jax.experimental import pallas as pl
from jax.experimental.pallas import tpu as pltpu
from jax.sharding import PartitionSpec as P

NORM_EPS = 1e-05
GROUP_FLOOR = 1.0
BF16 = jnp.bfloat16
F32 = jnp.float32
TINY = pl.CostEstimate(flops=1, bytes_accessed=1, transcendentals=0)


def document_ids(counts, position, length):
    half_len = length // 2
    quarter_len = length // 4
    long_end = counts[2] * length
    half_end = long_end + counts[1] * half_len
    quarter_end = half_end + counts[0] * quarter_len
    long_ids = position // length
    half_ids = counts[2] + (position - long_end) // half_len
    quarter_ids = counts[2] + counts[1] + (position - half_end) // quarter_len
    inner = jnp.where(position < quarter_end, quarter_ids, -1)
    inner = jnp.where(position < half_end, half_ids, inner)
    return jnp.where(position < long_end, long_ids, inner)


def dot_nt(left, right):
    return lax.dot_general(left, right, (((1,), (1,)), ((), ())), preferred_element_type=F32)


def dot_tn(left, right):
    return lax.dot_general(left, right, (((0,), (0,)), ((), ())), preferred_element_type=F32)


def dot_nn(left, right):
    return jnp.dot(left, right, preferred_element_type=F32)


def move(value, axis, step):
    size = lax.axis_size(axis)
    return lax.ppermute(value, axis, [(i, i ^ step) for i in range(size)])


def after(value, *earlier):
    return lax.optimization_barrier((value, earlier))[0]


def fence(*values):
    return lax.optimization_barrier(values)


class Transfer:
    def __init_subclass__(cls):
        jax.tree_util.register_pytree_node(
            cls, lambda self: (self.parts(), None), lambda _, parts: cls.rebuild(parts)
        )

    def parts(self):
        return (self.kept, self.pieces)

    @classmethod
    def rebuild(cls, parts):
        self = object.__new__(cls)
        self.kept, self.pieces = parts
        return self

    def result(self, *earlier):
        return after([*self.kept, *self.pieces], earlier)


class Gather(Transfer):
    def __init__(self, rows):
        steps = (1, 2) if lax.axis_size("mp") == 4 else range(1, lax.axis_size("mp"))
        self.kept = [rows]
        self.pieces = [move(rows, "mp", k) for k in steps]

    def middle(self):
        if lax.axis_size("mp") == 4:
            first, second = self.pieces
            half = first.shape[0] // 2
            self.kept = [*self.kept, first, second]
            self.pieces = [move(first[:half], "mp", 2), move(second[half:], "mp", 1)]


class ScatterSum(Transfer):
    def __init__(self, segments):
        if lax.axis_size("mp") == 4:
            self.kept = [*segments[:3]]
            upper, lower = segments[3:]
            self.pieces = [move(upper, "mp", 1), move(lower, "mp", 2)]
        else:
            self.kept = [segments[0]]
            self.pieces = [move(part, "mp", k + 1) for k, part in enumerate(segments[1:])]

    def middle(self):
        if lax.axis_size("mp") == 4:
            own, first, second = self.kept
            upper, lower = self.pieces
            half = upper.shape[0]
            first = jnp.concatenate([first[:half], first[half:] + lower], 0)
            second = jnp.concatenate([second[:half] + upper, second[half:]], 0)
            self.kept = [own]
            self.pieces = [move(first, "mp", 1), move(second, "mp", 2)]


class TallScatterSum(ScatterSum):
    def __init__(self, segments):
        if lax.axis_size("mp") == 4:
            self.kept = [*segments[:3]]
            self.pieces = [move(segments[3], "mp", 2)]
        else:
            super().__init__(segments)

    def middle(self):
        if lax.axis_size("mp") == 4:
            own, first, second = self.kept
            self.kept = [own]
            self.pieces = [move(first + self.pieces[0], "mp", 1), move(second, "mp", 2)]


class PairGather(Transfer):
    def __init__(self, rows):
        steps = (1,) if lax.axis_size("mp") == 4 else range(1, lax.axis_size("mp"))
        self.kept = [rows]
        self.pieces = [move(rows, "mp", k) for k in steps]


class PairScatter(Transfer):
    def __init__(self, segments):
        self.kept = [segments[0]]
        self.pieces = [move(part, "mp", k + 1) for k, part in enumerate(segments[1:])]


def small_sum(value):
    value = value + sum(move(value, "mp", k) for k in range(1, lax.axis_size("mp")))
    half = lax.axis_size("dp") // 2
    place = lax.axis_index("dp")
    split = value.reshape(value.shape[0], half, 2, -1)
    even = place % 2 == 0
    kept = jnp.where(even, split[:, :, 0], split[:, :, 1])
    sent = jnp.where(even, split[:, :, 1], split[:, :, 0])
    kept = kept + move(sent, "dp", 1)
    pick = lambda chip: lax.dynamic_index_in_dim(kept, chip, 1, False)
    chip = place // 2
    return pick(chip) + sum(move(pick(chip ^ k), "dp", 2 * k) for k in range(1, half))


LARGE, SMALL = 5 << 19, 1 << 18


def nbytes(array):
    return array.size * array.dtype.itemsize


def resident(shape):
    zeros = (0,) * len(shape)
    return pl.BlockSpec(tuple(shape), lambda i: zeros, pipeline_mode=pl.Buffered(1))


def smem():
    return pl.BlockSpec(memory_space=pltpu.SMEM)


def call(kernel, steps, in_specs, out_specs, out_shape, scratch=(), limit=32, aliases=None, far=LARGE):
    name = getattr(kernel, "func", kernel).__name__.removesuffix("_kernel")
    several = isinstance(out_shape, tuple)
    outs = [
        pltpu.HBM(out.shape, out.dtype) if nbytes(out) > far else out
        for out in (out_shape if several else (out_shape,))
    ]
    run = pl.pallas_call(
        kernel,
        name=name,
        grid=(steps,),
        in_specs=in_specs,
        out_specs=out_specs,
        out_shape=tuple(outs) if several else outs[0],
        scratch_shapes=list(scratch),
        input_output_aliases=aliases or {},
        compiler_params=pltpu.CompilerParams(vmem_limit_bytes=limit << 20),
        cost_estimate=TINY,
    )

    def placed(*operands):
        return run(
            *[
                pltpu.with_memory_space_constraint(operand, pltpu.HBM)
                if nbytes(operand) > far
                else operand
                for operand in operands
            ]
        )

    return placed


def assemble(out_ref, refs):
    offset = 0
    for ref in refs:
        rows = ref.shape[0]
        out_ref[offset : offset + rows, :] = ref[...]
        offset += rows


def dissolve(refs, value):
    offset = 0
    for ref in refs:
        rows = ref.shape[0]
        ref[...] = value[offset : offset + rows].astype(ref.dtype)
        offset += rows


def add_up(refs):
    total = refs[0][...].astype(F32)
    for ref in refs[1:]:
        total = total + ref[...].astype(F32)
    return total


def normalize(rows):
    center = rows - jnp.mean(rows, axis=-1, keepdims=True)
    variance = jnp.mean(center * center, axis=-1, keepdims=True)
    inverse = lax.rsqrt(variance + NORM_EPS)
    return center * inverse, inverse


def first_norm_kernel(rows_ref, gain_ref, out_ref):
    normal, _ = normalize(rows_ref[0].astype(F32))
    out_ref[...] = (normal * gain_ref[...].astype(F32)).astype(BF16)


def first_norm(m, rows, gain):
    _, count, width = rows.shape
    narrow = jax.ShapeDtypeStruct((count, width), BF16)
    return call(
        first_norm_kernel,
        1,
        [pl.BlockSpec((1, count, width), lambda i: (m, 0, 0)), resident((1, width))],
        resident((count, width)),
        narrow,
    )(rows, gain)


def second_norm_kernel(rows_ref, gain_ref, *refs):
    hidden_ref, out_ref = refs[-2:]
    hidden = rows_ref[0].astype(F32) + add_up(refs[:-2])
    hidden_ref[...] = hidden
    normal, _ = normalize(hidden)
    out_ref[...] = (normal * gain_ref[...].astype(F32)).astype(BF16)


def second_norm(m, rows, gain, terms):
    _, count, width = rows.shape
    narrow = jax.ShapeDtypeStruct((count, width), BF16)
    return call(
        second_norm_kernel,
        1,
        [pl.BlockSpec((1, count, width), lambda i: (m, 0, 0)), resident((1, width))]
        + [resident(piece.shape) for piece in terms],
        (resident((count, width)),) * 2,
        (jax.ShapeDtypeStruct((count, width), F32), narrow),
    )(rows, gain, *terms)


def norm_back(rows, gain, grad):
    normal, inverse = normalize(rows)
    scaled = grad * gain
    along = jnp.mean(scaled * normal, axis=-1, keepdims=True)
    inner = scaled - jnp.mean(scaled, axis=-1, keepdims=True) - normal * along
    return inverse * inner, jnp.sum(grad * normal, axis=0, keepdims=True)


def second_back_kernel(cot_ref, hidden_ref, gain_ref, *refs):
    total_ref, out_ref, ggain_ref = refs[-3:]
    grad = add_up(refs[:-3])
    part, ggain_ref[...] = norm_back(hidden_ref[...], gain_ref[...].astype(F32), grad)
    total = cot_ref[0].astype(F32) + part
    total_ref[...] = total
    out_ref[...] = total.astype(BF16)


def second_back(m, cotangent, hidden, gain, terms):
    count, width = hidden.shape
    narrow = jax.ShapeDtypeStruct((count, width), BF16)
    return call(
        second_back_kernel,
        1,
        [
            pl.BlockSpec((1, count, width), lambda i: (m, 0, 0)),
            resident((count, width)),
            resident((1, width)),
        ]
        + [resident(piece.shape) for piece in terms],
        (resident((count, width)), resident((count, width)), resident((1, width))),
        (
            jax.ShapeDtypeStruct((count, width), F32),
            narrow,
            jax.ShapeDtypeStruct((1, width), F32),
        ),
    )(cotangent, hidden, gain, *terms)


def first_back_kernel(terms, rows_ref, ghidden_ref, gain_ref, *refs):
    out_ref, ggain_ref = refs[-2:]
    grad = add_up(refs[:terms])
    part, ggain_ref[...] = norm_back(
        rows_ref[0].astype(F32), gain_ref[...].astype(F32), grad
    )
    out_ref[0] = ghidden_ref[...] + part


def first_back(m, rows, ghidden, gain, terms, before):
    micros, count, width = rows.shape
    block = pl.BlockSpec((1, count, width), lambda i: (m, 0, 0))
    specs = [block, resident((count, width)), resident((1, width))]
    specs += [resident(piece.shape) for piece in terms]
    operands = [rows, ghidden, gain, *terms]
    aliases = {}
    if before is not None:
        aliases = {len(operands): 0}
        operands.append(before)
        specs.append(pl.BlockSpec(memory_space=pl.ANY))
    return call(
        functools.partial(first_back_kernel, len(terms)),
        1,
        specs,
        (block, resident((1, width))),
        (
            jax.ShapeDtypeStruct((micros, count, width), F32),
            jax.ShapeDtypeStruct((1, width), F32),
        ),
        aliases=aliases,
    )(*operands)


def layer_end_kernel(terms, hidden_ref, *refs):
    out_ref = refs[-1]
    total = add_up(refs[:terms])
    out_ref[0] = (hidden_ref[...] + total).astype(BF16)


def layer_end(m, micros, hidden, terms, before):
    count, width = hidden.shape
    specs = [resident((count, width))] + [resident(piece.shape) for piece in terms]
    operands = [hidden, *terms]
    aliases = {}
    if before is not None:
        aliases = {len(operands): 0}
        operands.append(before)
        specs.append(pl.BlockSpec(memory_space=pl.ANY))
    return call(
        functools.partial(layer_end_kernel, len(terms)),
        1,
        specs,
        pl.BlockSpec((1, count, width), lambda i: (m, 0, 0)),
        jax.ShapeDtypeStruct((micros, count, width), BF16),
        aliases=aliases,
    )(*operands)


def gather_product_kernel(dot, pieces, *refs):
    right_ref, all_ref, out_ref = refs[pieces:]

    @pl.when(pl.program_id(0) == 0)
    def _():
        assemble(all_ref, refs[:pieces])

    out_ref[...] = dot(all_ref[...], right_ref[...]).astype(out_ref.dtype)


def gather_product(segments, right, transposed, tile=512):
    rows = sum(segment.shape[0] for segment in segments)
    width = segments[0].shape[1]
    cols = right.shape[0] if transposed else right.shape[1]
    tile = min(tile, cols)
    if transposed:
        spec = pl.BlockSpec((tile, width), lambda i: (i, 0))
    else:
        spec = pl.BlockSpec((width, tile), lambda i: (0, i))
    return call(
        functools.partial(
            gather_product_kernel, dot_nt if transposed else dot_nn, len(segments)
        ),
        cols // tile,
        [resident(segment.shape) for segment in segments] + [spec],
        (resident((rows, width)), pl.BlockSpec((rows, tile), lambda i: (0, i))),
        (jax.ShapeDtypeStruct((rows, width), BF16), jax.ShapeDtypeStruct((rows, cols), BF16)),
    )(*segments, right)


def product_scatter_kernel(transposed, lefts, rights, *refs):
    left_refs = refs[:lefts]
    right_refs = refs[lefts : lefts + rights]
    axis = 1 if transposed else 0
    width = min(
        [ref.shape[1] for ref in left_refs] + [ref.shape[axis] for ref in right_refs]
    )
    depth = sum(ref.shape[1] for ref in left_refs)
    total = None
    for start in range(0, depth, width):
        place, offset = divmod(start, left_refs[0].shape[1])
        left = left_refs[place][:, offset : offset + width]
        place, offset = divmod(start, right_refs[0].shape[axis])
        if transposed:
            term = dot_nt(left, right_refs[place][:, offset : offset + width])
        else:
            term = dot_nn(left, right_refs[place][offset : offset + width, :])
        total = term if total is None else total + term
    dissolve(refs[lefts + rights :], total)


def product_scatter(lefts, rights, transposed, counts, tile=512, far=LARGE):
    cols = rights[0].shape[0] if transposed else rights[0].shape[1]
    tile = min(tile, cols)
    if transposed:
        specs = [pl.BlockSpec((tile, right.shape[1]), lambda i: (i, 0)) for right in rights]
    else:
        specs = [pl.BlockSpec((right.shape[0], tile), lambda i: (0, i)) for right in rights]
    return call(
        functools.partial(product_scatter_kernel, transposed, len(lefts), len(rights)),
        cols // tile,
        [resident(left.shape) for left in lefts] + specs,
        tuple(pl.BlockSpec((count, tile), lambda i: (0, i)) for count in counts),
        tuple(jax.ShapeDtypeStruct((count, cols), BF16) for count in counts),
        far=far,
    )(*lefts, *rights)


def weight_total(micros, refs):
    total = dot_tn(refs[0][...], refs[micros][...])
    for m in range(1, micros):
        total = total + dot_tn(refs[m][...], refs[micros + m][...])
    return total


def weight_rows_kernel(micros, core_ref, *refs):
    keep_ref, send_ref = refs[-2:]
    total = weight_total(micros, refs)
    kept = pl.program_id(0) % 2 == core_ref[0]

    @pl.when(kept)
    def _():
        keep_ref[...] = total.astype(BF16)

    @pl.when(jnp.logical_not(kept))
    def _():
        send_ref[...] = total.astype(BF16)


def weight_rows(ranks, core, lefts, rights):
    tokens, rows = lefts[0].shape
    cols = rights[0].shape[1]
    tile = rows // ranks
    micros = len(lefts)
    return call(
        functools.partial(weight_rows_kernel, micros),
        ranks,
        [smem()]
        + [pl.BlockSpec((tokens, tile), lambda i: (0, i))] * micros
        + [resident((tokens, cols))] * micros,
        (pl.BlockSpec((tile, cols), lambda i: (i // 2, 0)),) * 2,
        (jax.ShapeDtypeStruct((rows // 2, cols), BF16),) * 2,
    far=SMALL,
    )(core, *lefts, *rights)


def weight_cols_kernel(micros, ranks, pieces, core_ref, *refs):
    keep_ref, send_ref = refs[2 * micros + pieces - 1 : 2 * micros + pieces + 1]
    sides = list(refs[: 2 * micros - 1])
    if pieces == 1:
        sides.append(refs[2 * micros - 1])
    else:
        last_ref = refs[-1]
        sides.append(last_ref)

        @pl.when(pl.program_id(0) == 0)
        def _():
            assemble(last_ref, refs[2 * micros - 1 : 2 * micros - 1 + pieces])

    total = weight_total(micros, sides).astype(BF16)
    width = total.shape[1] // ranks
    even = core_ref[0] == 0
    for k in range(ranks // 2):
        first = total[:, 2 * k * width : (2 * k + 1) * width]
        second = total[:, (2 * k + 1) * width : (2 * k + 2) * width]
        place = slice(k * width, (k + 1) * width)
        keep_ref[:, place] = jnp.where(even, first, second)
        send_ref[:, place] = jnp.where(even, second, first)


def weight_cols(ranks, core, lefts, rights, tile=256):
    tokens, rows = lefts[0].shape
    *whole, last = rights
    pieces = last if isinstance(last, (list, tuple)) else [last]
    cols = pieces[0].shape[1]
    tile = min(tile, rows)
    micros = len(lefts)
    scratch = [] if len(pieces) == 1 else [pltpu.VMEM((tokens, cols), BF16)]
    return call(
        functools.partial(weight_cols_kernel, micros, ranks, len(pieces)),
        rows // tile,
        [smem()]
        + [pl.BlockSpec((tokens, tile), lambda i: (0, i))] * micros
        + [resident(side.shape) for side in (*whole, *pieces)],
        (pl.BlockSpec((tile, cols // 2), lambda i: (i, 0)),) * 2,
        (jax.ShapeDtypeStruct((rows, cols // 2), BF16),) * 2,
        scratch,
        far=SMALL,
    )(core, *lefts, *whole, *pieces)


def weight_kernel(micros, *refs):
    refs[-1][...] = weight_total(micros, refs).astype(BF16)


def weight_product(lefts, rights, tile=512):
    tokens, rows = lefts[0].shape
    cols = rights[0].shape[1]
    tile = min(tile, rows)
    micros = len(lefts)
    return call(
        functools.partial(weight_kernel, micros),
        rows // tile,
        [pl.BlockSpec((tokens, tile), lambda i: (0, i))] * micros
        + [resident((tokens, cols))] * micros,
        pl.BlockSpec((tile, cols), lambda i: (i, 0)),
        jax.ShapeDtypeStruct((rows, cols), BF16),
        far=SMALL,
    )(*lefts, *rights)


def add_kernel(left_ref, right_ref, out_ref):
    out_ref[...] = (left_ref[...].astype(F32) + right_ref[...].astype(F32)).astype(BF16)


def add_pair(left, right, tile=256):
    rows, cols = left.shape
    tile = min(tile, rows)
    spec = pl.BlockSpec((tile, cols), lambda i: (i, 0))
    return call(
        add_kernel,
        rows // tile,
        [spec, spec],
        spec,
        jax.ShapeDtypeStruct((rows, cols), BF16),
        far=SMALL,
    )(left, right)


def feed_tile(rows_ref, grad_ref, up_ref, down_ref, active_ref, gupper_ref):
    upper = dot_nn(rows_ref[...], up_ref[...])
    square = upper * upper
    slope = 0.7978845608028654
    bent = jnp.tanh(slope * upper * (1.0 + 0.044715 * square))
    half = 0.5 * (1.0 + bent)
    active_ref[...] = (upper * half).astype(BF16)
    inner = slope * (1.0 + 0.134145 * square)
    turn = half + 0.5 * upper * (1.0 - bent * bent) * inner
    gactive = dot_nt(grad_ref[...], down_ref[...])
    gupper_ref[...] = (gactive * turn).astype(BF16)


def feed_kernel(pieces, parts, steps, *refs):
    weights = refs[2 * pieces : 2 * (pieces + parts)]
    rows_ref, grad_ref, active_ref, gupper_ref = refs[2 * (pieces + parts) :]
    step = pl.program_id(0)

    @pl.when(step == 0)
    def _():
        assemble(rows_ref, refs[:pieces])
        assemble(grad_ref, refs[pieces : 2 * pieces])

    for part in range(parts):

        @pl.when(step // steps == part)
        def _(up_ref=weights[part], down_ref=weights[parts + part]):
            feed_tile(rows_ref, grad_ref, up_ref, down_ref, active_ref, gupper_ref)


def feed_forward(segments, cotangents, ups, downs, total, tile=512):
    rows = sum(segment.shape[0] for segment in segments)
    width = segments[0].shape[1]
    units = ups[0].shape[1]
    tile = min(tile, units)
    steps = units // tile
    parts = len(ups)

    def column(part):
        return lambda i: (0, jnp.clip(i - part * steps, 0, steps - 1))

    def row(part):
        return lambda i: (jnp.clip(i - part * steps, 0, steps - 1), 0)

    narrow = jax.ShapeDtypeStruct((rows, total * units), BF16)
    wide = jax.ShapeDtypeStruct((rows, width), BF16)
    return call(
        functools.partial(feed_kernel, len(segments), parts, steps),
        parts * steps,
        [resident(segment.shape) for segment in (*segments, *cotangents)]
        + [pl.BlockSpec((width, tile), column(part)) for part in range(parts)]
        + [pl.BlockSpec((tile, width), row(part)) for part in range(parts)],
        (resident((rows, width)),) * 2 + (pl.BlockSpec((rows, tile), lambda i: (0, i)),) * 2,
        (wide, wide, narrow, narrow),
        limit=44,
    )(*segments, *cotangents, *ups, *downs)


def feed_more_kernel(rows_ref, grad_ref, up_ref, down_ref, *refs):
    feed_tile(rows_ref, grad_ref, up_ref, down_ref, *refs[-2:])


def feed_more(rows, cotangents, up, down, part, before, tile=512):
    count, width = rows.shape
    tile = min(tile, up.shape[1])
    steps = up.shape[1] // tile
    held = pl.BlockSpec(memory_space=pl.ANY)
    return call(
        feed_more_kernel,
        steps,
        [
            resident((count, width)),
            resident((count, width)),
            pl.BlockSpec((width, tile), lambda i: (0, i)),
            pl.BlockSpec((tile, width), lambda i: (i, 0)),
            held,
            held,
        ],
        (pl.BlockSpec((count, tile), lambda i: (0, i + part * steps)),) * 2,
        tuple(jax.ShapeDtypeStruct(array.shape, BF16) for array in before),
        limit=44,
        aliases={4: 0, 5: 1},
    )(rows, cotangents, up, down, *before)


def unpack_kernel(kd, vd, grad_ref, *refs):
    start = 0
    for out_ref, width in zip(refs[-4:], (kd, kd, vd, vd)):
        out_ref[...] = grad_ref[:, start : start + width].astype(F32)
        start += width


def unpack(head, heads, kd, vd, grad, before):
    rows = grad.shape[0]
    widths = (kd, kd, vd, vd)
    operands = [grad]
    specs = [resident(grad.shape)]
    aliases = {}
    if before is not None:
        operands += before
        specs += [pl.BlockSpec(memory_space=pl.ANY)] * 4
        aliases = {1 + n: n for n in range(4)}
    return call(
        functools.partial(unpack_kernel, kd, vd),
        1,
        specs,
        tuple(pl.BlockSpec((rows, width), lambda i: (0, head)) for width in widths),
        tuple(jax.ShapeDtypeStruct((rows, heads * width), F32) for width in widths),
        aliases=aliases,
    )(*operands)


def decay_table(log_gamma, size, scale):
    row = lax.broadcasted_iota(jnp.int32, (size, size), 0)
    col = lax.broadcasted_iota(jnp.int32, (size, size), 1)
    table = jnp.exp((row - col).astype(F32) * log_gamma) * scale
    return table, jnp.where(row >= col, table, 0.0)


def pair_scale(docs, i, j, log_gamma, size):
    same = jnp.logical_and(docs[i] == docs[j], docs[i] >= 0)
    far = jnp.exp(jnp.full((1, 1), (i - j) * size, F32) * log_gamma)
    return jnp.where(same, far, 0.0)


def retention_forward_kernel(
    blocks, kd, vd, me_ref, docs_ref, rates_ref, proj_ref, mixed_ref, full_ref, diag_ref
):
    head = pl.program_id(0)
    size = proj_ref.shape[0] // blocks
    log_gamma = rates_ref[head]
    full_ref[...], diag_ref[...] = decay_table(log_gamma, size, kd**-0.5)
    me = me_ref[0]
    docs = [docs_ref[i] for i in range(blocks)]
    slots = [pl.ds(pl.multiple_of((i ^ me) * size, size), size) for i in range(blocks)]
    keys = slice(kd, 2 * kd)
    values = slice(2 * kd, 2 * kd + vd)
    for i in range(blocks):
        query = proj_ref[slots[i], :kd]
        total = None
        for j in range(i + 1):
            table = diag_ref if j == i else full_ref
            raw = dot_nt(query, proj_ref[slots[j], keys])
            scores = (raw * (table[...] * pair_scale(docs, i, j, log_gamma, size))).astype(BF16)
            term = dot_nn(scores, proj_ref[slots[j], values])
            total = term if total is None else total + term
        center = total - jnp.mean(total, axis=-1, keepdims=True)
        variance = jnp.mean(center * center, axis=-1, keepdims=True)
        normal = center * lax.rsqrt(jnp.maximum(variance, GROUP_FLOOR))
        gate = proj_ref[slots[i], 2 * kd + vd :].astype(F32)
        mixed_ref[slots[i], :] = (gate * jax.nn.sigmoid(gate) * normal).astype(BF16)


def retention_backward_kernel(
    head,
    blocks,
    kd,
    vd,
    me_ref,
    docs_ref,
    rates_ref,
    proj_ref,
    grad_ref,
    gproj_ref,
    full_ref,
    diag_ref,
    gkey_ref,
    gvalue_ref,
):
    size = proj_ref.shape[0] // blocks
    log_gamma = rates_ref[head]
    full_ref[...], diag_ref[...] = decay_table(log_gamma, size, kd**-0.5)
    me = me_ref[0]
    docs = [docs_ref[i] for i in range(blocks)]
    slots = [pl.ds(pl.multiple_of((i ^ me) * size, size), size) for i in range(blocks)]
    keys = slice(kd, 2 * kd)
    values = slice(2 * kd, 2 * kd + vd)
    gates = slice(2 * kd + vd, 2 * kd + 2 * vd)
    for i in range(blocks):
        query = proj_ref[slots[i], :kd]
        total = None
        masks = []
        kept = []
        for j in range(i + 1):
            table = diag_ref if j == i else full_ref
            mask = table[...] * pair_scale(docs, i, j, log_gamma, size)
            raw = dot_nt(query, proj_ref[slots[j], keys])
            scores = (raw * mask).astype(BF16)
            term = dot_nn(scores, proj_ref[slots[j], values])
            total = term if total is None else total + term
            kept.append(scores)
            masks.append(mask)
        center = total - jnp.mean(total, axis=-1, keepdims=True)
        variance = jnp.mean(center * center, axis=-1, keepdims=True)
        inverse = lax.rsqrt(jnp.maximum(variance, GROUP_FLOOR))
        normal = center * inverse
        gate = proj_ref[slots[i], gates].astype(F32)
        grad = grad_ref[slots[i], :].astype(F32)
        sig = jax.nn.sigmoid(gate)
        ggate = grad * normal * (sig * (1.0 + gate * (1.0 - sig)))
        gproj_ref[slots[i], gates] = ggate.astype(BF16)
        gnormal = grad * gate * sig
        along = jnp.mean(gnormal * normal, axis=-1, keepdims=True)
        along = jnp.where(variance > GROUP_FLOOR, along, 0.0)
        gcenter = inverse * (gnormal - normal * along)
        gret = (gcenter - jnp.mean(gcenter, axis=-1, keepdims=True)).astype(BF16)
        gquery = None
        for j in range(i + 1):
            graw = dot_nt(gret, proj_ref[slots[j], values])
            graw = (graw * masks[j]).astype(BF16)
            term = dot_nn(graw, proj_ref[slots[j], keys])
            gquery = term if gquery is None else gquery + term
            place = pl.ds(j * size, size)
            gkey = dot_tn(graw, query)
            gvalue = dot_tn(kept[j], gret)
            if j == i:
                gkey_ref[place, :] = gkey
                gvalue_ref[place, :] = gvalue
            else:
                gkey_ref[place, :] += gkey
                gvalue_ref[place, :] += gvalue
        gproj_ref[slots[i], :kd] = gquery.astype(BF16)
    for i in range(blocks):
        place = pl.ds(i * size, size)
        gproj_ref[slots[i], keys] = gkey_ref[place, :].astype(BF16)
        gproj_ref[slots[i], values] = gvalue_ref[place, :].astype(BF16)


def retention_forward(blocks, heads, kd, vd, me, docs, rates, proj):
    length = proj.shape[0]
    size = length // blocks
    return call(
        functools.partial(retention_forward_kernel, blocks, kd, vd),
        heads,
        [smem(), smem(), smem(), pl.BlockSpec((length, 2 * (kd + vd)), lambda h: (0, h))],
        pl.BlockSpec((length, vd), lambda h: (0, h)),
        jax.ShapeDtypeStruct((length, heads * vd), BF16),
        [pltpu.VMEM((size, size), F32)] * 2,
    )(me, docs, rates, proj)


def retention_backward(head, blocks, kd, vd, me, docs, rates, proj, grad):
    length = proj.shape[0]
    size = length // blocks
    width = 2 * (kd + vd)
    one = pl.Buffered(1)
    return call(
        functools.partial(retention_backward_kernel, head, blocks, kd, vd),
        1,
        [
            smem(),
            smem(),
            smem(),
            pl.BlockSpec((length, width), lambda i: (0, head), pipeline_mode=one),
            pl.BlockSpec((length, vd), lambda i: (0, head), pipeline_mode=one),
        ],
        resident((length, width)),
        jax.ShapeDtypeStruct((length, width), BF16),
        [pltpu.VMEM((size, size), F32)] * 2
        + [pltpu.VMEM((length, kd), F32), pltpu.VMEM((length, vd), F32)],
    )(me, docs, rates, proj, grad)


def body(
    layer_in,
    norm1_gain,
    w_query,
    w_key,
    w_value,
    w_gate,
    w_out,
    norm2_gain,
    w_up,
    w_down,
    decay_rates,
    seq_counts,
    out_grad,
):
    heads = decay_rates.shape[0]
    kd = w_query.shape[1] // heads
    vd = w_value.shape[1] // heads
    micros, rows_dev, width = layer_in.shape
    blocks = lax.axis_size("mp")
    length = rows_dev * blocks
    tall = [rows_dev] * blocks
    wide = [rows_dev] * 3 + [rows_dev // 2] * 2 if blocks == 4 else tall
    pieces = []
    for h in range(heads):
        pieces += [
            w_query[:, h * kd : (h + 1) * kd],
            w_key[:, h * kd : (h + 1) * kd],
            w_value[:, h * vd : (h + 1) * vd],
            w_gate[:, h * vd : (h + 1) * vd],
        ]
    w_in = jnp.concatenate(pieces, 1)
    gain_one = norm1_gain.reshape(1, -1)
    gain_two = norm2_gain.reshape(1, -1)
    rates = jnp.log1p(-decay_rates)
    me = lax.axis_index("mp").reshape(1).astype(jnp.int32)
    starts = jnp.arange(blocks, dtype=jnp.int32) * rows_dev
    a, b = range(micros)
    docs = [document_ids(seq_counts[0, m], starts, length) for m in (a, b)]
    def backward(h, m, proj, grad):
        return retention_backward(h, blocks, kd, vd, me, docs[m], rates, proj, grad)

    up_rows, down_rows = (
        weight.shape[0] // lax.axis_size("dp") for weight in (w_up, w_down)
    )

    def eighth_rows():
        place = lax.axis_index("dp")
        up = lax.dynamic_slice_in_dim(w_up, place * up_rows, up_rows, 0)
        down = lax.dynamic_slice_in_dim(w_down, place * down_rows, down_rows, 0)
        cut = w_up.shape[1]
        return jnp.concatenate(
            [up] + [down[:, k : k + cut] for k in range(0, width, cut)], 0
        )

    def exchange(rows):
        return move(rows, "mp", 2) if blocks == 4 else rows

    def neighbour_weights(rows):
        if blocks != 4:
            return []
        down = [
            rows[k : k + down_rows] for k in range(up_rows, rows.shape[0], down_rows)
        ]
        return [
            lax.all_gather(part, "dp", axis=0, tiled=True)
            for part in (rows[:up_rows], jnp.concatenate(down, 1))
        ]

    def pair_send(total, dim):
        if blocks != 4:
            return [total]
        half = total.shape[1 - dim] // 2
        own = lax.slice_in_dim(total, 0, half, axis=1 - dim)
        other = lax.slice_in_dim(total, half, 2 * half, axis=1 - dim)
        return [own, move(other, "mp", 2)]

    def pair_sum(halves):
        return sum(half.astype(F32) for half in halves)

    ranks = lax.axis_size("dp")
    core = (lax.axis_index("dp") % 2).reshape(1).astype(jnp.int32)

    def cores(kept_sent):
        kept, sent = kept_sent
        return kept, move(sent, "dp", 1)

    def weight_sum(total, dim, whole=False):
        groups = [list(range(parity, ranks, 2)) for parity in (0, 1)]
        return lax.psum_scatter(
            total,
            "dp",
            scatter_dimension=dim,
            tiled=True,
            axis_index_groups=None if whole else groups,
        )

    normed_a = first_norm(a, layer_in, gain_one)
    normed_b = first_norm(b, after(layer_in, normed_a, w_in), gain_one)
    go_one_a = Gather(normed_a)
    eighths = eighth_rows()
    fenced = fence(go_one_a, normed_b, eighths, docs, rates, me)
    go_one_a, normed_b, eighths, docs, rates, me = fenced
    forward = (blocks, heads, kd, vd, me)
    go_one_a.middle()
    go_one_a, normed_b = fence(go_one_a, normed_b)

    go_one_b = Gather(normed_b)
    eighths = exchange(after(eighths, normed_b))
    cot_a = PairGather(after(out_grad[a], normed_b))
    gathered_a, proj_a = gather_product(go_one_a.result(), w_in, False)
    mixed_a = retention_forward(*forward, docs[a], rates, proj_a)
    go_one_b, eighths, cot_a, mixed_a = fence(go_one_b, eighths, cot_a, mixed_a)
    go_one_b.middle()
    more = neighbour_weights(eighths)
    parts = product_scatter([mixed_a], [w_out], False, tall)
    go_one_b, parts = fence(go_one_b, parts)

    sum_one_a = TallScatterSum(parts)
    cot_b = PairGather(after(out_grad[b], parts))
    gathered_b, proj_b = gather_product(go_one_b.result(), w_in, False)
    sum_one_a, cot_b, proj_b = fence(sum_one_a, cot_b, proj_b)
    sum_one_a.middle()
    mixed_b = retention_forward(*forward, docs[b], rates, proj_b)
    parts = product_scatter([mixed_b], [w_out], False, tall)
    sum_one_a, parts = fence(sum_one_a, parts)

    pair = [rows_dev] * 2 if blocks == 4 else tall
    hidden_a, normed = second_norm(a, layer_in, gain_two, sum_one_a.result())
    go_two_a = PairGather(normed)
    sum_one_b = TallScatterSum(parts)
    go_two_a, sum_one_b, hidden_a = fence(go_two_a, sum_one_b, hidden_a)
    sum_one_b.middle()
    total = 2 if blocks == 4 else 1
    rows_two_a, cotangent_a, *feed_a = feed_forward(
        go_two_a.result(), cot_a.result(), [w_up], [w_down], total
    )
    sum_one_b, more, rows_two_a, cotangent_a, feed_a = fence(
        sum_one_b, more, rows_two_a, cotangent_a, feed_a
    )

    ups, downs = [w_up, *more[:1]], [w_down, *more[1:]]
    hidden_b, normed = second_norm(b, layer_in, gain_two, sum_one_b.result())
    go_two_b = PairGather(normed)
    feed_a = after(feed_a, hidden_b)
    if blocks == 4:
        feed_a = feed_more(rows_two_a, cotangent_a, *more, 1, feed_a)
    active_a, gupper_a = feed_a
    parts = product_scatter([gupper_a], ups, True, pair)
    go_two_b, parts = fence(go_two_b, parts)

    sum_three_a = PairScatter(parts)
    rows_two_b, cotangent_b, active_b, gupper_b = feed_forward(
        go_two_b.result(), cot_b.result(), ups, downs, total
    )
    dw_down = weight_product((active_a, active_b), (cotangent_a, cotangent_b))
    fenced = fence(sum_three_a, dw_down, gupper_b, (active_a, active_b))
    sum_three_a, dw_down, gupper_b, actives = fenced

    down_total = weight_sum(dw_down, 1, True)
    parts = product_scatter([gupper_b], ups, True, pair)
    ghidden_a, normed_a, gain_two_a = second_back(
        a, out_grad, hidden_a, gain_two, sum_three_a.result(parts)
    )
    parts, normed_a = fence(parts, normed_a)
    sum_three_b = PairScatter(parts)
    dw_up = weight_rows(
        ranks, core, after((rows_two_a, rows_two_b), normed_a), (gupper_a, gupper_b)
    )
    feeds = [product_scatter([after(actives[0], dw_up)], downs, False, pair, far=SMALL)]
    sum_three_b, normed_a, dw_up, feeds = fence(sum_three_b, normed_a, dw_up, feeds)
    go_three_a = Gather(normed_a)
    dw_up = cores(dw_up)
    ghidden_b, normed_b, gain_two_b = second_back(
        b, out_grad, hidden_b, gain_two, sum_three_b.result()
    )
    feeds.append(
        product_scatter([after(actives[1], normed_b)], downs, False, pair, far=SMALL)
    )
    go_three_a, normed_b, dw_up, feeds = fence(go_three_a, normed_b, dw_up, feeds)
    go_three_a.middle()
    dw_up = add_pair(*dw_up)
    go_three_a, normed_b, dw_up, feeds = fence(go_three_a, normed_b, dw_up, feeds)

    up_total = weight_sum(dw_up, 0)
    go_three_b = Gather(normed_b)
    branch_a, gmixed_a = gather_product(go_three_a.result(), w_out, True)
    gproj_a = [backward(0, a, proj_a, gmixed_a)]
    go_three_b, gproj_a, gmixed_a = fence(go_three_b, gproj_a, gmixed_a)
    go_three_b.middle()
    for h in range(1, heads):
        gproj_a.append(backward(h, a, proj_a, gmixed_a))
    go_three_b, gproj_a, down_total = fence(go_three_b, gproj_a, down_total)

    dw_out = weight_cols(ranks, core, (mixed_a, mixed_b), (branch_a, go_three_b.result()))
    dw_out, go_three_b = fence(dw_out, go_three_b)
    dw_out = cores(dw_out)
    branch_b, gmixed_b = gather_product(go_three_b.result(), w_out, True)
    dw_out, gmixed_b = fence(dw_out, gmixed_b)
    dw_out = add_pair(*dw_out)
    dw_out, gmixed_b, feeds = fence(dw_out, gmixed_b, feeds)
    grad_w_out = weight_sum(dw_out, 1)
    sum_two_a = PairScatter(feeds[0])
    gproj_b = [backward(0, b, proj_b, gmixed_b)]
    dw_in = weight_product((gathered_a, gathered_b), (gproj_a[0], gproj_b[0]))
    fenced = fence(sum_two_a, dw_in, gproj_b, gproj_a, gmixed_b, feeds, up_total)
    sum_two_a, dw_in, gproj_b, gproj_a, gmixed_b, feeds, up_total = fenced
    grad_w_in = [weight_sum(dw_in, 0, True)]
    grad_w_down = pair_send(down_total, 1)
    sum_two_b = PairScatter(feeds[1])
    parts = product_scatter(gproj_a, [w_in], True, wide, far=SMALL)
    fenced = fence(sum_two_b, parts, gproj_b, grad_w_out, grad_w_down)
    sum_two_b, parts, gproj_b, grad_w_out, grad_w_down = fenced
    grad_w_up = pair_send(up_total, 0)
    sum_four_a = ScatterSum(parts)
    for h in range(1, heads):
        gproj_b.append(backward(h, b, proj_b, after(gmixed_b, gproj_b)))
        dw_in = weight_rows(ranks, core, (gathered_a, gathered_b), (gproj_a[h], gproj_b[h]))
    sum_four_a, dw_in, gproj_b, grad_w_up = fence(sum_four_a, dw_in, gproj_b, grad_w_up)
    sum_four_a.middle()
    if heads > 1:
        dw_in = cores(dw_in)
    parts = product_scatter(gproj_b, [w_in], True, wide)
    sum_four_a, dw_in, parts = fence(sum_four_a, dw_in, parts)
    if heads > 1:
        dw_in = add_pair(*dw_in)
    dw_in, grad_w_in, parts, sum_four_a = fence(dw_in, grad_w_in, parts, sum_four_a)
    in_grads = unpack(0, heads, kd, vd, grad_w_in[0], None)

    if heads > 1:
        grad_w_in.append(weight_sum(dw_in, 0))
    sum_four_b = ScatterSum(parts)
    grad_input, gain_one_a = first_back(
        a, layer_in, ghidden_a, gain_one, sum_four_a.result(), None
    )
    layer_out = layer_end(a, micros, hidden_a, sum_two_a.result(grad_input), None)
    layer_out = layer_end(b, micros, hidden_b, sum_two_b.result(), layer_out)
    sum_four_b, grad_input, layer_out = fence(sum_four_b, grad_input, layer_out)
    sum_four_b.middle()
    grad_w_down, grad_w_up = pair_sum(grad_w_down), pair_sum(grad_w_up)
    grad_w_out = grad_w_out.astype(F32)
    fenced = fence(sum_four_b, in_grads, grad_w_out, grad_w_down, grad_w_up)
    sum_four_b, in_grads, grad_w_out, grad_w_down, grad_w_up = fenced
    grad_input, gain_one_b = first_back(
        b, layer_in, ghidden_b, gain_one, sum_four_b.result(), grad_input
    )

    for h in range(1, heads):
        in_grads = unpack(h, heads, kd, vd, grad_w_in[h], in_grads)
    gains = small_sum(
        jnp.concatenate([gain_one_a + gain_one_b, gain_two_a + gain_two_b], 0)
    )
    return (
        layer_out,
        grad_input,
        gains[0],
        *in_grads,
        grad_w_out,
        gains[1],
        grad_w_up,
        grad_w_down,
    )


def solution(mesh):
    in_specs = (
        P(None, ("dp", "mp"), None),
        P(),
        P(None, "mp"),
        P(None, "mp"),
        P(None, "mp"),
        P(None, "mp"),
        P("mp", None),
        P(),
        P(None, "mp"),
        P("mp", None),
        P("mp"),
        P("dp", None, None),
        P(None, ("dp", "mp"), None),
    )
    out_specs = (
        P(None, ("dp", "mp"), None),
        P(None, ("dp", "mp"), None),
        P("dp"),
        P("dp", "mp"),
        P("dp", "mp"),
        P("dp", "mp"),
        P("dp", "mp"),
        P("mp", "dp"),
        P("dp"),
        P("dp", "mp"),
        P("mp", "dp"),
    )
    return jax.shard_map(body, mesh=mesh, in_specs=in_specs, out_specs=out_specs, check_vma=False)
```

```python
import functools

import jax
import jax.numpy as jnp
from jax import lax
from jax.experimental import pallas as pl
from jax.experimental.pallas import tpu as pltpu
from jax.sharding import PartitionSpec as P

NORM_EPS = 1e-05
GROUP_FLOOR = 1.0
BF16 = jnp.bfloat16
F32 = jnp.float32
TINY = pl.CostEstimate(flops=1, bytes_accessed=1, transcendentals=0)


def document_ids(counts, position, length):
    half_len = length // 2
    quarter_len = length // 4
    long_end = counts[2] * length
    half_end = long_end + counts[1] * half_len
    quarter_end = half_end + counts[0] * quarter_len
    long_ids = position // length
    half_ids = counts[2] + (position - long_end) // half_len
    quarter_ids = counts[2] + counts[1] + (position - half_end) // quarter_len
    inner = jnp.where(position < quarter_end, quarter_ids, -1)
    inner = jnp.where(position < half_end, half_ids, inner)
    return jnp.where(position < long_end, long_ids, inner)


def dot_nt(left, right):
    return lax.dot_general(left, right, (((1,), (1,)), ((), ())), preferred_element_type=F32)


def dot_tn(left, right):
    return lax.dot_general(left, right, (((0,), (0,)), ((), ())), preferred_element_type=F32)


def dot_nn(left, right):
    return jnp.dot(left, right, preferred_element_type=F32)


def move(value, axis, step):
    size = lax.axis_size(axis)
    return lax.ppermute(value, axis, [(i, i ^ step) for i in range(size)])


def after(value, *earlier):
    return lax.optimization_barrier((value, earlier))[0]


def fence(*values):
    return lax.optimization_barrier(values)


class Transfer:
    def __init_subclass__(cls):
        jax.tree_util.register_pytree_node(
            cls, lambda self: (self.parts(), None), lambda _, parts: cls.rebuild(parts)
        )

    def parts(self):
        return (self.kept, self.pieces)

    @classmethod
    def rebuild(cls, parts):
        self = object.__new__(cls)
        self.kept, self.pieces = parts
        return self

    def result(self, *earlier):
        return after([*self.kept, *self.pieces], earlier)


class Gather(Transfer):
    def __init__(self, rows):
        steps = (1, 2) if lax.axis_size("mp") == 4 else range(1, lax.axis_size("mp"))
        self.kept = [rows]
        self.pieces = [move(rows, "mp", k) for k in steps]

    def middle(self):
        if lax.axis_size("mp") == 4:
            first, second = self.pieces
            half = first.shape[0] // 2
            self.kept = [*self.kept, first, second]
            self.pieces = [move(first[:half], "mp", 2), move(second[half:], "mp", 1)]


class ScatterSum(Transfer):
    def __init__(self, segments):
        if lax.axis_size("mp") == 4:
            self.kept = [*segments[:3]]
            upper, lower = segments[3:]
            self.pieces = [move(upper, "mp", 1), move(lower, "mp", 2)]
        else:
            self.kept = [segments[0]]
            self.pieces = [move(part, "mp", k + 1) for k, part in enumerate(segments[1:])]

    def middle(self):
        if lax.axis_size("mp") == 4:
            own, first, second = self.kept
            upper, lower = self.pieces
            half = upper.shape[0]
            first = jnp.concatenate([first[:half], first[half:] + lower], 0)
            second = jnp.concatenate([second[:half] + upper, second[half:]], 0)
            self.kept = [own]
            self.pieces = [move(first, "mp", 1), move(second, "mp", 2)]


class TallScatterSum(ScatterSum):
    def __init__(self, segments):
        if lax.axis_size("mp") == 4:
            self.kept = [*segments[:3]]
            self.pieces = [move(segments[3], "mp", 2)]
        else:
            super().__init__(segments)

    def middle(self):
        if lax.axis_size("mp") == 4:
            own, first, second = self.kept
            self.kept = [own]
            self.pieces = [move(first + self.pieces[0], "mp", 1), move(second, "mp", 2)]


class PairGather(Transfer):
    def __init__(self, rows):
        steps = (1,) if lax.axis_size("mp") == 4 else range(1, lax.axis_size("mp"))
        self.kept = [rows]
        self.pieces = [move(rows, "mp", k) for k in steps]


class PairScatter(Transfer):
    def __init__(self, segments):
        self.kept = [segments[0]]
        self.pieces = [move(part, "mp", k + 1) for k, part in enumerate(segments[1:])]


def small_sum(value):
    value = value + sum(move(value, "mp", k) for k in range(1, lax.axis_size("mp")))
    half = lax.axis_size("dp") // 2
    place = lax.axis_index("dp")
    split = value.reshape(value.shape[0], half, 2, -1)
    even = place % 2 == 0
    kept = jnp.where(even, split[:, :, 0], split[:, :, 1])
    sent = jnp.where(even, split[:, :, 1], split[:, :, 0])
    kept = kept + move(sent, "dp", 1)
    pick = lambda chip: lax.dynamic_index_in_dim(kept, chip, 1, False)
    chip = place // 2
    return pick(chip) + sum(move(pick(chip ^ k), "dp", 2 * k) for k in range(1, half))


LARGE, SMALL = 5 << 19, 1 << 18


def nbytes(array):
    return array.size * array.dtype.itemsize


def resident(shape):
    zeros = (0,) * len(shape)
    return pl.BlockSpec(tuple(shape), lambda i: zeros, pipeline_mode=pl.Buffered(1))


def smem():
    return pl.BlockSpec(memory_space=pltpu.SMEM)


def call(kernel, steps, in_specs, out_specs, out_shape, scratch=(), limit=32, aliases=None, far=LARGE, in_far=None):
    name = getattr(kernel, "func", kernel).__name__.removesuffix("_kernel")
    several = isinstance(out_shape, tuple)
    outs = [
        pltpu.HBM(out.shape, out.dtype) if nbytes(out) > far else out
        for out in (out_shape if several else (out_shape,))
    ]
    run = pl.pallas_call(
        kernel,
        name=name,
        grid=(steps,),
        in_specs=in_specs,
        out_specs=out_specs,
        out_shape=tuple(outs) if several else outs[0],
        scratch_shapes=list(scratch),
        input_output_aliases=aliases or {},
        compiler_params=pltpu.CompilerParams(vmem_limit_bytes=limit << 20),
        cost_estimate=TINY,
    )

    def placed(*operands):
        return run(
            *[
                pltpu.with_memory_space_constraint(operand, pltpu.HBM)
                if nbytes(operand) > (in_far or far)
                else operand
                for operand in operands
            ]
        )

    return placed


def assemble(out_ref, refs):
    offset = 0
    for ref in refs:
        rows = ref.shape[0]
        out_ref[offset : offset + rows, :] = ref[...]
        offset += rows


def dissolve(refs, value):
    offset = 0
    for ref in refs:
        rows = ref.shape[0]
        ref[...] = value[offset : offset + rows].astype(ref.dtype)
        offset += rows


def add_up(refs):
    total = refs[0][...].astype(F32)
    for ref in refs[1:]:
        total = total + ref[...].astype(F32)
    return total


def normalize(rows):
    center = rows - jnp.mean(rows, axis=-1, keepdims=True)
    variance = jnp.mean(center * center, axis=-1, keepdims=True)
    inverse = lax.rsqrt(variance + NORM_EPS)
    return center * inverse, inverse


def first_norm_kernel(rows_ref, gain_ref, out_ref):
    normal, _ = normalize(rows_ref[0].astype(F32))
    out_ref[...] = (normal * gain_ref[...].astype(F32)).astype(BF16)


def first_norm(m, rows, gain):
    _, count, width = rows.shape
    narrow = jax.ShapeDtypeStruct((count, width), BF16)
    return call(
        first_norm_kernel,
        1,
        [pl.BlockSpec((1, count, width), lambda i: (m, 0, 0)), resident((1, width))],
        resident((count, width)),
        narrow,
    )(rows, gain)


def second_norm_kernel(rows_ref, gain_ref, *refs):
    hidden_ref, out_ref = refs[-2:]
    hidden = rows_ref[0].astype(F32) + add_up(refs[:-2])
    hidden_ref[...] = hidden
    normal, _ = normalize(hidden)
    out_ref[...] = (normal * gain_ref[...].astype(F32)).astype(BF16)


def second_norm(m, rows, gain, terms, far=LARGE):
    _, count, width = rows.shape
    narrow = jax.ShapeDtypeStruct((count, width), BF16)
    return call(
        second_norm_kernel,
        1,
        [pl.BlockSpec((1, count, width), lambda i: (m, 0, 0)), resident((1, width))]
        + [resident(piece.shape) for piece in terms],
        (resident((count, width)),) * 2,
        (jax.ShapeDtypeStruct((count, width), F32), narrow),
        far=far,
    )(rows, gain, *terms)


def norm_back(rows, gain, grad):
    normal, inverse = normalize(rows)
    scaled = grad * gain
    along = jnp.mean(scaled * normal, axis=-1, keepdims=True)
    inner = scaled - jnp.mean(scaled, axis=-1, keepdims=True) - normal * along
    return inverse * inner, jnp.sum(grad * normal, axis=0, keepdims=True)


def second_back_kernel(cot_ref, hidden_ref, gain_ref, *refs):
    total_ref, out_ref, ggain_ref = refs[-3:]
    grad = add_up(refs[:-3])
    part, ggain_ref[...] = norm_back(hidden_ref[...], gain_ref[...].astype(F32), grad)
    total = cot_ref[0].astype(F32) + part
    total_ref[...] = total
    out_ref[...] = total.astype(BF16)


def second_back(m, cotangent, hidden, gain, terms):
    count, width = hidden.shape
    narrow = jax.ShapeDtypeStruct((count, width), BF16)
    return call(
        second_back_kernel,
        1,
        [
            pl.BlockSpec((1, count, width), lambda i: (m, 0, 0)),
            resident((count, width)),
            resident((1, width)),
        ]
        + [resident(piece.shape) for piece in terms],
        (resident((count, width)), resident((count, width)), resident((1, width))),
        (
            jax.ShapeDtypeStruct((count, width), F32),
            narrow,
            jax.ShapeDtypeStruct((1, width), F32),
        ),
    )(cotangent, hidden, gain, *terms)


def first_back_kernel(terms, rows_ref, ghidden_ref, gain_ref, *refs):
    out_ref, ggain_ref = refs[-2:]
    grad = add_up(refs[:terms])
    part, ggain_ref[...] = norm_back(
        rows_ref[0].astype(F32), gain_ref[...].astype(F32), grad
    )
    out_ref[0] = ghidden_ref[...] + part


def first_back(m, rows, ghidden, gain, terms, before):
    micros, count, width = rows.shape
    block = pl.BlockSpec((1, count, width), lambda i: (m, 0, 0))
    specs = [block, resident((count, width)), resident((1, width))]
    specs += [resident(piece.shape) for piece in terms]
    operands = [rows, ghidden, gain, *terms]
    aliases = {}
    if before is not None:
        aliases = {len(operands): 0}
        operands.append(before)
        specs.append(pl.BlockSpec(memory_space=pl.ANY))
    return call(
        functools.partial(first_back_kernel, len(terms)),
        1,
        specs,
        (block, resident((1, width))),
        (
            jax.ShapeDtypeStruct((micros, count, width), F32),
            jax.ShapeDtypeStruct((1, width), F32),
        ),
        aliases=aliases,
    )(*operands)


def layer_end_kernel(terms, hidden_ref, *refs):
    out_ref = refs[-1]
    total = add_up(refs[:terms])
    out_ref[0] = (hidden_ref[...] + total).astype(BF16)


def layer_end(m, micros, hidden, terms, before):
    count, width = hidden.shape
    specs = [resident((count, width))] + [resident(piece.shape) for piece in terms]
    operands = [hidden, *terms]
    aliases = {}
    if before is not None:
        aliases = {len(operands): 0}
        operands.append(before)
        specs.append(pl.BlockSpec(memory_space=pl.ANY))
    return call(
        functools.partial(layer_end_kernel, len(terms)),
        1,
        specs,
        pl.BlockSpec((1, count, width), lambda i: (m, 0, 0)),
        jax.ShapeDtypeStruct((micros, count, width), BF16),
        aliases=aliases,
    )(*operands)


def gather_product_kernel(dot, pieces, *refs):
    right_ref, all_ref, out_ref = refs[pieces:]

    @pl.when(pl.program_id(0) == 0)
    def _():
        assemble(all_ref, refs[:pieces])

    out_ref[...] = dot(all_ref[...], right_ref[...]).astype(out_ref.dtype)


def gather_product(segments, right, transposed, tile=512):
    rows = sum(segment.shape[0] for segment in segments)
    width = segments[0].shape[1]
    cols = right.shape[0] if transposed else right.shape[1]
    tile = min(tile, cols)
    if transposed:
        spec = pl.BlockSpec((tile, width), lambda i: (i, 0))
    else:
        spec = pl.BlockSpec((width, tile), lambda i: (0, i))
    return call(
        functools.partial(
            gather_product_kernel, dot_nt if transposed else dot_nn, len(segments)
        ),
        cols // tile,
        [resident(segment.shape) for segment in segments] + [spec],
        (resident((rows, width)), pl.BlockSpec((rows, tile), lambda i: (0, i))),
        (jax.ShapeDtypeStruct((rows, width), BF16), jax.ShapeDtypeStruct((rows, cols), BF16)),
    )(*segments, right)


def product_scatter_kernel(transposed, lefts, rights, *refs):
    left_refs = refs[:lefts]
    right_refs = refs[lefts : lefts + rights]
    axis = 1 if transposed else 0
    width = min(
        [ref.shape[1] for ref in left_refs] + [ref.shape[axis] for ref in right_refs]
    )
    depth = sum(ref.shape[1] for ref in left_refs)
    total = None
    for start in range(0, depth, width):
        place, offset = divmod(start, left_refs[0].shape[1])
        left = left_refs[place][:, offset : offset + width]
        place, offset = divmod(start, right_refs[0].shape[axis])
        if transposed:
            term = dot_nt(left, right_refs[place][:, offset : offset + width])
        else:
            term = dot_nn(left, right_refs[place][offset : offset + width, :])
        total = term if total is None else total + term
    dissolve(refs[lefts + rights :], total)


def product_scatter(lefts, rights, transposed, counts, tile=512, far=LARGE):
    cols = rights[0].shape[0] if transposed else rights[0].shape[1]
    tile = min(tile, cols)
    if transposed:
        specs = [pl.BlockSpec((tile, right.shape[1]), lambda i: (i, 0)) for right in rights]
    else:
        specs = [pl.BlockSpec((right.shape[0], tile), lambda i: (0, i)) for right in rights]
    return call(
        functools.partial(product_scatter_kernel, transposed, len(lefts), len(rights)),
        cols // tile,
        [resident(left.shape) for left in lefts] + specs,
        tuple(pl.BlockSpec((count, tile), lambda i: (0, i)) for count in counts),
        tuple(jax.ShapeDtypeStruct((count, cols), BF16) for count in counts),
        far=far,
    )(*lefts, *rights)


def weight_total(micros, refs):
    total = dot_tn(refs[0][...], refs[micros][...])
    for m in range(1, micros):
        total = total + dot_tn(refs[m][...], refs[micros + m][...])
    return total


def weight_rows_kernel(micros, core_ref, *refs):
    keep_ref, send_ref = refs[-2:]
    total = weight_total(micros, refs)
    kept = pl.program_id(0) % 2 == core_ref[0]

    @pl.when(kept)
    def _():
        keep_ref[...] = total.astype(BF16)

    @pl.when(jnp.logical_not(kept))
    def _():
        send_ref[...] = total.astype(BF16)


def weight_rows(ranks, core, lefts, rights):
    tokens, rows = lefts[0].shape
    cols = rights[0].shape[1]
    tile = rows // ranks
    micros = len(lefts)
    return call(
        functools.partial(weight_rows_kernel, micros),
        ranks,
        [smem()]
        + [pl.BlockSpec((tokens, tile), lambda i: (0, i))] * micros
        + [resident((tokens, cols))] * micros,
        (pl.BlockSpec((tile, cols), lambda i: (i // 2, 0)),) * 2,
        (jax.ShapeDtypeStruct((rows // 2, cols), BF16),) * 2,
    far=SMALL,
    )(core, *lefts, *rights)


def weight_cols_kernel(micros, ranks, pieces, core_ref, *refs):
    keep_ref, send_ref = refs[2 * micros + pieces - 1 : 2 * micros + pieces + 1]
    sides = list(refs[: 2 * micros - 1])
    if pieces == 1:
        sides.append(refs[2 * micros - 1])
    else:
        last_ref = refs[-1]
        sides.append(last_ref)

        @pl.when(pl.program_id(0) == 0)
        def _():
            assemble(last_ref, refs[2 * micros - 1 : 2 * micros - 1 + pieces])

    total = weight_total(micros, sides).astype(BF16)
    width = total.shape[1] // ranks
    even = core_ref[0] == 0
    for k in range(ranks // 2):
        first = total[:, 2 * k * width : (2 * k + 1) * width]
        second = total[:, (2 * k + 1) * width : (2 * k + 2) * width]
        place = slice(k * width, (k + 1) * width)
        keep_ref[:, place] = jnp.where(even, first, second)
        send_ref[:, place] = jnp.where(even, second, first)


def weight_cols(ranks, core, lefts, rights, tile=256):
    tokens, rows = lefts[0].shape
    *whole, last = rights
    pieces = last if isinstance(last, (list, tuple)) else [last]
    cols = pieces[0].shape[1]
    tile = min(tile, rows)
    micros = len(lefts)
    scratch = [] if len(pieces) == 1 else [pltpu.VMEM((tokens, cols), BF16)]
    return call(
        functools.partial(weight_cols_kernel, micros, ranks, len(pieces)),
        rows // tile,
        [smem()]
        + [pl.BlockSpec((tokens, tile), lambda i: (0, i))] * micros
        + [resident(side.shape) for side in (*whole, *pieces)],
        (pl.BlockSpec((tile, cols // 2), lambda i: (i, 0)),) * 2,
        (jax.ShapeDtypeStruct((rows, cols // 2), BF16),) * 2,
        scratch,
        far=SMALL,
    )(core, *lefts, *whole, *pieces)


def weight_kernel(micros, *refs):
    refs[-1][...] = weight_total(micros, refs).astype(BF16)


def weight_product(lefts, rights, tile=512):
    tokens, rows = lefts[0].shape
    cols = rights[0].shape[1]
    tile = min(tile, rows)
    micros = len(lefts)
    return call(
        functools.partial(weight_kernel, micros),
        rows // tile,
        [pl.BlockSpec((tokens, tile), lambda i: (0, i))] * micros
        + [resident((tokens, cols))] * micros,
        pl.BlockSpec((tile, cols), lambda i: (i, 0)),
        jax.ShapeDtypeStruct((rows, cols), BF16),
        far=SMALL,
    )(*lefts, *rights)


def add_kernel(left_ref, right_ref, out_ref):
    out_ref[...] = (left_ref[...].astype(F32) + right_ref[...].astype(F32)).astype(BF16)


def add_pair(left, right, tile=256):
    rows, cols = left.shape
    tile = min(tile, rows)
    spec = pl.BlockSpec((tile, cols), lambda i: (i, 0))
    return call(
        add_kernel,
        rows // tile,
        [spec, spec],
        spec,
        jax.ShapeDtypeStruct((rows, cols), BF16),
        far=SMALL,
    )(left, right)


def feed_tile(rows_ref, grad_ref, up_ref, down_ref, active_ref, gupper_ref):
    upper = dot_nn(rows_ref[...], up_ref[...])
    square = upper * upper
    slope = 0.7978845608028654
    bent = jnp.tanh(slope * upper * (1.0 + 0.044715 * square))
    half = 0.5 * (1.0 + bent)
    active_ref[...] = (upper * half).astype(BF16)
    inner = slope * (1.0 + 0.134145 * square)
    turn = half + 0.5 * upper * (1.0 - bent * bent) * inner
    gactive = dot_nt(grad_ref[...], down_ref[...])
    gupper_ref[...] = (gactive * turn).astype(BF16)


def feed_kernel(pieces, parts, steps, *refs):
    weights = refs[2 * pieces : 2 * (pieces + parts)]
    rows_ref, grad_ref, active_ref, gupper_ref = refs[2 * (pieces + parts) :]
    step = pl.program_id(0)

    @pl.when(step == 0)
    def _():
        assemble(rows_ref, refs[:pieces])
        assemble(grad_ref, refs[pieces : 2 * pieces])

    for part in range(parts):

        @pl.when(step // steps == part)
        def _(up_ref=weights[part], down_ref=weights[parts + part]):
            feed_tile(rows_ref, grad_ref, up_ref, down_ref, active_ref, gupper_ref)


def feed_forward(segments, cotangents, ups, downs, total, tile=512):
    rows = sum(segment.shape[0] for segment in segments)
    width = segments[0].shape[1]
    units = ups[0].shape[1]
    tile = min(tile, units)
    steps = units // tile
    parts = len(ups)

    def column(part):
        return lambda i: (0, jnp.clip(i - part * steps, 0, steps - 1))

    def row(part):
        return lambda i: (jnp.clip(i - part * steps, 0, steps - 1), 0)

    narrow = jax.ShapeDtypeStruct((rows, total * units), BF16)
    wide = jax.ShapeDtypeStruct((rows, width), BF16)
    return call(
        functools.partial(feed_kernel, len(segments), parts, steps),
        parts * steps,
        [resident(segment.shape) for segment in (*segments, *cotangents)]
        + [pl.BlockSpec((width, tile), column(part)) for part in range(parts)]
        + [pl.BlockSpec((tile, width), row(part)) for part in range(parts)],
        (resident((rows, width)),) * 2 + (pl.BlockSpec((rows, tile), lambda i: (0, i)),) * 2,
        (wide, wide, narrow, narrow),
        limit=44,
        far=SMALL,
        in_far=LARGE,
    )(*segments, *cotangents, *ups, *downs)


def feed_more_kernel(rows_ref, grad_ref, up_ref, down_ref, *refs):
    feed_tile(rows_ref, grad_ref, up_ref, down_ref, *refs[-2:])


def feed_more(rows, cotangents, up, down, part, before, tile=256):
    count, width = rows.shape
    tile = min(tile, up.shape[1])
    steps = up.shape[1] // tile
    held = pl.BlockSpec(memory_space=pl.ANY)
    return call(
        feed_more_kernel,
        steps,
        [
            resident((count, width)),
            resident((count, width)),
            pl.BlockSpec((width, tile), lambda i: (0, i)),
            pl.BlockSpec((tile, width), lambda i: (i, 0)),
            held,
            held,
        ],
        (pl.BlockSpec((count, tile), lambda i: (0, i + part * steps)),) * 2,
        tuple(jax.ShapeDtypeStruct(array.shape, BF16) for array in before),
        limit=44,
        aliases={4: 0, 5: 1},
        far=SMALL,
    )(rows, cotangents, up, down, *before)


def unpack_kernel(kd, vd, grad_ref, *refs):
    start = 0
    for out_ref, width in zip(refs[-4:], (kd, kd, vd, vd)):
        out_ref[...] = grad_ref[:, start : start + width].astype(F32)
        start += width


def unpack(head, heads, kd, vd, grad, before):
    rows = grad.shape[0]
    widths = (kd, kd, vd, vd)
    operands = [grad]
    specs = [resident(grad.shape)]
    aliases = {}
    if before is not None:
        operands += before
        specs += [pl.BlockSpec(memory_space=pl.ANY)] * 4
        aliases = {1 + n: n for n in range(4)}
    return call(
        functools.partial(unpack_kernel, kd, vd),
        1,
        specs,
        tuple(pl.BlockSpec((rows, width), lambda i: (0, head)) for width in widths),
        tuple(jax.ShapeDtypeStruct((rows, heads * width), F32) for width in widths),
        aliases=aliases,
    )(*operands)


def decay_table(log_gamma, size, scale):
    row = lax.broadcasted_iota(jnp.int32, (size, size), 0)
    col = lax.broadcasted_iota(jnp.int32, (size, size), 1)
    table = jnp.exp((row - col).astype(F32) * log_gamma) * scale
    return table, jnp.where(row >= col, table, 0.0)


def pair_scale(docs, i, j, log_gamma, size):
    same = jnp.logical_and(docs[i] == docs[j], docs[i] >= 0)
    far = jnp.exp(jnp.full((1, 1), (i - j) * size, F32) * log_gamma)
    return jnp.where(same, far, 0.0)


def retention_forward_kernel(
    blocks, kd, vd, me_ref, docs_ref, rates_ref, proj_ref, mixed_ref, full_ref, diag_ref
):
    head = pl.program_id(0)
    size = proj_ref.shape[0] // blocks
    log_gamma = rates_ref[head]
    full_ref[...], diag_ref[...] = decay_table(log_gamma, size, kd**-0.5)
    me = me_ref[0]
    docs = [docs_ref[i] for i in range(blocks)]
    slots = [pl.ds(pl.multiple_of((i ^ me) * size, size), size) for i in range(blocks)]
    keys = slice(kd, 2 * kd)
    values = slice(2 * kd, 2 * kd + vd)
    for i in range(blocks):
        query = proj_ref[slots[i], :kd]
        total = None
        for j in range(i + 1):
            table = diag_ref if j == i else full_ref
            raw = dot_nt(query, proj_ref[slots[j], keys])
            scores = (raw * (table[...] * pair_scale(docs, i, j, log_gamma, size))).astype(BF16)
            term = dot_nn(scores, proj_ref[slots[j], values])
            total = term if total is None else total + term
        center = total - jnp.mean(total, axis=-1, keepdims=True)
        variance = jnp.mean(center * center, axis=-1, keepdims=True)
        normal = center * lax.rsqrt(jnp.maximum(variance, GROUP_FLOOR))
        gate = proj_ref[slots[i], 2 * kd + vd :].astype(F32)
        mixed_ref[slots[i], :] = (gate * jax.nn.sigmoid(gate) * normal).astype(BF16)


def retention_backward_kernel(
    head,
    blocks,
    kd,
    vd,
    me_ref,
    docs_ref,
    rates_ref,
    proj_ref,
    grad_ref,
    gproj_ref,
    full_ref,
    diag_ref,
    gkey_ref,
    gvalue_ref,
):
    size = proj_ref.shape[0] // blocks
    log_gamma = rates_ref[head]
    full_ref[...], diag_ref[...] = decay_table(log_gamma, size, kd**-0.5)
    me = me_ref[0]
    docs = [docs_ref[i] for i in range(blocks)]
    slots = [pl.ds(pl.multiple_of((i ^ me) * size, size), size) for i in range(blocks)]
    keys = slice(kd, 2 * kd)
    values = slice(2 * kd, 2 * kd + vd)
    gates = slice(2 * kd + vd, 2 * kd + 2 * vd)
    for i in range(blocks):
        query = proj_ref[slots[i], :kd]
        total = None
        masks = []
        kept = []
        for j in range(i + 1):
            table = diag_ref if j == i else full_ref
            mask = table[...] * pair_scale(docs, i, j, log_gamma, size)
            raw = dot_nt(query, proj_ref[slots[j], keys])
            scores = (raw * mask).astype(BF16)
            term = dot_nn(scores, proj_ref[slots[j], values])
            total = term if total is None else total + term
            kept.append(scores)
            masks.append(mask)
        center = total - jnp.mean(total, axis=-1, keepdims=True)
        variance = jnp.mean(center * center, axis=-1, keepdims=True)
        inverse = lax.rsqrt(jnp.maximum(variance, GROUP_FLOOR))
        normal = center * inverse
        gate = proj_ref[slots[i], gates].astype(F32)
        grad = grad_ref[slots[i], :].astype(F32)
        sig = jax.nn.sigmoid(gate)
        ggate = grad * normal * (sig * (1.0 + gate * (1.0 - sig)))
        gproj_ref[slots[i], gates] = ggate.astype(BF16)
        gnormal = grad * gate * sig
        along = jnp.mean(gnormal * normal, axis=-1, keepdims=True)
        along = jnp.where(variance > GROUP_FLOOR, along, 0.0)
        gcenter = inverse * (gnormal - normal * along)
        gret = (gcenter - jnp.mean(gcenter, axis=-1, keepdims=True)).astype(BF16)
        gquery = None
        for j in range(i + 1):
            graw = dot_nt(gret, proj_ref[slots[j], values])
            graw = (graw * masks[j]).astype(BF16)
            term = dot_nn(graw, proj_ref[slots[j], keys])
            gquery = term if gquery is None else gquery + term
            place = pl.ds(j * size, size)
            gkey = dot_tn(graw, query)
            gvalue = dot_tn(kept[j], gret)
            if j == i:
                gkey_ref[place, :] = gkey
                gvalue_ref[place, :] = gvalue
            else:
                gkey_ref[place, :] += gkey
                gvalue_ref[place, :] += gvalue
        gproj_ref[slots[i], :kd] = gquery.astype(BF16)
    for i in range(blocks):
        place = pl.ds(i * size, size)
        gproj_ref[slots[i], keys] = gkey_ref[place, :].astype(BF16)
        gproj_ref[slots[i], values] = gvalue_ref[place, :].astype(BF16)


def retention_forward(blocks, heads, kd, vd, me, docs, rates, proj):
    length = proj.shape[0]
    size = length // blocks
    return call(
        functools.partial(retention_forward_kernel, blocks, kd, vd),
        heads,
        [smem(), smem(), smem(), pl.BlockSpec((length, 2 * (kd + vd)), lambda h: (0, h))],
        pl.BlockSpec((length, vd), lambda h: (0, h)),
        jax.ShapeDtypeStruct((length, heads * vd), BF16),
        [pltpu.VMEM((size, size), F32)] * 2,
    )(me, docs, rates, proj)


def retention_backward(head, blocks, kd, vd, me, docs, rates, proj, grad):
    length = proj.shape[0]
    size = length // blocks
    width = 2 * (kd + vd)
    one = pl.Buffered(1)
    return call(
        functools.partial(retention_backward_kernel, head, blocks, kd, vd),
        1,
        [
            smem(),
            smem(),
            smem(),
            pl.BlockSpec((length, width), lambda i: (0, head), pipeline_mode=one),
            pl.BlockSpec((length, vd), lambda i: (0, head), pipeline_mode=one),
        ],
        resident((length, width)),
        jax.ShapeDtypeStruct((length, width), BF16),
        [pltpu.VMEM((size, size), F32)] * 2
        + [pltpu.VMEM((length, kd), F32), pltpu.VMEM((length, vd), F32)],
    )(me, docs, rates, proj, grad)


def body(
    layer_in,
    norm1_gain,
    w_query,
    w_key,
    w_value,
    w_gate,
    w_out,
    norm2_gain,
    w_up,
    w_down,
    decay_rates,
    seq_counts,
    out_grad,
):
    heads = decay_rates.shape[0]
    kd = w_query.shape[1] // heads
    vd = w_value.shape[1] // heads
    micros, rows_dev, width = layer_in.shape
    blocks = lax.axis_size("mp")
    length = rows_dev * blocks
    tall = [rows_dev] * blocks
    wide = [rows_dev] * 3 + [rows_dev // 2] * 2 if blocks == 4 else tall
    pieces = []
    for h in range(heads):
        pieces += [
            w_query[:, h * kd : (h + 1) * kd],
            w_key[:, h * kd : (h + 1) * kd],
            w_value[:, h * vd : (h + 1) * vd],
            w_gate[:, h * vd : (h + 1) * vd],
        ]
    w_in = jnp.concatenate(pieces, 1)
    gain_one = norm1_gain.reshape(1, -1)
    gain_two = norm2_gain.reshape(1, -1)
    rates = jnp.log1p(-decay_rates)
    me = lax.axis_index("mp").reshape(1).astype(jnp.int32)
    starts = jnp.arange(blocks, dtype=jnp.int32) * rows_dev
    a, b = range(micros)
    docs = [document_ids(seq_counts[0, m], starts, length) for m in (a, b)]
    def backward(h, m, proj, grad):
        return retention_backward(h, blocks, kd, vd, me, docs[m], rates, proj, grad)

    up_rows, down_rows = (
        weight.shape[0] // lax.axis_size("dp") for weight in (w_up, w_down)
    )

    def eighth_rows():
        place = lax.axis_index("dp")
        up = lax.dynamic_slice_in_dim(w_up, place * up_rows, up_rows, 0)
        down = lax.dynamic_slice_in_dim(w_down, place * down_rows, down_rows, 0)
        cut = w_up.shape[1]
        return jnp.concatenate(
            [up] + [down[:, k : k + cut] for k in range(0, width, cut)], 0
        )

    def exchange(rows):
        return move(rows, "mp", 2) if blocks == 4 else rows

    def neighbour_weights(rows):
        if blocks != 4:
            return []
        down = [
            rows[k : k + down_rows] for k in range(up_rows, rows.shape[0], down_rows)
        ]
        return [
            lax.all_gather(part, "dp", axis=0, tiled=True)
            for part in (rows[:up_rows], jnp.concatenate(down, 1))
        ]

    def pair_send(total, dim):
        if blocks != 4:
            return [total]
        half = total.shape[1 - dim] // 2
        own = lax.slice_in_dim(total, 0, half, axis=1 - dim)
        other = lax.slice_in_dim(total, half, 2 * half, axis=1 - dim)
        return [own, move(other, "mp", 2)]

    def pair_sum(halves):
        return sum(half.astype(F32) for half in halves)

    ranks = lax.axis_size("dp")
    core = (lax.axis_index("dp") % 2).reshape(1).astype(jnp.int32)

    def cores(kept_sent):
        kept, sent = kept_sent
        return kept, move(sent, "dp", 1)

    def weight_sum(total, dim, whole=False):
        groups = [list(range(parity, ranks, 2)) for parity in (0, 1)]
        return lax.psum_scatter(
            total,
            "dp",
            scatter_dimension=dim,
            tiled=True,
            axis_index_groups=None if whole else groups,
        )

    normed_a = first_norm(a, layer_in, gain_one)
    normed_b = first_norm(b, after(layer_in, normed_a, w_in), gain_one)
    go_one_a = Gather(normed_a)
    eighths = eighth_rows()
    fenced = fence(go_one_a, normed_b, eighths, docs, rates, me)
    go_one_a, normed_b, eighths, docs, rates, me = fenced
    forward = (blocks, heads, kd, vd, me)
    go_one_a.middle()
    go_one_a, normed_b = fence(go_one_a, normed_b)

    go_one_b = Gather(normed_b)
    eighths = exchange(after(eighths, normed_b))
    cot_a = PairGather(after(out_grad[a], normed_b))
    gathered_a, proj_a = gather_product(go_one_a.result(), w_in, False)
    mixed_a = retention_forward(*forward, docs[a], rates, proj_a)
    go_one_b, eighths, cot_a, mixed_a = fence(go_one_b, eighths, cot_a, mixed_a)
    go_one_b.middle()
    more = neighbour_weights(eighths)
    parts = product_scatter([mixed_a], [w_out], False, tall)
    go_one_b, parts = fence(go_one_b, parts)

    sum_one_a = TallScatterSum(parts)
    cot_b = PairGather(after(out_grad[b], parts))
    gathered_b, proj_b = gather_product(go_one_b.result(), w_in, False)
    sum_one_a, cot_b, proj_b = fence(sum_one_a, cot_b, proj_b)
    sum_one_a.middle()
    mixed_b = retention_forward(*forward, docs[b], rates, proj_b)
    parts = product_scatter([mixed_b], [w_out], False, tall)
    sum_one_a, parts = fence(sum_one_a, parts)

    pair = [rows_dev] * 2 if blocks == 4 else tall
    hidden_a, normed = second_norm(a, layer_in, gain_two, sum_one_a.result())
    go_two_a = PairGather(normed)
    sum_one_b = TallScatterSum(parts)
    go_two_a, sum_one_b, hidden_a = fence(go_two_a, sum_one_b, hidden_a)
    sum_one_b.middle()
    total = 2 if blocks == 4 else 1
    rows_two_a, cotangent_a, *feed_a = feed_forward(
        go_two_a.result(), cot_a.result(), [w_up], [w_down], total
    )
    sum_one_b, more, rows_two_a, cotangent_a, feed_a = fence(
        sum_one_b, more, rows_two_a, cotangent_a, feed_a
    )

    ups, downs = [w_up, *more[:1]], [w_down, *more[1:]]
    hidden_b, normed = second_norm(b, layer_in, gain_two, sum_one_b.result(), SMALL)
    go_two_b = PairGather(normed)
    feed_a = after(feed_a, hidden_b)
    if blocks == 4:
        feed_a = feed_more(rows_two_a, cotangent_a, *more, 1, feed_a)
    active_a, gupper_a = feed_a
    parts = product_scatter([gupper_a], ups, True, pair)
    go_two_b, parts = fence(go_two_b, parts)

    sum_three_a = PairScatter(parts)
    rows_two_b, cotangent_b, active_b, gupper_b = feed_forward(
        go_two_b.result(), cot_b.result(), ups, downs, total
    )
    dw_down = weight_product((active_a, active_b), (cotangent_a, cotangent_b))
    fenced = fence(sum_three_a, dw_down, gupper_b, (active_a, active_b))
    sum_three_a, dw_down, gupper_b, actives = fenced

    down_total = weight_sum(dw_down, 1, True)
    parts = product_scatter([gupper_b], ups, True, pair)
    ghidden_a, normed_a, gain_two_a = second_back(
        a, out_grad, hidden_a, gain_two, sum_three_a.result(parts)
    )
    parts, normed_a = fence(parts, normed_a)
    sum_three_b = PairScatter(parts)
    dw_up = weight_rows(
        ranks, core, after((rows_two_a, rows_two_b), normed_a), (gupper_a, gupper_b)
    )
    feeds = [product_scatter([after(actives[0], dw_up)], downs, False, pair, far=SMALL)]
    sum_three_b, normed_a, dw_up, feeds = fence(sum_three_b, normed_a, dw_up, feeds)
    go_three_a = Gather(normed_a)
    dw_up = cores(dw_up)
    ghidden_b, normed_b, gain_two_b = second_back(
        b, out_grad, hidden_b, gain_two, sum_three_b.result()
    )
    feeds.append(
        product_scatter([after(actives[1], normed_b)], downs, False, pair, far=SMALL)
    )
    go_three_a, normed_b, dw_up, feeds = fence(go_three_a, normed_b, dw_up, feeds)
    go_three_a.middle()
    dw_up = add_pair(*dw_up)
    go_three_a, normed_b, dw_up, feeds = fence(go_three_a, normed_b, dw_up, feeds)

    up_total = weight_sum(dw_up, 0)
    go_three_b = Gather(normed_b)
    branch_a, gmixed_a = gather_product(go_three_a.result(), w_out, True)
    gproj_a = [backward(0, a, proj_a, gmixed_a)]
    go_three_b, gproj_a, gmixed_a = fence(go_three_b, gproj_a, gmixed_a)
    go_three_b.middle()
    for h in range(1, heads):
        gproj_a.append(backward(h, a, proj_a, gmixed_a))
    go_three_b, gproj_a, down_total = fence(go_three_b, gproj_a, down_total)

    dw_out = weight_cols(ranks, core, (mixed_a, mixed_b), (branch_a, go_three_b.result()))
    dw_out, go_three_b = fence(dw_out, go_three_b)
    dw_out = cores(dw_out)
    branch_b, gmixed_b = gather_product(go_three_b.result(), w_out, True)
    dw_out, gmixed_b = fence(dw_out, gmixed_b)
    dw_out = add_pair(*dw_out)
    dw_out, gmixed_b, feeds = fence(dw_out, gmixed_b, feeds)
    grad_w_out = weight_sum(dw_out, 1)
    sum_two_a = PairScatter(feeds[0])
    gproj_b = [backward(0, b, proj_b, gmixed_b)]
    dw_in = weight_product((gathered_a, gathered_b), (gproj_a[0], gproj_b[0]))
    fenced = fence(sum_two_a, dw_in, gproj_b, gproj_a, gmixed_b, feeds, up_total)
    sum_two_a, dw_in, gproj_b, gproj_a, gmixed_b, feeds, up_total = fenced
    grad_w_in = [weight_sum(dw_in, 0, True)]
    grad_w_down = pair_send(down_total, 1)
    sum_two_b = PairScatter(feeds[1])
    parts = product_scatter(gproj_a, [w_in], True, wide, far=SMALL)
    fenced = fence(sum_two_b, parts, gproj_b, grad_w_out, grad_w_down)
    sum_two_b, parts, gproj_b, grad_w_out, grad_w_down = fenced
    grad_w_up = pair_send(up_total, 0)
    sum_four_a = ScatterSum(parts)
    for h in range(1, heads):
        gproj_b.append(backward(h, b, proj_b, after(gmixed_b, gproj_b)))
        dw_in = weight_rows(ranks, core, (gathered_a, gathered_b), (gproj_a[h], gproj_b[h]))
    sum_four_a, dw_in, gproj_b, grad_w_up = fence(sum_four_a, dw_in, gproj_b, grad_w_up)
    sum_four_a.middle()
    if heads > 1:
        dw_in = cores(dw_in)
    parts = product_scatter(gproj_b, [w_in], True, wide)
    sum_four_a, dw_in, parts = fence(sum_four_a, dw_in, parts)
    if heads > 1:
        dw_in = add_pair(*dw_in)
    dw_in, grad_w_in, parts, sum_four_a = fence(dw_in, grad_w_in, parts, sum_four_a)
    in_grads = unpack(0, heads, kd, vd, grad_w_in[0], None)

    if heads > 1:
        grad_w_in.append(weight_sum(dw_in, 0))
    sum_four_b = ScatterSum(parts)
    grad_input, gain_one_a = first_back(
        a, layer_in, ghidden_a, gain_one, sum_four_a.result(), None
    )
    layer_out = layer_end(a, micros, hidden_a, sum_two_a.result(grad_input), None)
    layer_out = layer_end(b, micros, hidden_b, sum_two_b.result(), layer_out)
    sum_four_b, grad_input, layer_out = fence(sum_four_b, grad_input, layer_out)
    sum_four_b.middle()
    grad_w_down, grad_w_up = pair_sum(grad_w_down), pair_sum(grad_w_up)
    grad_w_out = grad_w_out.astype(F32)
    fenced = fence(sum_four_b, in_grads, grad_w_out, grad_w_down, grad_w_up)
    sum_four_b, in_grads, grad_w_out, grad_w_down, grad_w_up = fenced
    grad_input, gain_one_b = first_back(
        b, layer_in, ghidden_b, gain_one, sum_four_b.result(), grad_input
    )

    for h in range(1, heads):
        in_grads = unpack(h, heads, kd, vd, grad_w_in[h], in_grads)
    gains = small_sum(
        jnp.concatenate([gain_one_a + gain_one_b, gain_two_a + gain_two_b], 0)
    )
    return (
        layer_out,
        grad_input,
        gains[0],
        *in_grads,
        grad_w_out,
        gains[1],
        grad_w_up,
        grad_w_down,
    )


def solution(mesh):
    in_specs = (
        P(None, ("dp", "mp"), None),
        P(),
        P(None, "mp"),
        P(None, "mp"),
        P(None, "mp"),
        P(None, "mp"),
        P("mp", None),
        P(),
        P(None, "mp"),
        P("mp", None),
        P("mp"),
        P("dp", None, None),
        P(None, ("dp", "mp"), None),
    )
    out_specs = (
        P(None, ("dp", "mp"), None),
        P(None, ("dp", "mp"), None),
        P("dp"),
        P("dp", "mp"),
        P("dp", "mp"),
        P("dp", "mp"),
        P("dp", "mp"),
        P("mp", "dp"),
        P("dp"),
        P("dp", "mp"),
        P("mp", "dp"),
    )
    return jax.shard_map(body, mesh=mesh, in_specs=in_specs, out_specs=out_specs, check_vma=False)
```

```python
import functools

import jax
import jax.numpy as jnp
from jax import lax
from jax.experimental import pallas as pl
from jax.experimental.pallas import tpu as pltpu
from jax.sharding import PartitionSpec as P

NORM_EPS = 1e-05
GROUP_FLOOR = 1.0
BF16 = jnp.bfloat16
F32 = jnp.float32
TINY = pl.CostEstimate(flops=1, bytes_accessed=1, transcendentals=0)


def document_ids(counts, position, length):
    half_len = length // 2
    quarter_len = length // 4
    long_end = counts[2] * length
    half_end = long_end + counts[1] * half_len
    quarter_end = half_end + counts[0] * quarter_len
    long_ids = position // length
    half_ids = counts[2] + (position - long_end) // half_len
    quarter_ids = counts[2] + counts[1] + (position - half_end) // quarter_len
    inner = jnp.where(position < quarter_end, quarter_ids, -1)
    inner = jnp.where(position < half_end, half_ids, inner)
    return jnp.where(position < long_end, long_ids, inner)


def dot_nt(left, right):
    return lax.dot_general(left, right, (((1,), (1,)), ((), ())), preferred_element_type=F32)


def dot_tn(left, right):
    return lax.dot_general(left, right, (((0,), (0,)), ((), ())), preferred_element_type=F32)


def dot_nn(left, right):
    return jnp.dot(left, right, preferred_element_type=F32)


def move(value, axis, step):
    size = lax.axis_size(axis)
    return lax.ppermute(value, axis, [(i, i ^ step) for i in range(size)])


def after(value, *earlier):
    return lax.optimization_barrier((value, earlier))[0]


def fence(*values):
    return lax.optimization_barrier(values)


class Transfer:
    def __init_subclass__(cls):
        jax.tree_util.register_pytree_node(
            cls, lambda self: (self.parts(), None), lambda _, parts: cls.rebuild(parts)
        )

    def parts(self):
        return (self.kept, self.pieces)

    @classmethod
    def rebuild(cls, parts):
        self = object.__new__(cls)
        self.kept, self.pieces = parts
        return self

    def result(self, *earlier):
        return after([*self.kept, *self.pieces], earlier)


class Gather(Transfer):
    def __init__(self, rows):
        steps = (1, 2) if lax.axis_size("mp") == 4 else range(1, lax.axis_size("mp"))
        self.kept = [rows]
        self.pieces = [move(rows, "mp", k) for k in steps]

    def middle(self):
        if lax.axis_size("mp") == 4:
            first, second = self.pieces
            half = first.shape[0] // 2
            self.kept = [*self.kept, first, second]
            self.pieces = [move(first[:half], "mp", 2), move(second[half:], "mp", 1)]


class ScatterSum(Transfer):
    def __init__(self, segments):
        if lax.axis_size("mp") == 4:
            self.kept = [*segments[:3]]
            upper, lower = segments[3:]
            self.pieces = [move(upper, "mp", 1), move(lower, "mp", 2)]
        else:
            self.kept = [segments[0]]
            self.pieces = [move(part, "mp", k + 1) for k, part in enumerate(segments[1:])]

    def middle(self):
        if lax.axis_size("mp") == 4:
            own, first, second = self.kept
            upper, lower = self.pieces
            half = upper.shape[0]
            first = jnp.concatenate([first[:half], first[half:] + lower], 0)
            second = jnp.concatenate([second[:half] + upper, second[half:]], 0)
            self.kept = [own]
            self.pieces = [move(first, "mp", 1), move(second, "mp", 2)]


class TallScatterSum(ScatterSum):
    def __init__(self, segments):
        if lax.axis_size("mp") == 4:
            self.kept = [*segments[:3]]
            self.pieces = [move(segments[3], "mp", 2)]
        else:
            super().__init__(segments)

    def middle(self):
        if lax.axis_size("mp") == 4:
            own, first, second = self.kept
            self.kept = [own]
            self.pieces = [move(first + self.pieces[0], "mp", 1), move(second, "mp", 2)]


class PairGather(Transfer):
    def __init__(self, rows):
        steps = (1,) if lax.axis_size("mp") == 4 else range(1, lax.axis_size("mp"))
        self.kept = [rows]
        self.pieces = [move(rows, "mp", k) for k in steps]


class PairScatter(Transfer):
    def __init__(self, segments):
        self.kept = [segments[0]]
        self.pieces = [move(part, "mp", k + 1) for k, part in enumerate(segments[1:])]


def small_sum(value):
    value = value + sum(move(value, "mp", k) for k in range(1, lax.axis_size("mp")))
    half = lax.axis_size("dp") // 2
    place = lax.axis_index("dp")
    split = value.reshape(value.shape[0], half, 2, -1)
    even = place % 2 == 0
    kept = jnp.where(even, split[:, :, 0], split[:, :, 1])
    sent = jnp.where(even, split[:, :, 1], split[:, :, 0])
    kept = kept + move(sent, "dp", 1)
    pick = lambda chip: lax.dynamic_index_in_dim(kept, chip, 1, False)
    chip = place // 2
    return pick(chip) + sum(move(pick(chip ^ k), "dp", 2 * k) for k in range(1, half))


LARGE, SMALL = 5 << 19, 1 << 18


def nbytes(array):
    return array.size * array.dtype.itemsize


def resident(shape):
    zeros = (0,) * len(shape)
    return pl.BlockSpec(tuple(shape), lambda i: zeros, pipeline_mode=pl.Buffered(1))


def smem():
    return pl.BlockSpec(memory_space=pltpu.SMEM)


def call(kernel, steps, in_specs, out_specs, out_shape, scratch=(), limit=32, aliases=None, far=LARGE, in_far=None):
    name = getattr(kernel, "func", kernel).__name__.removesuffix("_kernel")
    several = isinstance(out_shape, tuple)
    outs = [
        pltpu.HBM(out.shape, out.dtype) if nbytes(out) > far else out
        for out in (out_shape if several else (out_shape,))
    ]
    run = pl.pallas_call(
        kernel,
        name=name,
        grid=(steps,),
        in_specs=in_specs,
        out_specs=out_specs,
        out_shape=tuple(outs) if several else outs[0],
        scratch_shapes=list(scratch),
        input_output_aliases=aliases or {},
        compiler_params=pltpu.CompilerParams(vmem_limit_bytes=limit << 20),
        cost_estimate=TINY,
    )

    def placed(*operands):
        return run(
            *[
                pltpu.with_memory_space_constraint(operand, pltpu.HBM)
                if nbytes(operand) > (in_far or far)
                else operand
                for operand in operands
            ]
        )

    return placed


def assemble(out_ref, refs):
    offset = 0
    for ref in refs:
        rows = ref.shape[0]
        out_ref[offset : offset + rows, :] = ref[...]
        offset += rows


def dissolve(refs, value):
    offset = 0
    for ref in refs:
        rows = ref.shape[0]
        ref[...] = value[offset : offset + rows].astype(ref.dtype)
        offset += rows


def add_up(refs):
    total = refs[0][...].astype(F32)
    for ref in refs[1:]:
        total = total + ref[...].astype(F32)
    return total


def normalize(rows):
    center = rows - jnp.mean(rows, axis=-1, keepdims=True)
    variance = jnp.mean(center * center, axis=-1, keepdims=True)
    inverse = lax.rsqrt(variance + NORM_EPS)
    return center * inverse, inverse


def first_norm_kernel(rows_ref, gain_ref, out_ref):
    normal, _ = normalize(rows_ref[0].astype(F32))
    out_ref[...] = (normal * gain_ref[...].astype(F32)).astype(BF16)


def first_norm(m, rows, gain):
    _, count, width = rows.shape
    narrow = jax.ShapeDtypeStruct((count, width), BF16)
    return call(
        first_norm_kernel,
        1,
        [pl.BlockSpec((1, count, width), lambda i: (m, 0, 0)), resident((1, width))],
        resident((count, width)),
        narrow,
    )(rows, gain)


def second_norm_kernel(rows_ref, gain_ref, *refs):
    hidden_ref, out_ref = refs[-2:]
    hidden = rows_ref[0].astype(F32) + add_up(refs[:-2])
    hidden_ref[...] = hidden
    normal, _ = normalize(hidden)
    out_ref[...] = (normal * gain_ref[...].astype(F32)).astype(BF16)


def second_norm(m, rows, gain, terms, far=LARGE):
    _, count, width = rows.shape
    narrow = jax.ShapeDtypeStruct((count, width), BF16)
    return call(
        second_norm_kernel,
        1,
        [pl.BlockSpec((1, count, width), lambda i: (m, 0, 0)), resident((1, width))]
        + [resident(piece.shape) for piece in terms],
        (resident((count, width)),) * 2,
        (jax.ShapeDtypeStruct((count, width), F32), narrow),
        far=far,
    )(rows, gain, *terms)


def norm_back(rows, gain, grad):
    normal, inverse = normalize(rows)
    scaled = grad * gain
    along = jnp.mean(scaled * normal, axis=-1, keepdims=True)
    inner = scaled - jnp.mean(scaled, axis=-1, keepdims=True) - normal * along
    return inverse * inner, jnp.sum(grad * normal, axis=0, keepdims=True)


def second_back_kernel(cot_ref, hidden_ref, gain_ref, *refs):
    total_ref, out_ref, ggain_ref = refs[-3:]
    grad = add_up(refs[:-3])
    part, ggain_ref[...] = norm_back(hidden_ref[...], gain_ref[...].astype(F32), grad)
    total = cot_ref[0].astype(F32) + part
    total_ref[...] = total
    out_ref[...] = total.astype(BF16)


def second_back(m, cotangent, hidden, gain, terms):
    count, width = hidden.shape
    narrow = jax.ShapeDtypeStruct((count, width), BF16)
    return call(
        second_back_kernel,
        1,
        [
            pl.BlockSpec((1, count, width), lambda i: (m, 0, 0)),
            resident((count, width)),
            resident((1, width)),
        ]
        + [resident(piece.shape) for piece in terms],
        (resident((count, width)), resident((count, width)), resident((1, width))),
        (
            jax.ShapeDtypeStruct((count, width), F32),
            narrow,
            jax.ShapeDtypeStruct((1, width), F32),
        ),
    )(cotangent, hidden, gain, *terms)


def first_back_kernel(terms, rows_ref, ghidden_ref, gain_ref, *refs):
    out_ref, ggain_ref = refs[-2:]
    grad = add_up(refs[:terms])
    part, ggain_ref[...] = norm_back(
        rows_ref[0].astype(F32), gain_ref[...].astype(F32), grad
    )
    out_ref[0] = ghidden_ref[...] + part


def first_back(m, rows, ghidden, gain, terms, before):
    micros, count, width = rows.shape
    block = pl.BlockSpec((1, count, width), lambda i: (m, 0, 0))
    specs = [block, resident((count, width)), resident((1, width))]
    specs += [resident(piece.shape) for piece in terms]
    operands = [rows, ghidden, gain, *terms]
    aliases = {}
    if before is not None:
        aliases = {len(operands): 0}
        operands.append(before)
        specs.append(pl.BlockSpec(memory_space=pl.ANY))
    return call(
        functools.partial(first_back_kernel, len(terms)),
        1,
        specs,
        (block, resident((1, width))),
        (
            jax.ShapeDtypeStruct((micros, count, width), F32),
            jax.ShapeDtypeStruct((1, width), F32),
        ),
        aliases=aliases,
    )(*operands)


def layer_end_kernel(terms, hidden_ref, *refs):
    out_ref = refs[-1]
    total = add_up(refs[:terms])
    out_ref[0] = (hidden_ref[...] + total).astype(BF16)


def layer_end(m, micros, hidden, terms, before):
    count, width = hidden.shape
    specs = [resident((count, width))] + [resident(piece.shape) for piece in terms]
    operands = [hidden, *terms]
    aliases = {}
    if before is not None:
        aliases = {len(operands): 0}
        operands.append(before)
        specs.append(pl.BlockSpec(memory_space=pl.ANY))
    return call(
        functools.partial(layer_end_kernel, len(terms)),
        1,
        specs,
        pl.BlockSpec((1, count, width), lambda i: (m, 0, 0)),
        jax.ShapeDtypeStruct((micros, count, width), BF16),
        aliases=aliases,
    )(*operands)


def gather_product_kernel(dot, pieces, *refs):
    right_ref, all_ref, out_ref = refs[pieces:]

    @pl.when(pl.program_id(0) == 0)
    def _():
        assemble(all_ref, refs[:pieces])

    out_ref[...] = dot(all_ref[...], right_ref[...]).astype(out_ref.dtype)


def gather_product(segments, right, transposed, tile=512):
    rows = sum(segment.shape[0] for segment in segments)
    width = segments[0].shape[1]
    cols = right.shape[0] if transposed else right.shape[1]
    tile = min(tile, cols)
    if transposed:
        spec = pl.BlockSpec((tile, width), lambda i: (i, 0))
    else:
        spec = pl.BlockSpec((width, tile), lambda i: (0, i))
    return call(
        functools.partial(
            gather_product_kernel, dot_nt if transposed else dot_nn, len(segments)
        ),
        cols // tile,
        [resident(segment.shape) for segment in segments] + [spec],
        (resident((rows, width)), pl.BlockSpec((rows, tile), lambda i: (0, i))),
        (jax.ShapeDtypeStruct((rows, width), BF16), jax.ShapeDtypeStruct((rows, cols), BF16)),
    )(*segments, right)


def product_scatter_kernel(transposed, lefts, rights, *refs):
    left_refs = refs[:lefts]
    right_refs = refs[lefts : lefts + rights]
    axis = 1 if transposed else 0
    width = min(
        [ref.shape[1] for ref in left_refs] + [ref.shape[axis] for ref in right_refs]
    )
    depth = sum(ref.shape[1] for ref in left_refs)
    total = None
    for start in range(0, depth, width):
        place, offset = divmod(start, left_refs[0].shape[1])
        left = left_refs[place][:, offset : offset + width]
        place, offset = divmod(start, right_refs[0].shape[axis])
        if transposed:
            term = dot_nt(left, right_refs[place][:, offset : offset + width])
        else:
            term = dot_nn(left, right_refs[place][offset : offset + width, :])
        total = term if total is None else total + term
    dissolve(refs[lefts + rights :], total)


def product_scatter(lefts, rights, transposed, counts, tile=512, far=LARGE):
    cols = rights[0].shape[0] if transposed else rights[0].shape[1]
    tile = min(tile, cols)
    if transposed:
        specs = [pl.BlockSpec((tile, right.shape[1]), lambda i: (i, 0)) for right in rights]
    else:
        specs = [pl.BlockSpec((right.shape[0], tile), lambda i: (0, i)) for right in rights]
    return call(
        functools.partial(product_scatter_kernel, transposed, len(lefts), len(rights)),
        cols // tile,
        [resident(left.shape) for left in lefts] + specs,
        tuple(pl.BlockSpec((count, tile), lambda i: (0, i)) for count in counts),
        tuple(jax.ShapeDtypeStruct((count, cols), BF16) for count in counts),
        far=far,
    )(*lefts, *rights)


def weight_total(micros, refs):
    total = dot_tn(refs[0][...], refs[micros][...])
    for m in range(1, micros):
        total = total + dot_tn(refs[m][...], refs[micros + m][...])
    return total


def weight_rows_kernel(micros, core_ref, *refs):
    keep_ref, send_ref = refs[-2:]
    total = weight_total(micros, refs)
    kept = pl.program_id(0) % 2 == core_ref[0]

    @pl.when(kept)
    def _():
        keep_ref[...] = total.astype(BF16)

    @pl.when(jnp.logical_not(kept))
    def _():
        send_ref[...] = total.astype(BF16)


def weight_rows(ranks, core, lefts, rights):
    tokens, rows = lefts[0].shape
    cols = rights[0].shape[1]
    tile = rows // ranks
    micros = len(lefts)
    return call(
        functools.partial(weight_rows_kernel, micros),
        ranks,
        [smem()]
        + [pl.BlockSpec((tokens, tile), lambda i: (0, i))] * micros
        + [resident((tokens, cols))] * micros,
        (pl.BlockSpec((tile, cols), lambda i: (i // 2, 0)),) * 2,
        (jax.ShapeDtypeStruct((rows // 2, cols), BF16),) * 2,
    far=SMALL,
    )(core, *lefts, *rights)


def weight_cols_kernel(micros, ranks, pieces, core_ref, *refs):
    keep_ref, send_ref = refs[2 * micros + pieces - 1 : 2 * micros + pieces + 1]
    sides = list(refs[: 2 * micros - 1])
    if pieces == 1:
        sides.append(refs[2 * micros - 1])
    else:
        last_ref = refs[-1]
        sides.append(last_ref)

        @pl.when(pl.program_id(0) == 0)
        def _():
            assemble(last_ref, refs[2 * micros - 1 : 2 * micros - 1 + pieces])

    total = weight_total(micros, sides).astype(BF16)
    width = total.shape[1] // ranks
    even = core_ref[0] == 0
    for k in range(ranks // 2):
        first = total[:, 2 * k * width : (2 * k + 1) * width]
        second = total[:, (2 * k + 1) * width : (2 * k + 2) * width]
        place = slice(k * width, (k + 1) * width)
        keep_ref[:, place] = jnp.where(even, first, second)
        send_ref[:, place] = jnp.where(even, second, first)


def weight_cols(ranks, core, lefts, rights, tile=256):
    tokens, rows = lefts[0].shape
    *whole, last = rights
    pieces = last if isinstance(last, (list, tuple)) else [last]
    cols = pieces[0].shape[1]
    tile = min(tile, rows)
    micros = len(lefts)
    scratch = [] if len(pieces) == 1 else [pltpu.VMEM((tokens, cols), BF16)]
    return call(
        functools.partial(weight_cols_kernel, micros, ranks, len(pieces)),
        rows // tile,
        [smem()]
        + [pl.BlockSpec((tokens, tile), lambda i: (0, i))] * micros
        + [resident(side.shape) for side in (*whole, *pieces)],
        (pl.BlockSpec((tile, cols // 2), lambda i: (i, 0)),) * 2,
        (jax.ShapeDtypeStruct((rows, cols // 2), BF16),) * 2,
        scratch,
        far=SMALL,
    )(core, *lefts, *whole, *pieces)


def weight_kernel(micros, *refs):
    refs[-1][...] = weight_total(micros, refs).astype(BF16)


def weight_product(lefts, rights, tile=512):
    tokens, rows = lefts[0].shape
    cols = rights[0].shape[1]
    tile = min(tile, rows)
    micros = len(lefts)
    return call(
        functools.partial(weight_kernel, micros),
        rows // tile,
        [pl.BlockSpec((tokens, tile), lambda i: (0, i))] * micros
        + [resident((tokens, cols))] * micros,
        pl.BlockSpec((tile, cols), lambda i: (i, 0)),
        jax.ShapeDtypeStruct((rows, cols), BF16),
        far=SMALL,
    )(*lefts, *rights)


def add_kernel(left_ref, right_ref, out_ref):
    out_ref[...] = (left_ref[...].astype(F32) + right_ref[...].astype(F32)).astype(BF16)


def add_pair(left, right, tile=256):
    rows, cols = left.shape
    tile = min(tile, rows)
    spec = pl.BlockSpec((tile, cols), lambda i: (i, 0))
    return call(
        add_kernel,
        rows // tile,
        [spec, spec],
        spec,
        jax.ShapeDtypeStruct((rows, cols), BF16),
        far=SMALL,
    )(left, right)


def feed_tile(rows_ref, grad_ref, up_ref, down_ref, active_ref, gupper_ref):
    upper = dot_nn(rows_ref[...], up_ref[...])
    square = upper * upper
    slope = 0.7978845608028654
    bent = jnp.tanh(slope * upper * (1.0 + 0.044715 * square))
    half = 0.5 * (1.0 + bent)
    active_ref[...] = (upper * half).astype(BF16)
    inner = slope * (1.0 + 0.134145 * square)
    turn = half + 0.5 * upper * (1.0 - bent * bent) * inner
    gactive = dot_nt(grad_ref[...], down_ref[...])
    gupper_ref[...] = (gactive * turn).astype(BF16)


def feed_kernel(pieces, parts, steps, *refs):
    weights = refs[2 * pieces : 2 * (pieces + parts)]
    rows_ref, grad_ref, active_ref, gupper_ref = refs[2 * (pieces + parts) :]
    step = pl.program_id(0)

    @pl.when(step == 0)
    def _():
        assemble(rows_ref, refs[:pieces])
        assemble(grad_ref, refs[pieces : 2 * pieces])

    for part in range(parts):

        @pl.when(step // steps == part)
        def _(up_ref=weights[part], down_ref=weights[parts + part]):
            feed_tile(rows_ref, grad_ref, up_ref, down_ref, active_ref, gupper_ref)


def feed_forward(segments, cotangents, ups, downs, total, tile=512):
    rows = sum(segment.shape[0] for segment in segments)
    width = segments[0].shape[1]
    units = ups[0].shape[1]
    tile = min(tile, units)
    steps = units // tile
    parts = len(ups)

    def column(part):
        return lambda i: (0, jnp.clip(i - part * steps, 0, steps - 1))

    def row(part):
        return lambda i: (jnp.clip(i - part * steps, 0, steps - 1), 0)

    narrow = jax.ShapeDtypeStruct((rows, total * units), BF16)
    wide = jax.ShapeDtypeStruct((rows, width), BF16)
    return call(
        functools.partial(feed_kernel, len(segments), parts, steps),
        parts * steps,
        [resident(segment.shape) for segment in (*segments, *cotangents)]
        + [pl.BlockSpec((width, tile), column(part)) for part in range(parts)]
        + [pl.BlockSpec((tile, width), row(part)) for part in range(parts)],
        (resident((rows, width)),) * 2 + (pl.BlockSpec((rows, tile), lambda i: (0, i)),) * 2,
        (wide, wide, narrow, narrow),
        limit=44,
        far=SMALL,
        in_far=LARGE,
    )(*segments, *cotangents, *ups, *downs)


def feed_weight_kernel(pieces, parts, steps, *refs):
    other_active_ref, other_grad_ref = refs[:2]
    rows_ref, active_ref, gupper_ref, weight_ref, grad_ref = refs[-5:]
    held = (rows_ref, grad_ref, active_ref, gupper_ref)
    feed_kernel(pieces, parts, steps, *refs[2:-5], *held)
    total = dot_tn(other_active_ref[...], other_grad_ref[...])
    total = total + dot_tn(active_ref[...], grad_ref[...])
    weight_ref[...] = total.astype(BF16)


def feed_weight(other_active, other_grad, segments, cotangents, ups, downs, tile=512):
    rows = sum(segment.shape[0] for segment in segments)
    width = segments[0].shape[1]
    units = ups[0].shape[1]
    tile = min(tile, units)
    steps = units // tile
    parts = len(ups)

    def column(part):
        return lambda i: (0, jnp.clip(i - part * steps, 0, steps - 1))

    def row(part):
        return lambda i: (jnp.clip(i - part * steps, 0, steps - 1), 0)

    narrow = jax.ShapeDtypeStruct((rows, parts * units), BF16)
    wide = jax.ShapeDtypeStruct((rows, width), BF16)
    block = pl.BlockSpec((rows, tile), lambda i: (0, i))
    return call(
        functools.partial(feed_weight_kernel, len(segments), parts, steps),
        parts * steps,
        [block, resident((rows, width))]
        + [resident(segment.shape) for segment in (*segments, *cotangents)]
        + [pl.BlockSpec((width, tile), column(part)) for part in range(parts)]
        + [pl.BlockSpec((tile, width), row(part)) for part in range(parts)],
        (
            resident((rows, width)),
            block,
            block,
            pl.BlockSpec((tile, width), lambda i: (i, 0)),
        ),
        (wide, narrow, narrow, jax.ShapeDtypeStruct((parts * units, width), BF16)),
        [pltpu.VMEM((rows, width), BF16)],
        limit=54,
        far=SMALL,
        in_far=LARGE,
    )(other_active, other_grad, *segments, *cotangents, *ups, *downs)


def feed_more_kernel(rows_ref, grad_ref, up_ref, down_ref, *refs):
    feed_tile(rows_ref, grad_ref, up_ref, down_ref, *refs[-2:])


def feed_more(rows, cotangents, up, down, part, before, tile=256):
    count, width = rows.shape
    tile = min(tile, up.shape[1])
    steps = up.shape[1] // tile
    held = pl.BlockSpec(memory_space=pl.ANY)
    return call(
        feed_more_kernel,
        steps,
        [
            resident((count, width)),
            resident((count, width)),
            pl.BlockSpec((width, tile), lambda i: (0, i)),
            pl.BlockSpec((tile, width), lambda i: (i, 0)),
            held,
            held,
        ],
        (pl.BlockSpec((count, tile), lambda i: (0, i + part * steps)),) * 2,
        tuple(jax.ShapeDtypeStruct(array.shape, BF16) for array in before),
        limit=44,
        aliases={4: 0, 5: 1},
        far=SMALL,
    )(rows, cotangents, up, down, *before)


def unpack_kernel(kd, vd, grad_ref, *refs):
    start = 0
    for out_ref, width in zip(refs[-4:], (kd, kd, vd, vd)):
        out_ref[...] = grad_ref[:, start : start + width].astype(F32)
        start += width


def unpack(head, heads, kd, vd, grad, before):
    rows = grad.shape[0]
    widths = (kd, kd, vd, vd)
    operands = [grad]
    specs = [resident(grad.shape)]
    aliases = {}
    if before is not None:
        operands += before
        specs += [pl.BlockSpec(memory_space=pl.ANY)] * 4
        aliases = {1 + n: n for n in range(4)}
    return call(
        functools.partial(unpack_kernel, kd, vd),
        1,
        specs,
        tuple(pl.BlockSpec((rows, width), lambda i: (0, head)) for width in widths),
        tuple(jax.ShapeDtypeStruct((rows, heads * width), F32) for width in widths),
        aliases=aliases,
    )(*operands)


def decay_table(log_gamma, size, scale):
    row = lax.broadcasted_iota(jnp.int32, (size, size), 0)
    col = lax.broadcasted_iota(jnp.int32, (size, size), 1)
    table = jnp.exp((row - col).astype(F32) * log_gamma) * scale
    return table, jnp.where(row >= col, table, 0.0)


def pair_scale(docs, i, j, log_gamma, size):
    same = jnp.logical_and(docs[i] == docs[j], docs[i] >= 0)
    far = jnp.exp(jnp.full((1, 1), (i - j) * size, F32) * log_gamma)
    return jnp.where(same, far, 0.0)


def retention_forward_kernel(
    blocks, kd, vd, me_ref, docs_ref, rates_ref, proj_ref, mixed_ref, full_ref, diag_ref
):
    head = pl.program_id(0)
    size = proj_ref.shape[0] // blocks
    log_gamma = rates_ref[head]
    full_ref[...], diag_ref[...] = decay_table(log_gamma, size, kd**-0.5)
    me = me_ref[0]
    docs = [docs_ref[i] for i in range(blocks)]
    slots = [pl.ds(pl.multiple_of((i ^ me) * size, size), size) for i in range(blocks)]
    keys = slice(kd, 2 * kd)
    values = slice(2 * kd, 2 * kd + vd)
    for i in range(blocks):
        query = proj_ref[slots[i], :kd]
        total = None
        for j in range(i + 1):
            table = diag_ref if j == i else full_ref
            raw = dot_nt(query, proj_ref[slots[j], keys])
            scores = (raw * (table[...] * pair_scale(docs, i, j, log_gamma, size))).astype(BF16)
            term = dot_nn(scores, proj_ref[slots[j], values])
            total = term if total is None else total + term
        center = total - jnp.mean(total, axis=-1, keepdims=True)
        variance = jnp.mean(center * center, axis=-1, keepdims=True)
        normal = center * lax.rsqrt(jnp.maximum(variance, GROUP_FLOOR))
        gate = proj_ref[slots[i], 2 * kd + vd :].astype(F32)
        mixed_ref[slots[i], :] = (gate * jax.nn.sigmoid(gate) * normal).astype(BF16)


def retention_backward_kernel(
    head,
    blocks,
    kd,
    vd,
    me_ref,
    docs_ref,
    rates_ref,
    proj_ref,
    grad_ref,
    gproj_ref,
    full_ref,
    diag_ref,
    gkey_ref,
    gvalue_ref,
):
    size = proj_ref.shape[0] // blocks
    log_gamma = rates_ref[head]
    full_ref[...], diag_ref[...] = decay_table(log_gamma, size, kd**-0.5)
    me = me_ref[0]
    docs = [docs_ref[i] for i in range(blocks)]
    slots = [pl.ds(pl.multiple_of((i ^ me) * size, size), size) for i in range(blocks)]
    keys = slice(kd, 2 * kd)
    values = slice(2 * kd, 2 * kd + vd)
    gates = slice(2 * kd + vd, 2 * kd + 2 * vd)
    for i in range(blocks):
        query = proj_ref[slots[i], :kd]
        total = None
        masks = []
        kept = []
        for j in range(i + 1):
            table = diag_ref if j == i else full_ref
            mask = table[...] * pair_scale(docs, i, j, log_gamma, size)
            raw = dot_nt(query, proj_ref[slots[j], keys])
            scores = (raw * mask).astype(BF16)
            term = dot_nn(scores, proj_ref[slots[j], values])
            total = term if total is None else total + term
            kept.append(scores)
            masks.append(mask)
        center = total - jnp.mean(total, axis=-1, keepdims=True)
        variance = jnp.mean(center * center, axis=-1, keepdims=True)
        inverse = lax.rsqrt(jnp.maximum(variance, GROUP_FLOOR))
        normal = center * inverse
        gate = proj_ref[slots[i], gates].astype(F32)
        grad = grad_ref[slots[i], :].astype(F32)
        sig = jax.nn.sigmoid(gate)
        ggate = grad * normal * (sig * (1.0 + gate * (1.0 - sig)))
        gproj_ref[slots[i], gates] = ggate.astype(BF16)
        gnormal = grad * gate * sig
        along = jnp.mean(gnormal * normal, axis=-1, keepdims=True)
        along = jnp.where(variance > GROUP_FLOOR, along, 0.0)
        gcenter = inverse * (gnormal - normal * along)
        gret = (gcenter - jnp.mean(gcenter, axis=-1, keepdims=True)).astype(BF16)
        gquery = None
        for j in range(i + 1):
            graw = dot_nt(gret, proj_ref[slots[j], values])
            graw = (graw * masks[j]).astype(BF16)
            term = dot_nn(graw, proj_ref[slots[j], keys])
            gquery = term if gquery is None else gquery + term
            place = pl.ds(j * size, size)
            gkey = dot_tn(graw, query)
            gvalue = dot_tn(kept[j], gret)
            if j == i:
                gkey_ref[place, :] = gkey
                gvalue_ref[place, :] = gvalue
            else:
                gkey_ref[place, :] += gkey
                gvalue_ref[place, :] += gvalue
        gproj_ref[slots[i], :kd] = gquery.astype(BF16)
    for i in range(blocks):
        place = pl.ds(i * size, size)
        gproj_ref[slots[i], keys] = gkey_ref[place, :].astype(BF16)
        gproj_ref[slots[i], values] = gvalue_ref[place, :].astype(BF16)


def retention_forward(blocks, heads, kd, vd, me, docs, rates, proj):
    length = proj.shape[0]
    size = length // blocks
    return call(
        functools.partial(retention_forward_kernel, blocks, kd, vd),
        heads,
        [smem(), smem(), smem(), pl.BlockSpec((length, 2 * (kd + vd)), lambda h: (0, h))],
        pl.BlockSpec((length, vd), lambda h: (0, h)),
        jax.ShapeDtypeStruct((length, heads * vd), BF16),
        [pltpu.VMEM((size, size), F32)] * 2,
    )(me, docs, rates, proj)


def retention_backward(head, blocks, kd, vd, me, docs, rates, proj, grad):
    length = proj.shape[0]
    size = length // blocks
    width = 2 * (kd + vd)
    one = pl.Buffered(1)
    return call(
        functools.partial(retention_backward_kernel, head, blocks, kd, vd),
        1,
        [
            smem(),
            smem(),
            smem(),
            pl.BlockSpec((length, width), lambda i: (0, head), pipeline_mode=one),
            pl.BlockSpec((length, vd), lambda i: (0, head), pipeline_mode=one),
        ],
        resident((length, width)),
        jax.ShapeDtypeStruct((length, width), BF16),
        [pltpu.VMEM((size, size), F32)] * 2
        + [pltpu.VMEM((length, kd), F32), pltpu.VMEM((length, vd), F32)],
    )(me, docs, rates, proj, grad)


def body(
    layer_in,
    norm1_gain,
    w_query,
    w_key,
    w_value,
    w_gate,
    w_out,
    norm2_gain,
    w_up,
    w_down,
    decay_rates,
    seq_counts,
    out_grad,
):
    heads = decay_rates.shape[0]
    kd = w_query.shape[1] // heads
    vd = w_value.shape[1] // heads
    micros, rows_dev, width = layer_in.shape
    blocks = lax.axis_size("mp")
    length = rows_dev * blocks
    tall = [rows_dev] * blocks
    wide = [rows_dev] * 3 + [rows_dev // 2] * 2 if blocks == 4 else tall
    pieces = []
    for h in range(heads):
        pieces += [
            w_query[:, h * kd : (h + 1) * kd],
            w_key[:, h * kd : (h + 1) * kd],
            w_value[:, h * vd : (h + 1) * vd],
            w_gate[:, h * vd : (h + 1) * vd],
        ]
    w_in = jnp.concatenate(pieces, 1)
    gain_one = norm1_gain.reshape(1, -1)
    gain_two = norm2_gain.reshape(1, -1)
    rates = jnp.log1p(-decay_rates)
    me = lax.axis_index("mp").reshape(1).astype(jnp.int32)
    starts = jnp.arange(blocks, dtype=jnp.int32) * rows_dev
    a, b = range(micros)
    docs = [document_ids(seq_counts[0, m], starts, length) for m in (a, b)]
    def backward(h, m, proj, grad):
        return retention_backward(h, blocks, kd, vd, me, docs[m], rates, proj, grad)

    up_rows, down_rows = (
        weight.shape[0] // lax.axis_size("dp") for weight in (w_up, w_down)
    )

    def eighth_rows():
        place = lax.axis_index("dp")
        up = lax.dynamic_slice_in_dim(w_up, place * up_rows, up_rows, 0)
        down = lax.dynamic_slice_in_dim(w_down, place * down_rows, down_rows, 0)
        cut = w_up.shape[1]
        return jnp.concatenate(
            [up] + [down[:, k : k + cut] for k in range(0, width, cut)], 0
        )

    def exchange(rows):
        return move(rows, "mp", 2) if blocks == 4 else rows

    def neighbour_weights(rows):
        if blocks != 4:
            return []
        down = [
            rows[k : k + down_rows] for k in range(up_rows, rows.shape[0], down_rows)
        ]
        return [
            lax.all_gather(part, "dp", axis=0, tiled=True)
            for part in (rows[:up_rows], jnp.concatenate(down, 1))
        ]

    def pair_send(total, dim):
        if blocks != 4:
            return [total]
        half = total.shape[1 - dim] // 2
        own = lax.slice_in_dim(total, 0, half, axis=1 - dim)
        other = lax.slice_in_dim(total, half, 2 * half, axis=1 - dim)
        return [own, move(other, "mp", 2)]

    def pair_sum(halves):
        return sum(half.astype(F32) for half in halves)

    ranks = lax.axis_size("dp")
    core = (lax.axis_index("dp") % 2).reshape(1).astype(jnp.int32)

    def cores(kept_sent):
        kept, sent = kept_sent
        return kept, move(sent, "dp", 1)

    def weight_sum(total, dim, whole=False):
        groups = [list(range(parity, ranks, 2)) for parity in (0, 1)]
        return lax.psum_scatter(
            total,
            "dp",
            scatter_dimension=dim,
            tiled=True,
            axis_index_groups=None if whole else groups,
        )

    normed_a = first_norm(a, layer_in, gain_one)
    normed_b = first_norm(b, after(layer_in, normed_a, w_in), gain_one)
    go_one_a = Gather(normed_a)
    eighths = eighth_rows()
    fenced = fence(go_one_a, normed_b, eighths, docs, rates, me)
    go_one_a, normed_b, eighths, docs, rates, me = fenced
    forward = (blocks, heads, kd, vd, me)
    go_one_a.middle()
    go_one_a, normed_b = fence(go_one_a, normed_b)

    go_one_b = Gather(normed_b)
    eighths = exchange(after(eighths, normed_b))
    cot_a = PairGather(after(out_grad[a], normed_b))
    gathered_a, proj_a = gather_product(go_one_a.result(), w_in, False)
    mixed_a = retention_forward(*forward, docs[a], rates, proj_a)
    go_one_b, eighths, cot_a, mixed_a = fence(go_one_b, eighths, cot_a, mixed_a)
    go_one_b.middle()
    more = neighbour_weights(eighths)
    parts = product_scatter([mixed_a], [w_out], False, tall)
    go_one_b, parts = fence(go_one_b, parts)

    sum_one_a = TallScatterSum(parts)
    cot_b = PairGather(after(out_grad[b], parts))
    gathered_b, proj_b = gather_product(go_one_b.result(), w_in, False)
    sum_one_a, cot_b, proj_b = fence(sum_one_a, cot_b, proj_b)
    sum_one_a.middle()
    mixed_b = retention_forward(*forward, docs[b], rates, proj_b)
    parts = product_scatter([mixed_b], [w_out], False, tall)
    sum_one_a, parts = fence(sum_one_a, parts)

    pair = [rows_dev] * 2 if blocks == 4 else tall
    hidden_a, normed = second_norm(a, layer_in, gain_two, sum_one_a.result())
    go_two_a = PairGather(normed)
    sum_one_b = TallScatterSum(parts)
    go_two_a, sum_one_b, hidden_a = fence(go_two_a, sum_one_b, hidden_a)
    sum_one_b.middle()
    total = 2 if blocks == 4 else 1
    rows_two_a, cotangent_a, *feed_a = feed_forward(
        go_two_a.result(), cot_a.result(), [w_up], [w_down], total
    )
    sum_one_b, more, rows_two_a, cotangent_a, feed_a = fence(
        sum_one_b, more, rows_two_a, cotangent_a, feed_a
    )

    ups, downs = [w_up, *more[:1]], [w_down, *more[1:]]
    hidden_b, normed = second_norm(b, layer_in, gain_two, sum_one_b.result(), SMALL)
    go_two_b = PairGather(normed)
    feed_a = after(feed_a, hidden_b)
    if blocks == 4:
        feed_a = feed_more(rows_two_a, cotangent_a, *more, 1, feed_a)
    active_a, gupper_a = feed_a
    parts = product_scatter([gupper_a], ups, True, pair)
    go_two_b, parts = fence(go_two_b, parts)

    sum_three_a = PairScatter(parts)
    rows_two_b, active_b, gupper_b, dw_down = feed_weight(
        active_a, cotangent_a, go_two_b.result(), cot_b.result(), ups, downs
    )
    fenced = fence(sum_three_a, dw_down, gupper_b, (active_a, active_b))
    sum_three_a, dw_down, gupper_b, actives = fenced

    down_total = weight_sum(dw_down, 1, True)
    parts = product_scatter([gupper_b], ups, True, pair)
    ghidden_a, normed_a, gain_two_a = second_back(
        a, out_grad, hidden_a, gain_two, sum_three_a.result(parts)
    )
    parts, normed_a = fence(parts, normed_a)
    sum_three_b = PairScatter(parts)
    dw_up = weight_rows(
        ranks, core, after((rows_two_a, rows_two_b), normed_a), (gupper_a, gupper_b)
    )
    feeds = [product_scatter([after(actives[0], dw_up)], downs, False, pair, far=SMALL)]
    sum_three_b, normed_a, dw_up, feeds = fence(sum_three_b, normed_a, dw_up, feeds)
    go_three_a = Gather(normed_a)
    dw_up = cores(dw_up)
    ghidden_b, normed_b, gain_two_b = second_back(
        b, out_grad, hidden_b, gain_two, sum_three_b.result()
    )
    feeds.append(
        product_scatter([after(actives[1], normed_b)], downs, False, pair, far=SMALL)
    )
    go_three_a, normed_b, dw_up, feeds = fence(go_three_a, normed_b, dw_up, feeds)
    go_three_a.middle()
    dw_up = add_pair(*dw_up)
    go_three_a, normed_b, dw_up, feeds = fence(go_three_a, normed_b, dw_up, feeds)

    up_total = weight_sum(dw_up, 0)
    go_three_b = Gather(normed_b)
    branch_a, gmixed_a = gather_product(go_three_a.result(), w_out, True)
    gproj_a = [backward(0, a, proj_a, gmixed_a)]
    go_three_b, gproj_a, gmixed_a = fence(go_three_b, gproj_a, gmixed_a)
    go_three_b.middle()
    for h in range(1, heads):
        gproj_a.append(backward(h, a, proj_a, gmixed_a))
    go_three_b, gproj_a, down_total = fence(go_three_b, gproj_a, down_total)

    dw_out = weight_cols(ranks, core, (mixed_a, mixed_b), (branch_a, go_three_b.result()))
    dw_out, go_three_b = fence(dw_out, go_three_b)
    dw_out = cores(dw_out)
    branch_b, gmixed_b = gather_product(go_three_b.result(), w_out, True)
    dw_out, gmixed_b = fence(dw_out, gmixed_b)
    dw_out = add_pair(*dw_out)
    dw_out, gmixed_b, feeds = fence(dw_out, gmixed_b, feeds)
    grad_w_out = weight_sum(dw_out, 1)
    sum_two_a = PairScatter(feeds[0])
    gproj_b = [backward(0, b, proj_b, gmixed_b)]
    dw_in = weight_product((gathered_a, gathered_b), (gproj_a[0], gproj_b[0]))
    fenced = fence(sum_two_a, dw_in, gproj_b, gproj_a, gmixed_b, feeds, up_total)
    sum_two_a, dw_in, gproj_b, gproj_a, gmixed_b, feeds, up_total = fenced
    grad_w_in = [weight_sum(dw_in, 0, True)]
    grad_w_down = pair_send(down_total, 1)
    sum_two_b = PairScatter(feeds[1])
    parts = product_scatter(gproj_a, [w_in], True, wide, far=SMALL)
    fenced = fence(sum_two_b, parts, gproj_b, grad_w_out, grad_w_down)
    sum_two_b, parts, gproj_b, grad_w_out, grad_w_down = fenced
    grad_w_up = pair_send(up_total, 0)
    sum_four_a = ScatterSum(parts)
    for h in range(1, heads):
        gproj_b.append(backward(h, b, proj_b, after(gmixed_b, gproj_b)))
        dw_in = weight_rows(ranks, core, (gathered_a, gathered_b), (gproj_a[h], gproj_b[h]))
    sum_four_a, dw_in, gproj_b, grad_w_up = fence(sum_four_a, dw_in, gproj_b, grad_w_up)
    sum_four_a.middle()
    if heads > 1:
        dw_in = cores(dw_in)
    parts = product_scatter(gproj_b, [w_in], True, wide)
    sum_four_a, dw_in, parts = fence(sum_four_a, dw_in, parts)
    if heads > 1:
        dw_in = add_pair(*dw_in)
    dw_in, grad_w_in, parts, sum_four_a = fence(dw_in, grad_w_in, parts, sum_four_a)
    in_grads = unpack(0, heads, kd, vd, grad_w_in[0], None)

    if heads > 1:
        grad_w_in.append(weight_sum(dw_in, 0))
    sum_four_b = ScatterSum(parts)
    grad_input, gain_one_a = first_back(
        a, layer_in, ghidden_a, gain_one, sum_four_a.result(), None
    )
    layer_out = layer_end(a, micros, hidden_a, sum_two_a.result(grad_input), None)
    layer_out = layer_end(b, micros, hidden_b, sum_two_b.result(), layer_out)
    sum_four_b, grad_input, layer_out = fence(sum_four_b, grad_input, layer_out)
    sum_four_b.middle()
    grad_w_down, grad_w_up = pair_sum(grad_w_down), pair_sum(grad_w_up)
    grad_w_out = grad_w_out.astype(F32)
    fenced = fence(sum_four_b, in_grads, grad_w_out, grad_w_down, grad_w_up)
    sum_four_b, in_grads, grad_w_out, grad_w_down, grad_w_up = fenced
    grad_input, gain_one_b = first_back(
        b, layer_in, ghidden_b, gain_one, sum_four_b.result(), grad_input
    )

    for h in range(1, heads):
        in_grads = unpack(h, heads, kd, vd, grad_w_in[h], in_grads)
    gains = small_sum(
        jnp.concatenate([gain_one_a + gain_one_b, gain_two_a + gain_two_b], 0)
    )
    return (
        layer_out,
        grad_input,
        gains[0],
        *in_grads,
        grad_w_out,
        gains[1],
        grad_w_up,
        grad_w_down,
    )


def solution(mesh):
    in_specs = (
        P(None, ("dp", "mp"), None),
        P(),
        P(None, "mp"),
        P(None, "mp"),
        P(None, "mp"),
        P(None, "mp"),
        P("mp", None),
        P(),
        P(None, "mp"),
        P("mp", None),
        P("mp"),
        P("dp", None, None),
        P(None, ("dp", "mp"), None),
    )
    out_specs = (
        P(None, ("dp", "mp"), None),
        P(None, ("dp", "mp"), None),
        P("dp"),
        P("dp", "mp"),
        P("dp", "mp"),
        P("dp", "mp"),
        P("dp", "mp"),
        P("mp", "dp"),
        P("dp"),
        P("dp", "mp"),
        P("mp", "dp"),
    )
    return jax.shard_map(body, mesh=mesh, in_specs=in_specs, out_specs=out_specs, check_vma=False)
```
